32 devices in a mesh: groups: 2 (over y), chan: 4 (over z), space: 4 (over x, core).
Axes of the slice: x: 2, y: 2, z: 4, core: 2. Of those that a mesh axis runs over, the one named last changes fastest.
Arguments:
- volume: bfloat16 [2048, 16, 512], P(('groups', 'chan'), 'space'), parts along dimension 0, may hold values from -6 to 6
- out_grad: bfloat16 [2048, 16, 512], P(('groups', 'chan'), 'space'), parts along dimension 0, may hold values from -6 to 6
- weight_in: bfloat16 [1024, 1024], P('chan'), may hold values from -0.1875 to 0.1875
- weight_out: bfloat16 [1024, 1024], P('chan'), may hold values from -0.1875 to 0.1875
- filter_taps: float32 [1024, 27], P('chan'), may hold values from -1.25 to 1.25
- filter_bias: float32 [1024], P('chan'), may hold values from -3 to 3
Outputs:
- block_out: bfloat16 [2048, 16, 512], P(('groups', 'chan'), 'space'), parts along dimension 0
- volume_grad: bfloat16 [2048, 16, 512], P(('groups', 'chan'), 'space'), parts along dimension 0
The draws below stay inside these ranges and needn't reach their ends.
There are 2 independent parts, one for each index of `groups`. The reference program is written for one: setup_inputs(seed, part) draws one part's arguments, and reference() takes and returns one part's arrays. A program takes and returns all parts, laid end to end along the dimension named above; an argument that names none is the same for every part. Nothing has to cross between parts.
All inputs are finite; a program needn't handle non-finite values.
Results may differ from the reference program's by a relative error of at most 0.0085.
Values may be sent and summed in bfloat16 or wider, within the bound.
No kernel may reach another device: no remote copies, remote signals or barrier semaphores. Data moves between devices by JAX's collectives and lax.ppermute only.
A program may use at most 64 MiB of HBM per device.

```python
import jax
import jax.numpy as jnp
from jax import lax

C = 1024
TAPS = 27
CX = 32
CY = 16
NZ = 16
PLANE = 512


def shard_levels(rng, dims, split, low, largest):
    level, own = 1.0, jax.random.fold_in(rng, 6)
    for dim, parts in split:
        heights = jnp.exp(jax.random.uniform(jax.random.fold_in(own, dim), (parts,), jnp.float32, low / len(split), largest / len(split)))
        level = level * jnp.repeat(heights, dims[dim] // parts).reshape([-1 if axis == dim else 1 for axis in range(len(dims))])
    return level


def gaussian(own_key, dims, width, limit, cuts=(), dtype=jnp.bfloat16):
    entries = width * jax.random.normal(own_key, dims, jnp.float32)
    if cuts:
        entries = entries * shard_levels(own_key, dims, cuts, -0.22, 0.18)
    return jnp.clip(entries, -limit, limit).astype(dtype)


def setup_inputs(seed: int = 0, part: int = 0) -> dict:
    streams_of = jax.random.split(jax.random.key(seed), 7)
    part_splits = jax.random.split(jax.random.fold_in(streams_of[6], part), 7)
    return {
        "volume": gaussian(part_splits[0], (C, NZ, PLANE), 1.0, 6.0, ((0, 4), (1, 4))),
        "out_grad": gaussian(part_splits[1], (C, NZ, PLANE), 1.0, 6.0, ((0, 4), (1, 4))),
        "weight_in": gaussian(streams_of[2], (C, C), C ** -0.5, 0.1875, ((0, 4),)),
        "weight_out": gaussian(streams_of[3], (C, C), C ** -0.5, 0.1875, ((0, 4),)),
        "filter_taps": gaussian(streams_of[4], (C, TAPS), TAPS ** -0.5, 1.25, ((0, 4),), jnp.float32),
        "filter_bias": gaussian(streams_of[5], (C,), 0.5, 3.0, ((0, 4),), jnp.float32),
    }


root_half = 0.7071067811865476
inv_root_two_pi = 0.3989422804014327


def gelu_value(field):
    return 0.5 * field * (1.0 + lax.erf(field * root_half))


def gelu_slope(field):
    return 0.5 * (1.0 + lax.erf(field * root_half)) + field * jnp.exp(-0.5 * field * field) * inv_root_two_pi


def core(padded, filter_taps, direction):
    extent_z = padded.shape[1] - 2
    extent_y = padded.shape[2] - 2
    extent_x = padded.shape[3] - 2
    summed = jnp.zeros((padded.shape[0], extent_z, extent_y, extent_x), jnp.float32)
    for shift_z in range(3):
        for shift_y in range(3):
            for shift_x in range(3):
                tap_index = (shift_z * 3 + shift_y) * 3 + shift_x
                begin_z = 1 + direction * (shift_z - 1)
                begin_y = 1 + direction * (shift_y - 1)
                begin_x = 1 + direction * (shift_x - 1)
                window = padded[:, begin_z:begin_z + extent_z, begin_y:begin_y + extent_y, begin_x:begin_x + extent_x]
                summed = summed + filter_taps[:, tap_index][:, None, None, None] * window
    return summed


def reference(volume, out_grad, weight_in, weight_out, filter_taps, filter_bias):
    channels = volume.shape[0]
    slab_shape = volume.shape
    grid_shape = (channels, volume.shape[1], CY, CX)
    pads = ((0, 0), (1, 1), (1, 1), (1, 1))
    flat_in = volume.reshape(channels, -1)
    hidden = jnp.dot(weight_in, flat_in, preferred_element_type=jnp.float32).astype(jnp.bfloat16)
    padded = jnp.pad(hidden.astype(jnp.float32).reshape(grid_shape), pads)
    mixed = core(padded, filter_taps, 1) + filter_bias[:, None, None, None]
    active = gelu_value(mixed).astype(jnp.bfloat16)
    block_out = (flat_in.astype(jnp.float32) + jnp.dot(weight_out, active.reshape(channels, -1), preferred_element_type=jnp.float32)).astype(jnp.bfloat16).reshape(slab_shape)
    flat_grad = out_grad.reshape(channels, -1)
    act_grad = jnp.dot(weight_out.T, flat_grad, preferred_element_type=jnp.float32).astype(jnp.bfloat16)
    mix_grad = (act_grad.astype(jnp.float32).reshape(grid_shape) * gelu_slope(mixed)).astype(jnp.bfloat16)
    padded_grad = jnp.pad(mix_grad.astype(jnp.float32), pads)
    hid_grad = core(padded_grad, filter_taps, -1).astype(jnp.bfloat16)
    volume_grad = (flat_grad.astype(jnp.float32) + jnp.dot(weight_in.T, hid_grad.reshape(channels, -1), preferred_element_type=jnp.float32)).astype(jnp.bfloat16).reshape(slab_shape)
    return block_out, volume_grad
```

```python
import jax
import jax.numpy as jnp
from jax import lax
from jax.experimental import pallas as pl
from jax.experimental.pallas import tpu as pltpu
from jax.sharding import PartitionSpec as P

CX = 32
CY = 16
LANES = 128


root_half = 0.7071067811865476
inv_root_two_pi = 0.3989422804014327


def gelu_value(field):
    return 0.5 * field * (1.0 + lax.erf(field * root_half))


def gelu_slope(field):
    return (
        0.5 * (1.0 + lax.erf(field * root_half))
        + field * jnp.exp(-0.5 * field * field) * inv_root_two_pi
    )


def fill_padded(padded, own, row_low, row_high, plane_low, plane_high):
    planes, rows = own.shape[0], own.shape[1]
    for z in range(planes):
        padded[z + 1, 0] = row_low[z].astype(jnp.float32)
        padded[z + 1, rows + 1] = row_high[z].astype(jnp.float32)
        for y in range(rows):
            padded[z + 1, y + 1] = own[z, y].astype(jnp.float32)
    for y in range(rows + 2):
        padded[0, y] = plane_low[y].astype(jnp.float32)
        padded[planes + 1, y] = plane_high[y].astype(jnp.float32)


def stencil_row(padded, taps, z, y, flip):
    sums = [None, None, None]
    for a in range(3):
        for b in range(3):
            row = padded[z + a, y + b]
            for e in range(3):
                index = (a * 3 + b) * 3 + e
                tap = taps[26 - index if flip else index]
                term = row * tap[None, :]
                sums[e] = term if sums[e] is None else sums[e] + term
    x = lax.broadcasted_iota(jnp.int32, sums[0].shape, 0)
    extent = sums[0].shape[0]
    before = jnp.where(x == 0, 0.0, pltpu.roll(sums[0], 1, 0))
    after = jnp.where(x == extent - 1, 0.0, pltpu.roll(sums[2], extent - 1, 0))
    return sums[1] + (before + after)


def forward_kernel(own, row_low, row_high, plane_low, plane_high, taps, bias, active, slope, padded):
    fill_padded(padded, own, row_low, row_high, plane_low, plane_high)
    for z in range(own.shape[0]):
        for y in range(own.shape[1]):
            mixed = stencil_row(padded, taps, z, y, False) + bias[0][None, :]
            half = 0.5 * (1.0 + lax.erf(mixed * root_half))
            active[z, y] = (mixed * half).astype(active.dtype)
            slope[z, y] = half + mixed * jnp.exp(-0.5 * mixed * mixed) * inv_root_two_pi


def backward_kernel(own, row_low, row_high, plane_low, plane_high, taps, out, padded):
    fill_padded(padded, own, row_low, row_high, plane_low, plane_high)
    for z in range(own.shape[0]):
        for y in range(own.shape[1]):
            out[z, y] = stencil_row(padded, taps, z, y, True).astype(out.dtype)


def stencil(own, halo, taps, bias=None):
    planes, rows, extent, channels = own.shape

    def block(*lead):
        zeros = (0,) * len(lead)
        return pl.BlockSpec(lead + (LANES,), lambda c: zeros + (c,))

    in_specs = [
        block(planes, rows, extent),
        block(planes, extent),
        block(planes, extent),
        block(rows + 2, extent),
        block(rows + 2, extent),
        block(27),
    ]
    args = (own,) + halo + (taps,)
    scratch = [pltpu.VMEM((planes + 2, rows + 2, extent, LANES), jnp.float32)]
    shape = jax.ShapeDtypeStruct(own.shape, own.dtype)
    if bias is None:
        return pl.pallas_call(
            backward_kernel,
            grid=(channels // LANES,),
            in_specs=in_specs,
            out_specs=block(planes, rows, extent),
            out_shape=shape,
            scratch_shapes=scratch,
        )(*args)
    return pl.pallas_call(
        forward_kernel,
        grid=(channels // LANES,),
        in_specs=in_specs + [block(1)],
        out_specs=[block(planes, rows, extent)] * 2,
        out_shape=[shape, jax.ShapeDtypeStruct(own.shape, jnp.float32)],
        scratch_shapes=scratch,
    )(*args, bias)


def shift_pairs(axis):
    count = lax.axis_size(axis)
    forward = [(i, i + 1) for i in range(count - 1)]
    return forward, [(target, source) for source, target in forward]


def halo_of(field):
    forward, backward = shift_pairs("chan")
    row_low = lax.ppermute(field[:, -1], "chan", forward)
    row_high = lax.ppermute(field[:, 0], "chan", backward)
    forward, backward = shift_pairs("space")

    def plane(z):
        return jnp.concatenate([row_low[z][None], field[z], row_high[z][None]], axis=0)

    plane_low = lax.ppermute(plane(-1), "space", forward)
    plane_high = lax.ppermute(plane(0), "space", backward)
    return row_low, row_high, plane_low, plane_high


def split_cells_body(volume, out_grad, weight_in, weight_out, filter_taps, filter_bias):
    own, planes, cells = volume.shape
    parts = lax.axis_size("chan")
    rows = CY // parts
    channels = own * parts

    def to_cells(field):
        blocks = field.reshape(own, planes, parts, rows * CX).transpose(2, 1, 0, 3)
        return lax.all_to_all(blocks, "chan", split_axis=0, concat_axis=0, tiled=True)

    def to_channels(blocks):
        back = lax.all_to_all(blocks, "chan", split_axis=0, concat_axis=0, tiled=True)
        return back.transpose(2, 1, 0, 3).reshape(own, planes, cells)

    def gather(part):
        return lax.all_gather(part, "chan", axis=0, tiled=True)

    full_in, full_out = gather(weight_in), gather(weight_out)
    taps = gather(filter_taps).T
    bias = gather(filter_bias)[None, :]
    grid = (planes, rows, CX, channels)

    vol_cells = to_cells(volume)
    hidden = jnp.einsum(
        "kzcl,okc->zlo",
        vol_cells,
        full_in.reshape(channels, parts, own),
        preferred_element_type=jnp.float32,
    ).astype(jnp.bfloat16)
    hidden = hidden.reshape(grid)
    active, slope = stencil(hidden, halo_of(hidden), taps, bias)
    out_cells = jnp.einsum(
        "kcd,zld->kzcl",
        full_out.reshape(parts, own, channels),
        active.reshape(planes, rows * CX, channels),
        preferred_element_type=jnp.float32,
    )
    block_out = to_channels((vol_cells.astype(jnp.float32) + out_cells).astype(jnp.bfloat16))

    grad_cells = to_cells(out_grad)
    act_grad = jnp.einsum(
        "kzcl,kcd->zld",
        grad_cells,
        full_out.reshape(parts, own, channels),
        preferred_element_type=jnp.float32,
    ).astype(jnp.bfloat16)
    mix_grad = (act_grad.reshape(grid).astype(jnp.float32) * slope).astype(jnp.bfloat16)
    hid_grad = stencil(mix_grad, halo_of(mix_grad), taps)
    back_cells = jnp.einsum(
        "dkc,zld->kzcl",
        full_in.reshape(channels, parts, own),
        hid_grad.reshape(planes, rows * CX, channels),
        preferred_element_type=jnp.float32,
    )
    volume_grad = to_channels((grad_cells.astype(jnp.float32) + back_cells).astype(jnp.bfloat16))
    return block_out, volume_grad


def with_halo(block, axis, dim):
    forward, backward = shift_pairs(axis)
    low = lax.ppermute(lax.slice_in_dim(block, block.shape[dim] - 1, None, axis=dim), axis, forward)
    high = lax.ppermute(lax.slice_in_dim(block, 0, 1, axis=dim), axis, backward)
    return jnp.concatenate([low, block, high], axis=dim)


def core(padded, filter_taps, direction):
    extent_z = padded.shape[1] - 2
    extent_y = padded.shape[2] - 2
    extent_x = padded.shape[3] - 2
    summed = jnp.zeros((padded.shape[0], extent_z, extent_y, extent_x), jnp.float32)
    for shift_z in range(3):
        for shift_y in range(3):
            for shift_x in range(3):
                tap_index = (shift_z * 3 + shift_y) * 3 + shift_x
                begin_z = 1 + direction * (shift_z - 1)
                begin_y = 1 + direction * (shift_y - 1)
                begin_x = 1 + direction * (shift_x - 1)
                window = padded[
                    :,
                    begin_z : begin_z + extent_z,
                    begin_y : begin_y + extent_y,
                    begin_x : begin_x + extent_x,
                ]
                summed = summed + filter_taps[:, tap_index][:, None, None, None] * window
    return summed


def lift(field_z):
    extended = field_z.astype(jnp.float32).reshape(field_z.shape[0], field_z.shape[1], CY, CX)
    return jnp.pad(extended, ((0, 0), (0, 0), (1, 1), (1, 1)))


def exchange_body(volume, out_grad, weight_in, weight_out, filter_taps, filter_bias):
    slab_shape = volume.shape
    contract_first = (((0,), (0,)), ((), ()))

    def to_cells(field):
        return lax.all_to_all(
            field.reshape(field.shape[0], -1), "chan", split_axis=1, concat_axis=0, tiled=True
        )

    def to_channels(field):
        return lax.all_to_all(field, "chan", split_axis=0, concat_axis=1, tiled=True).reshape(
            slab_shape
        )

    full_in = lax.all_gather(weight_in, "chan", axis=0, tiled=True)
    full_out = lax.all_gather(weight_out, "chan", axis=0, tiled=True)
    vol_cells = to_cells(volume)
    hidden = to_channels(
        jnp.dot(full_in, vol_cells, preferred_element_type=jnp.float32).astype(jnp.bfloat16)
    )
    padded = lift(with_halo(hidden, "space", 1))
    mixed = core(padded, filter_taps, 1) + filter_bias[:, None, None, None]
    active = gelu_value(mixed).astype(jnp.bfloat16).reshape(slab_shape)
    out_cells = vol_cells.astype(jnp.float32) + jnp.dot(
        full_out, to_cells(active), preferred_element_type=jnp.float32
    )
    block_out = to_channels(out_cells.astype(jnp.bfloat16))
    grad_cells = to_cells(out_grad)
    act_part = lax.dot_general(
        full_out, grad_cells, contract_first, preferred_element_type=jnp.float32
    )
    act_grad = to_channels(act_part.astype(jnp.bfloat16))
    slope = gelu_slope(mixed)
    mix_grad = (
        (act_grad.astype(jnp.float32).reshape(slope.shape) * slope)
        .astype(jnp.bfloat16)
        .reshape(slab_shape)
    )
    padded_grad = lift(with_halo(mix_grad, "space", 1))
    hid_grad = core(padded_grad, filter_taps, -1).astype(jnp.bfloat16).reshape(slab_shape)
    back_part = lax.dot_general(
        full_in, to_cells(hid_grad), contract_first, preferred_element_type=jnp.float32
    )
    volume_grad = to_channels((grad_cells.astype(jnp.float32) + back_part).astype(jnp.bfloat16))
    return block_out, volume_grad


def solution(mesh):
    field = P(("groups", "chan"), "space", None)
    placed = (field, field, P("chan", None), P("chan", None), P("chan", None), P("chan"))
    parts = mesh.shape["chan"]
    whole_rows = CY % parts == 0 and (CY // parts * CX) % LANES == 0
    return jax.shard_map(
        split_cells_body if whole_rows else exchange_body,
        mesh=mesh,
        in_specs=placed,
        out_specs=(field, field),
        check_vma=False,
    )
```

```python
import jax
import jax.numpy as jnp
from jax import lax
from jax.experimental import pallas as pl
from jax.experimental.pallas import tpu as pltpu
from jax.sharding import PartitionSpec as P

CX = 32
CY = 16
LANES = 128


root_half = 0.7071067811865476
inv_root_two_pi = 0.3989422804014327


def gelu_value(field):
    return 0.5 * field * (1.0 + lax.erf(field * root_half))


def gelu_slope(field):
    return (
        0.5 * (1.0 + lax.erf(field * root_half))
        + field * jnp.exp(-0.5 * field * field) * inv_root_two_pi
    )


def fill_padded(padded, own, row_low, row_high, plane_low, plane_high):
    planes, rows = own.shape[0], own.shape[1]
    for z in range(planes):
        padded[z + 1, 0] = row_low[z].astype(jnp.float32)
        padded[z + 1, rows + 1] = row_high[z].astype(jnp.float32)
        for y in range(rows):
            padded[z + 1, y + 1] = own[z, y].astype(jnp.float32)
    for y in range(rows + 2):
        padded[0, y] = plane_low[y].astype(jnp.float32)
        padded[planes + 1, y] = plane_high[y].astype(jnp.float32)


def stencil_row(padded, taps, z, y, flip):
    sums = [None, None, None]
    for a in range(3):
        for b in range(3):
            row = padded[z + a, y + b]
            for e in range(3):
                index = (a * 3 + b) * 3 + e
                tap = taps[26 - index if flip else index]
                term = row * tap[None, :]
                sums[e] = term if sums[e] is None else sums[e] + term
    x = lax.broadcasted_iota(jnp.int32, sums[0].shape, 0)
    extent = sums[0].shape[0]
    before = jnp.where(x == 0, 0.0, pltpu.roll(sums[0], 1, 0))
    after = jnp.where(x == extent - 1, 0.0, pltpu.roll(sums[2], extent - 1, 0))
    return sums[1] + (before + after)


def forward_kernel(
    here, own, row_low, row_high, plane_low, plane_high, taps, bias, weight, *rest
):
    count = (len(rest) - 3) // 2
    inputs, outputs = rest[:count], rest[count : 2 * count]
    slope, padded, active = rest[2 * count :]
    step = pl.program_id(0)
    planes, rows, extent = own.shape[:3]
    fill_padded(padded, own, row_low, row_high, plane_low, plane_high)
    lanes = pl.ds(pl.multiple_of(step * LANES, LANES), LANES)
    for z in range(planes):
        for y in range(rows):
            mixed = stencil_row(padded, taps, z, y, False) + bias[0][None, :]
            half = 0.5 * (1.0 + lax.erf(mixed * root_half))
            at = (z * rows + y) * extent
            active[at : at + extent, lanes] = (mixed * half).astype(active.dtype)
            slope[z, y] = half + mixed * jnp.exp(-0.5 * mixed * mixed) * inv_root_two_pi

    @pl.when(step == pl.num_programs(0) - 1)
    def _():
        own_channels = inputs[0].shape[0]
        for shift in range(count):
            start = pl.multiple_of((here[0] ^ shift) * own_channels, own_channels)
            product = lax.dot_general(
                weight[pl.ds(start, own_channels), :],
                active[...],
                (((1,), (1,)), ((), ())),
                preferred_element_type=jnp.float32,
            )
            total = inputs[shift][...].astype(jnp.float32) + product
            outputs[shift][...] = total.astype(outputs[shift].dtype)


def backward_kernel(here, own, row_low, row_high, plane_low, plane_high, taps, weight, *rest):
    count = (len(rest) - 2) // 2
    inputs, outputs = rest[:count], rest[count : 2 * count]
    padded, grads = rest[2 * count :]
    step = pl.program_id(0)
    planes, rows, extent = own.shape[:3]
    fill_padded(padded, own, row_low, row_high, plane_low, plane_high)
    lanes = pl.ds(pl.multiple_of(step * LANES, LANES), LANES)
    for z in range(planes):
        for y in range(rows):
            at = (z * rows + y) * extent
            total = stencil_row(padded, taps, z, y, True)
            grads[at : at + extent, lanes] = total.astype(grads.dtype)

    @pl.when(step == pl.num_programs(0) - 1)
    def _():
        own_channels = inputs[0].shape[0]
        for shift in range(count):
            start = pl.multiple_of((here[0] ^ shift) * own_channels, own_channels)
            product = jnp.dot(
                grads[...],
                weight[:, pl.ds(start, own_channels)],
                preferred_element_type=jnp.float32,
            )
            total = inputs[shift][...].astype(jnp.float32) + product.T
            outputs[shift][...] = total.astype(outputs[shift].dtype)


def stencil(here, own, halo, taps, bias, weight, blocks):
    planes, rows, extent, channels = own.shape
    cells = planes * rows * extent

    def block(*lead):
        zeros = (0,) * len(lead)
        return pl.BlockSpec(lead + (LANES,), lambda c, here: zeros + (c,))

    def resident(shape):
        return pl.BlockSpec(shape, lambda c, here: (0,) * len(shape), pipeline_mode=pl.Buffered(1))

    in_specs = [
        block(planes, rows, extent),
        block(planes, extent),
        block(planes, extent),
        block(rows + 2, extent),
        block(rows + 2, extent),
        block(27),
    ]
    args = [own, *halo, taps]
    out_specs = [resident(piece.shape) for piece in blocks]
    out_shape = [jax.ShapeDtypeStruct(piece.shape, piece.dtype) for piece in blocks]
    if bias is not None:
        in_specs.append(block(1))
        args.append(bias)
        out_specs.append(block(planes, rows, extent))
        out_shape.append(jax.ShapeDtypeStruct(own.shape, jnp.float32))
    in_specs += [resident(weight.shape)] + [resident(piece.shape) for piece in blocks]
    return pl.pallas_call(
        backward_kernel if bias is None else forward_kernel,
        grid_spec=pltpu.PrefetchScalarGridSpec(
            num_scalar_prefetch=1,
            grid=(channels // LANES,),
            in_specs=in_specs,
            out_specs=out_specs,
            scratch_shapes=[
                pltpu.VMEM((planes + 2, rows + 2, extent, LANES), jnp.float32),
                pltpu.VMEM((cells, channels), own.dtype),
            ],
        ),
        out_shape=out_shape,
    )(here, *args, weight, *blocks)


def turn_kernel(here, *refs, count):
    inputs, turned = refs[:count], refs[-1]

    @pl.when(pl.program_id(0) == 0)
    def _():
        own = inputs[0].shape[0]
        for shift in range(count):
            start = pl.multiple_of((here[0] ^ shift) * own, own)
            turned[:, pl.ds(start, own)] = inputs[shift][...].T


def hidden_kernel(here, *refs, count):
    turn_kernel(here, *refs, count=count)
    weight, out, turned = refs[count:]
    out[...] = lax.dot_general(
        turned[...],
        weight[...],
        (((1,), (1,)), ((), ())),
        preferred_element_type=jnp.float32,
    ).astype(out.dtype)


def mix_kernel(here, *refs, count):
    turn_kernel(here, *refs, count=count)
    weight, slope, out, turned = refs[count:]
    grad = jnp.dot(turned[...], weight[...], preferred_element_type=jnp.float32)
    grad = grad.astype(out.dtype).astype(jnp.float32)
    out[...] = (grad * slope[...]).astype(out.dtype)


def product_call(here, blocks, weight, slope=None):
    own, cells = blocks[0].shape
    channels = weight.shape[0]
    count = len(blocks)
    width = 2 * LANES
    columns = pl.BlockSpec((cells, width), lambda c, here: (0, c))
    whole = pl.BlockSpec((own, cells), lambda c, here: (0, 0), pipeline_mode=pl.Buffered(1))
    if slope is None:
        kernel, extra = hidden_kernel, []
        weight_spec = pl.BlockSpec((width, channels), lambda c, here: (c, 0))
    else:
        kernel, extra = mix_kernel, [slope]
        weight_spec = pl.BlockSpec((channels, width), lambda c, here: (0, c))
    return pl.pallas_call(
        lambda *refs: kernel(*refs, count=count),
        grid_spec=pltpu.PrefetchScalarGridSpec(
            num_scalar_prefetch=1,
            grid=(channels // width,),
            in_specs=[whole] * count + [weight_spec] + [columns] * len(extra),
            out_specs=columns,
            scratch_shapes=[pltpu.VMEM((cells, channels), blocks[0].dtype)],
        ),
        out_shape=jax.ShapeDtypeStruct((cells, channels), blocks[0].dtype),
    )(here, *blocks, weight, *extra)


def place_kernel(here, mine, other, full_in, full_out, sems):
    chan, seat = here[0], here[1]
    copies = []
    for side, pieces in enumerate((mine, other)):
        for turn in range(pieces.shape[0]):
            for shift in range(pieces.shape[1]):
                for which, full in enumerate((full_in, full_out)):
                    copies.append(
                        pltpu.make_async_copy(
                            pieces.at[turn, shift, which],
                            full.at[chan ^ shift, seat ^ side ^ (2 * turn)],
                            sems.at[len(copies)],
                        )
                    )
    for copy in copies:
        copy.start()
    for copy in copies:
        copy.wait()


def place(here, mine, other):
    turns, parts, _, share, channels = mine.shape
    full = jax.ShapeDtypeStruct((parts, 2 * turns, share, channels), mine.dtype)
    anywhere = pl.BlockSpec(memory_space=pl.ANY)
    found = pl.pallas_call(
        place_kernel,
        in_specs=[pl.BlockSpec(memory_space=pltpu.SMEM), anywhere, anywhere],
        out_specs=[anywhere] * 2,
        out_shape=[full] * 2,
        scratch_shapes=[pltpu.SemaphoreType.DMA((4 * turns * parts,))],
    )(here, mine, other)
    return [weight.reshape(channels, channels) for weight in found]


def shift_pairs(axis):
    count = lax.axis_size(axis)
    forward = [(i, i + 1) for i in range(count - 1)]
    return forward, [(target, source) for source, target in forward]


def split_cells_body(volume, out_grad, weight_in, weight_out, filter_taps, filter_bias):
    own, planes, cells = volume.shape
    parts = lax.axis_size("chan")
    rows = CY // parts
    width = rows * CX
    channels = own * parts
    others = ("groups", "space")
    seat = lax.axis_index(others)
    chan = lax.axis_index("chan")
    share = own // lax.axis_size(others)
    here = jnp.stack([chan, seat]).astype(jnp.int32)
    shifts = sorted(range(1, parts), key=lambda shift: (shift & (parts // 2) == 0, shift))

    def swap(part, axes, partner):
        count = lax.axis_size(axes)
        return lax.ppermute(part, axes, [(i, partner(i)) for i in range(count)])

    def exchange(blocks):
        got = {0: blocks(0)}
        for shift in shifts:
            got[shift] = swap(blocks(shift), "chan", lambda i: i ^ shift)
        return [got[shift] for shift in range(parts)]

    def cut(field):
        def blocks(shift):
            start = (chan ^ shift) * width
            piece = lax.dynamic_slice_in_dim(field, start, width, axis=2)
            return piece.reshape(own, planes * width)

        return blocks

    def paste(pieces):
        field = jnp.zeros((own, planes, cells), pieces[0].dtype)
        for shift in [0] + shifts:
            piece = pieces[shift].reshape(own, planes, width)
            field = lax.dynamic_update_slice_in_dim(field, piece, (chan ^ shift) * width, axis=2)
        return field

    def gather_weights():
        begin = seat * share
        pair = jnp.stack(
            [
                lax.dynamic_slice_in_dim(weight, begin, share, axis=0)
                for weight in (weight_in, weight_out)
            ]
        )
        column = jnp.stack(exchange(lambda shift: pair))
        over_x = swap(column, others, lambda i: i ^ 2)
        over_y = swap(column, others, lambda i: i ^ 4)
        mixed = jnp.where(seat & 1 == 0, over_y, over_x)
        far = swap(mixed, others, lambda i: i ^ (4 if i & 1 else 2))
        mine = jnp.stack([column, over_x, over_y, far])
        other = swap(mine, others, lambda i: i ^ 1)
        return place(here, mine, other)

    def gather_taps():
        table = jnp.concatenate([filter_taps, filter_bias[:, None]], axis=1).T
        found = exchange(lambda shift: table)
        full = jnp.zeros((28, channels), jnp.float32)
        for shift in range(parts):
            full = lax.dynamic_update_slice_in_dim(full, found[shift], (chan ^ shift) * own, axis=1)
        return full[:27], full[27:]

    def halo_of(field):
        forward, backward = shift_pairs("chan")
        row_low = lax.ppermute(field[:, -1], "chan", forward)
        row_high = lax.ppermute(field[:, 0], "chan", backward)
        forward, backward = shift_pairs("space")

        def plane(z):
            return jnp.concatenate([row_low[z][None], field[z], row_high[z][None]], axis=0)

        plane_low = lax.ppermute(plane(-1), "space", forward)
        plane_high = lax.ppermute(plane(0), "space", backward)
        return row_low, row_high, plane_low, plane_high

    grid = (planes, rows, CX, channels)
    full_in, full_out = gather_weights()
    taps, bias = gather_taps()
    vol_blocks = exchange(cut(volume))
    grad_blocks = exchange(cut(out_grad))
    hidden = in_grid(product_call(here, vol_blocks, full_in), grid)
    *out_blocks, slope = stencil(here, hidden, halo_of(hidden), taps, bias, full_out, vol_blocks)
    block_out = paste(exchange(lambda shift: out_blocks[shift]))
    mix_grad = product_call(here, grad_blocks, full_out, slope.reshape(planes * width, channels))
    mix_grad = in_grid(mix_grad, grid)
    back_blocks = stencil(here, mix_grad, halo_of(mix_grad), taps, None, full_in, grad_blocks)
    volume_grad = paste(exchange(lambda shift: back_blocks[shift]))
    return block_out, volume_grad


def in_grid(field, grid):
    return field.reshape(grid)


def with_halo(block, axis, dim):
    forward, backward = shift_pairs(axis)
    low = lax.ppermute(lax.slice_in_dim(block, block.shape[dim] - 1, None, axis=dim), axis, forward)
    high = lax.ppermute(lax.slice_in_dim(block, 0, 1, axis=dim), axis, backward)
    return jnp.concatenate([low, block, high], axis=dim)


def core(padded, filter_taps, direction):
    extent_z = padded.shape[1] - 2
    extent_y = padded.shape[2] - 2
    extent_x = padded.shape[3] - 2
    summed = jnp.zeros((padded.shape[0], extent_z, extent_y, extent_x), jnp.float32)
    for shift_z in range(3):
        for shift_y in range(3):
            for shift_x in range(3):
                tap_index = (shift_z * 3 + shift_y) * 3 + shift_x
                begin_z = 1 + direction * (shift_z - 1)
                begin_y = 1 + direction * (shift_y - 1)
                begin_x = 1 + direction * (shift_x - 1)
                window = padded[
                    :,
                    begin_z : begin_z + extent_z,
                    begin_y : begin_y + extent_y,
                    begin_x : begin_x + extent_x,
                ]
                summed = summed + filter_taps[:, tap_index][:, None, None, None] * window
    return summed


def lift(field_z):
    extended = field_z.astype(jnp.float32).reshape(field_z.shape[0], field_z.shape[1], CY, CX)
    return jnp.pad(extended, ((0, 0), (0, 0), (1, 1), (1, 1)))


def exchange_body(volume, out_grad, weight_in, weight_out, filter_taps, filter_bias):
    slab_shape = volume.shape
    contract_first = (((0,), (0,)), ((), ()))

    def to_cells(field):
        return lax.all_to_all(
            field.reshape(field.shape[0], -1), "chan", split_axis=1, concat_axis=0, tiled=True
        )

    def to_channels(field):
        return lax.all_to_all(field, "chan", split_axis=0, concat_axis=1, tiled=True).reshape(
            slab_shape
        )

    full_in = lax.all_gather(weight_in, "chan", axis=0, tiled=True)
    full_out = lax.all_gather(weight_out, "chan", axis=0, tiled=True)
    vol_cells = to_cells(volume)
    hidden = to_channels(
        jnp.dot(full_in, vol_cells, preferred_element_type=jnp.float32).astype(jnp.bfloat16)
    )
    padded = lift(with_halo(hidden, "space", 1))
    mixed = core(padded, filter_taps, 1) + filter_bias[:, None, None, None]
    active = gelu_value(mixed).astype(jnp.bfloat16).reshape(slab_shape)
    out_cells = vol_cells.astype(jnp.float32) + jnp.dot(
        full_out, to_cells(active), preferred_element_type=jnp.float32
    )
    block_out = to_channels(out_cells.astype(jnp.bfloat16))
    grad_cells = to_cells(out_grad)
    act_part = lax.dot_general(
        full_out, grad_cells, contract_first, preferred_element_type=jnp.float32
    )
    act_grad = to_channels(act_part.astype(jnp.bfloat16))
    slope = gelu_slope(mixed)
    mix_grad = (
        (act_grad.astype(jnp.float32).reshape(slope.shape) * slope)
        .astype(jnp.bfloat16)
        .reshape(slab_shape)
    )
    padded_grad = lift(with_halo(mix_grad, "space", 1))
    hid_grad = core(padded_grad, filter_taps, -1).astype(jnp.bfloat16).reshape(slab_shape)
    back_part = lax.dot_general(
        full_in, to_cells(hid_grad), contract_first, preferred_element_type=jnp.float32
    )
    volume_grad = to_channels((grad_cells.astype(jnp.float32) + back_part).astype(jnp.bfloat16))
    return block_out, volume_grad


def body(volume, out_grad, weight_in, weight_out, filter_taps, filter_bias):
    own = volume.shape[0]
    parts = lax.axis_size("chan")
    groups, space = lax.axis_size("groups"), lax.axis_size("space")
    whole_rows = CY % parts == 0 and (CY // parts * CX) % LANES == 0 and parts & (parts - 1) == 0
    whole_shares = own % LANES == 0 and own % (16 * groups * space) == 0
    split = whole_rows and whole_shares and (groups, space) == (2, 4)
    chosen = split_cells_body if split else exchange_body
    return chosen(volume, out_grad, weight_in, weight_out, filter_taps, filter_bias)


def solution(mesh):
    field = P(("groups", "chan"), "space", None)
    placed = (field, field, P("chan", None), P("chan", None), P("chan", None), P("chan"))
    return jax.shard_map(
        body,
        mesh=mesh,
        in_specs=placed,
        out_specs=(field, field),
        check_vma=False,
    )
```

```python
import jax
import jax.numpy as jnp
from jax import lax
from jax.experimental import pallas as pl
from jax.experimental.pallas import tpu as pltpu
from jax.sharding import PartitionSpec as P

CX = 32
CY = 16
LANES = 128


root_half = 0.7071067811865476
inv_root_two_pi = 0.3989422804014327


def gelu_value(field):
    return 0.5 * field * (1.0 + lax.erf(field * root_half))


def gelu_slope(field):
    return (
        0.5 * (1.0 + lax.erf(field * root_half))
        + field * jnp.exp(-0.5 * field * field) * inv_root_two_pi
    )


def fill_padded(padded, own, row_low, row_high, plane_low, plane_high):
    planes, rows = own.shape[0], own.shape[1]
    for z in range(planes):
        padded[z + 1, 0] = row_low[z].astype(jnp.float32)
        padded[z + 1, rows + 1] = row_high[z].astype(jnp.float32)
        for y in range(rows):
            padded[z + 1, y + 1] = own[z, y].astype(jnp.float32)
    for y in range(rows + 2):
        padded[0, y] = plane_low[y].astype(jnp.float32)
        padded[planes + 1, y] = plane_high[y].astype(jnp.float32)


def stencil_row(padded, taps, z, y, flip):
    sums = [None, None, None]
    for a in range(3):
        for b in range(3):
            row = padded[z + a, y + b]
            for e in range(3):
                index = (a * 3 + b) * 3 + e
                tap = taps[26 - index if flip else index]
                term = row * tap[None, :]
                sums[e] = term if sums[e] is None else sums[e] + term
    x = lax.broadcasted_iota(jnp.int32, sums[0].shape, 0)
    extent = sums[0].shape[0]
    before = jnp.where(x == 0, 0.0, pltpu.roll(sums[0], 1, 0))
    after = jnp.where(x == extent - 1, 0.0, pltpu.roll(sums[2], extent - 1, 0))
    return sums[1] + (before + after)


def forward_kernel(
    here, own, row_low, row_high, plane_low, plane_high, taps, bias, weight, *rest
):
    count = (len(rest) - 3) // 2
    inputs, outputs = rest[:count], rest[count : 2 * count]
    slope, padded, active = rest[2 * count :]
    step = pl.program_id(0)
    planes, rows, extent = own.shape[:3]
    fill_padded(padded, own, row_low, row_high, plane_low, plane_high)
    lanes = pl.ds(pl.multiple_of(step * LANES, LANES), LANES)
    for z in range(planes):
        for y in range(rows):
            mixed = stencil_row(padded, taps, z, y, False) + bias[0][None, :]
            half = 0.5 * (1.0 + lax.erf(mixed * root_half))
            at = (z * rows + y) * extent
            active[at : at + extent, lanes] = (mixed * half).astype(active.dtype)
            slope[z, y] = half + mixed * jnp.exp(-0.5 * mixed * mixed) * inv_root_two_pi

    @pl.when(step == pl.num_programs(0) - 1)
    def _():
        own_channels = inputs[0].shape[0]
        for shift in range(count):
            start = pl.multiple_of((here[0] ^ shift) * own_channels, own_channels)
            product = lax.dot_general(
                weight[pl.ds(start, own_channels), :],
                active[...],
                (((1,), (1,)), ((), ())),
                preferred_element_type=jnp.float32,
            )
            total = inputs[shift][...].astype(jnp.float32) + product
            outputs[shift][...] = total.astype(outputs[shift].dtype)


def backward_kernel(here, own, row_low, row_high, plane_low, plane_high, taps, weight, *rest):
    count = (len(rest) - 2) // 2
    inputs, outputs = rest[:count], rest[count : 2 * count]
    padded, grads = rest[2 * count :]
    step = pl.program_id(0)
    planes, rows, extent = own.shape[:3]
    fill_padded(padded, own, row_low, row_high, plane_low, plane_high)
    lanes = pl.ds(pl.multiple_of(step * LANES, LANES), LANES)
    for z in range(planes):
        for y in range(rows):
            at = (z * rows + y) * extent
            total = stencil_row(padded, taps, z, y, True)
            grads[at : at + extent, lanes] = total.astype(grads.dtype)

    @pl.when(step == pl.num_programs(0) - 1)
    def _():
        own_channels = inputs[0].shape[0]
        for shift in range(count):
            start = pl.multiple_of((here[0] ^ shift) * own_channels, own_channels)
            product = jnp.dot(
                grads[...],
                weight[:, pl.ds(start, own_channels)],
                preferred_element_type=jnp.float32,
            )
            total = inputs[shift][...].astype(jnp.float32) + product.T
            outputs[shift][...] = total.astype(outputs[shift].dtype)


def stencil(here, own, halo, taps, bias, weight, blocks):
    planes, rows, extent, channels = own.shape
    cells = planes * rows * extent

    def block(*lead):
        zeros = (0,) * len(lead)
        return pl.BlockSpec(lead + (LANES,), lambda c, here: zeros + (c,))

    def resident(shape):
        return pl.BlockSpec(shape, lambda c, here: (0,) * len(shape), pipeline_mode=pl.Buffered(1))

    in_specs = [
        block(planes, rows, extent),
        block(planes, extent),
        block(planes, extent),
        block(rows + 2, extent),
        block(rows + 2, extent),
        block(27),
    ]
    args = [own, *halo, taps]
    out_specs = [resident(piece.shape) for piece in blocks]
    out_shape = [jax.ShapeDtypeStruct(piece.shape, piece.dtype) for piece in blocks]
    if bias is not None:
        in_specs.append(block(1))
        args.append(bias)
        out_specs.append(block(planes, rows, extent))
        out_shape.append(jax.ShapeDtypeStruct(own.shape, jnp.float32))
    in_specs += [resident(weight.shape)] + [resident(piece.shape) for piece in blocks]
    return pl.pallas_call(
        backward_kernel if bias is None else forward_kernel,
        grid_spec=pltpu.PrefetchScalarGridSpec(
            num_scalar_prefetch=1,
            grid=(channels // LANES,),
            in_specs=in_specs,
            out_specs=out_specs,
            scratch_shapes=[
                pltpu.VMEM((planes + 2, rows + 2, extent, LANES), jnp.float32),
                pltpu.VMEM((cells, channels), own.dtype),
            ],
        ),
        out_shape=out_shape,
    )(here, *args, weight, *blocks)


def turn_kernel(here, *refs, count):
    inputs, turned = refs[:count], refs[-1]

    @pl.when(pl.program_id(0) == 0)
    def _():
        own = inputs[0].shape[0]
        for shift in range(count):
            start = pl.multiple_of((here[0] ^ shift) * own, own)
            turned[:, pl.ds(start, own)] = inputs[shift][...].T


def hidden_kernel(here, *refs, count):
    turn_kernel(here, *refs, count=count)
    weight, out, turned = refs[count:]
    out[...] = lax.dot_general(
        turned[...],
        weight[...],
        (((1,), (1,)), ((), ())),
        preferred_element_type=jnp.float32,
    ).astype(out.dtype)


def mix_kernel(here, *refs, count):
    turn_kernel(here, *refs, count=count)
    weight, slope, out, turned = refs[count:]
    grad = jnp.dot(turned[...], weight[...], preferred_element_type=jnp.float32)
    grad = grad.astype(out.dtype).astype(jnp.float32)
    out[...] = (grad * slope[...]).astype(out.dtype)


def product_call(here, blocks, weight, slope=None):
    own, cells = blocks[0].shape
    channels = weight.shape[0]
    count = len(blocks)
    width = 2 * LANES
    columns = pl.BlockSpec((cells, width), lambda c, here: (0, c))
    whole = pl.BlockSpec((own, cells), lambda c, here: (0, 0), pipeline_mode=pl.Buffered(1))
    if slope is None:
        kernel, extra = hidden_kernel, []
        weight_spec = pl.BlockSpec((width, channels), lambda c, here: (c, 0))
    else:
        kernel, extra = mix_kernel, [slope]
        weight_spec = pl.BlockSpec((channels, width), lambda c, here: (0, c))
    return pl.pallas_call(
        lambda *refs: kernel(*refs, count=count),
        grid_spec=pltpu.PrefetchScalarGridSpec(
            num_scalar_prefetch=1,
            grid=(channels // width,),
            in_specs=[whole] * count + [weight_spec] + [columns] * len(extra),
            out_specs=columns,
            scratch_shapes=[pltpu.VMEM((cells, channels), blocks[0].dtype)],
        ),
        out_shape=jax.ShapeDtypeStruct((cells, channels), blocks[0].dtype),
    )(here, *blocks, weight, *extra)


def place_kernel(here, mine, other, full_in, full_out):
    chan, side = here[0], here[1] & 1
    for shift in range(mine.shape[1]):
        for which, full in enumerate((full_in, full_out)):
            full[chan ^ shift, 0, side] = mine[0, shift, which]
            full[chan ^ shift, 0, side ^ 1] = other[0, shift, which]


def place(here, mine, other):
    turns, parts, _, share, channels = mine.shape
    full = jax.ShapeDtypeStruct((parts, turns, 2, share, channels), mine.dtype)
    pieces = pl.BlockSpec((1,) + mine.shape[1:], lambda turn, here: (turn, 0, 0, 0, 0))
    placed = pl.BlockSpec(
        (parts, 1, 2, share, channels), lambda turn, here: (0, (here[1] >> 1) ^ turn, 0, 0, 0)
    )
    found = pl.pallas_call(
        place_kernel,
        grid_spec=pltpu.PrefetchScalarGridSpec(
            num_scalar_prefetch=1,
            grid=(turns,),
            in_specs=[pieces, pieces],
            out_specs=[placed, placed],
        ),
        out_shape=[full] * 2,
    )(here, mine, other)
    return [weight.reshape(channels, channels) for weight in found]


def shift_pairs(axis):
    count = lax.axis_size(axis)
    forward = [(i, i + 1) for i in range(count - 1)]
    return forward, [(target, source) for source, target in forward]


def split_cells_body(volume, out_grad, weight_in, weight_out, filter_taps, filter_bias):
    own, planes, cells = volume.shape
    parts = lax.axis_size("chan")
    rows = CY // parts
    width = rows * CX
    channels = own * parts
    others = ("groups", "space")
    seat = lax.axis_index(others)
    chan = lax.axis_index("chan")
    share = own // lax.axis_size(others)
    here = jnp.stack([chan, seat]).astype(jnp.int32)
    shifts = sorted(range(1, parts), key=lambda shift: (shift & (parts // 2) == 0, shift))

    def swap(part, axes, partner):
        count = lax.axis_size(axes)
        return lax.ppermute(part, axes, [(i, partner(i)) for i in range(count)])

    def exchange(blocks):
        got = {0: blocks(0)}
        for shift in shifts:
            got[shift] = swap(blocks(shift), "chan", lambda i: i ^ shift)
        return [got[shift] for shift in range(parts)]

    def cut(field):
        def blocks(shift):
            start = (chan ^ shift) * width
            piece = lax.dynamic_slice_in_dim(field, start, width, axis=2)
            return piece.reshape(own, planes * width)

        return blocks

    def paste(pieces):
        field = jnp.zeros((own, planes, cells), pieces[0].dtype)
        for shift in [0] + shifts:
            piece = pieces[shift].reshape(own, planes, width)
            field = lax.dynamic_update_slice_in_dim(field, piece, (chan ^ shift) * width, axis=2)
        return field

    def gather_weights():
        begin = seat * share
        pair = jnp.stack(
            [
                lax.dynamic_slice_in_dim(weight, begin, share, axis=0)
                for weight in (weight_in, weight_out)
            ]
        )
        column = jnp.stack(exchange(lambda shift: pair))
        over_x = swap(column, others, lambda i: i ^ 2)
        over_y = swap(column, others, lambda i: i ^ 4)
        mixed = jnp.where(seat & 1 == 0, over_y, over_x)
        far = swap(mixed, others, lambda i: i ^ (4 if i & 1 else 2))
        mine = jnp.stack([column, over_x, over_y, far])
        other = swap(mine, others, lambda i: i ^ 1)
        return place(here, mine, other)

    def gather_taps():
        table = jnp.concatenate([filter_taps, filter_bias[:, None]], axis=1).T
        found = exchange(lambda shift: table)
        full = jnp.zeros((28, channels), jnp.float32)
        for shift in range(parts):
            full = lax.dynamic_update_slice_in_dim(full, found[shift], (chan ^ shift) * own, axis=1)
        return full[:27], full[27:]

    def halo_of(field):
        forward, backward = shift_pairs("chan")
        row_low = lax.ppermute(field[:, -1], "chan", forward)
        row_high = lax.ppermute(field[:, 0], "chan", backward)
        forward, backward = shift_pairs("space")

        def plane(z):
            return jnp.concatenate([row_low[z][None], field[z], row_high[z][None]], axis=0)

        plane_low = lax.ppermute(plane(-1), "space", forward)
        plane_high = lax.ppermute(plane(0), "space", backward)
        return row_low, row_high, plane_low, plane_high

    grid = (planes, rows, CX, channels)
    taps, bias = gather_taps()
    full_in, full_out = gather_weights()
    vol_blocks = exchange(cut(volume))
    grad_blocks = exchange(cut(out_grad))
    hidden = in_grid(product_call(here, vol_blocks, full_in), grid)
    *out_blocks, slope = stencil(here, hidden, halo_of(hidden), taps, bias, full_out, vol_blocks)
    block_out = paste(exchange(lambda shift: out_blocks[shift]))
    mix_grad = product_call(here, grad_blocks, full_out, slope.reshape(planes * width, channels))
    mix_grad = in_grid(mix_grad, grid)
    back_blocks = stencil(here, mix_grad, halo_of(mix_grad), taps, None, full_in, grad_blocks)
    volume_grad = paste(exchange(lambda shift: back_blocks[shift]))
    return block_out, volume_grad


def in_grid(field, grid):
    return field.reshape(grid)


def with_halo(block, axis, dim):
    forward, backward = shift_pairs(axis)
    low = lax.ppermute(lax.slice_in_dim(block, block.shape[dim] - 1, None, axis=dim), axis, forward)
    high = lax.ppermute(lax.slice_in_dim(block, 0, 1, axis=dim), axis, backward)
    return jnp.concatenate([low, block, high], axis=dim)


def core(padded, filter_taps, direction):
    extent_z = padded.shape[1] - 2
    extent_y = padded.shape[2] - 2
    extent_x = padded.shape[3] - 2
    summed = jnp.zeros((padded.shape[0], extent_z, extent_y, extent_x), jnp.float32)
    for shift_z in range(3):
        for shift_y in range(3):
            for shift_x in range(3):
                tap_index = (shift_z * 3 + shift_y) * 3 + shift_x
                begin_z = 1 + direction * (shift_z - 1)
                begin_y = 1 + direction * (shift_y - 1)
                begin_x = 1 + direction * (shift_x - 1)
                window = padded[
                    :,
                    begin_z : begin_z + extent_z,
                    begin_y : begin_y + extent_y,
                    begin_x : begin_x + extent_x,
                ]
                summed = summed + filter_taps[:, tap_index][:, None, None, None] * window
    return summed


def lift(field_z):
    extended = field_z.astype(jnp.float32).reshape(field_z.shape[0], field_z.shape[1], CY, CX)
    return jnp.pad(extended, ((0, 0), (0, 0), (1, 1), (1, 1)))


def exchange_body(volume, out_grad, weight_in, weight_out, filter_taps, filter_bias):
    slab_shape = volume.shape
    contract_first = (((0,), (0,)), ((), ()))

    def to_cells(field):
        return lax.all_to_all(
            field.reshape(field.shape[0], -1), "chan", split_axis=1, concat_axis=0, tiled=True
        )

    def to_channels(field):
        return lax.all_to_all(field, "chan", split_axis=0, concat_axis=1, tiled=True).reshape(
            slab_shape
        )

    full_in = lax.all_gather(weight_in, "chan", axis=0, tiled=True)
    full_out = lax.all_gather(weight_out, "chan", axis=0, tiled=True)
    vol_cells = to_cells(volume)
    hidden = to_channels(
        jnp.dot(full_in, vol_cells, preferred_element_type=jnp.float32).astype(jnp.bfloat16)
    )
    padded = lift(with_halo(hidden, "space", 1))
    mixed = core(padded, filter_taps, 1) + filter_bias[:, None, None, None]
    active = gelu_value(mixed).astype(jnp.bfloat16).reshape(slab_shape)
    out_cells = vol_cells.astype(jnp.float32) + jnp.dot(
        full_out, to_cells(active), preferred_element_type=jnp.float32
    )
    block_out = to_channels(out_cells.astype(jnp.bfloat16))
    grad_cells = to_cells(out_grad)
    act_part = lax.dot_general(
        full_out, grad_cells, contract_first, preferred_element_type=jnp.float32
    )
    act_grad = to_channels(act_part.astype(jnp.bfloat16))
    slope = gelu_slope(mixed)
    mix_grad = (
        (act_grad.astype(jnp.float32).reshape(slope.shape) * slope)
        .astype(jnp.bfloat16)
        .reshape(slab_shape)
    )
    padded_grad = lift(with_halo(mix_grad, "space", 1))
    hid_grad = core(padded_grad, filter_taps, -1).astype(jnp.bfloat16).reshape(slab_shape)
    back_part = lax.dot_general(
        full_in, to_cells(hid_grad), contract_first, preferred_element_type=jnp.float32
    )
    volume_grad = to_channels((grad_cells.astype(jnp.float32) + back_part).astype(jnp.bfloat16))
    return block_out, volume_grad


def body(volume, out_grad, weight_in, weight_out, filter_taps, filter_bias):
    own = volume.shape[0]
    parts = lax.axis_size("chan")
    groups, space = lax.axis_size("groups"), lax.axis_size("space")
    whole_rows = CY % parts == 0 and (CY // parts * CX) % LANES == 0 and parts & (parts - 1) == 0
    whole_shares = own % LANES == 0 and own % (16 * groups * space) == 0
    split = whole_rows and whole_shares and (groups, space) == (2, 4)
    chosen = split_cells_body if split else exchange_body
    return chosen(volume, out_grad, weight_in, weight_out, filter_taps, filter_bias)


def solution(mesh):
    field = P(("groups", "chan"), "space", None)
    placed = (field, field, P("chan", None), P("chan", None), P("chan", None), P("chan"))
    return jax.shard_map(
        body,
        mesh=mesh,
        in_specs=placed,
        out_specs=(field, field),
        check_vma=False,
    )
```

```python
import jax
import jax.numpy as jnp
from jax import lax
from jax.experimental import pallas as pl
from jax.experimental.pallas import tpu as pltpu
from jax.sharding import PartitionSpec as P

CX = 32
CY = 16
LANES = 128


root_half = 0.7071067811865476
inv_root_two_pi = 0.3989422804014327


def gelu_value(field):
    return 0.5 * field * (1.0 + lax.erf(field * root_half))


def gelu_slope(field):
    return (
        0.5 * (1.0 + lax.erf(field * root_half))
        + field * jnp.exp(-0.5 * field * field) * inv_root_two_pi
    )


def fill_padded(padded, own, row_low, row_high, plane_low, plane_high):
    planes, rows = own.shape[0], own.shape[1]
    for z in range(planes):
        padded[z + 1, 0] = row_low[z].astype(jnp.float32)
        padded[z + 1, rows + 1] = row_high[z].astype(jnp.float32)
        for y in range(rows):
            padded[z + 1, y + 1] = own[z, y].astype(jnp.float32)
    for y in range(rows + 2):
        padded[0, y] = plane_low[y].astype(jnp.float32)
        padded[planes + 1, y] = plane_high[y].astype(jnp.float32)


def stencil_row(padded, taps, z, y, flip):
    sums = [None, None, None]
    for a in range(3):
        for b in range(3):
            row = padded[z + a, y + b]
            for e in range(3):
                index = (a * 3 + b) * 3 + e
                tap = taps[0, 26 - index if flip else index]
                term = row * tap[None, :]
                sums[e] = term if sums[e] is None else sums[e] + term
    x = lax.broadcasted_iota(jnp.int32, sums[0].shape, 0)
    extent = sums[0].shape[0]
    before = jnp.where(x == 0, 0.0, pltpu.roll(sums[0], 1, 0))
    after = jnp.where(x == extent - 1, 0.0, pltpu.roll(sums[2], extent - 1, 0))
    return sums[1] + (before + after)


def piece_copies(here, mine, other, full, sems):
    chan, seat = here[0], here[1]
    copies = []
    for side, pieces in enumerate((mine, other)):
        for turn in range(pieces.shape[0]):
            for shift in range(pieces.shape[1]):
                copies.append(
                    pltpu.make_async_copy(
                        pieces.at[turn, shift],
                        full.at[chan ^ shift, seat ^ side ^ (2 * turn)],
                        sems.at[len(copies)],
                    )
                )
    return copies


def start_all(copies):
    for copy in copies:
        copy.start()


def wait_all(copies):
    for copy in copies:
        copy.wait()


def forward_kernel(
    here, own, row_low, row_high, plane_low, plane_high, taps, mine, other, *rest
):
    count = (len(rest) - 5) // 2
    inputs, outputs = rest[:count], rest[count : 2 * count]
    slope, padded, active, weight, sems = rest[2 * count :]
    step = pl.program_id(0)
    planes, rows, extent = own.shape[:3]
    copies = piece_copies(here, mine, other, weight, sems)

    @pl.when(step == 0)
    def _():
        start_all(copies)

    fill_padded(padded, own, row_low, row_high, plane_low, plane_high)
    lanes = pl.ds(pl.multiple_of(step * LANES, LANES), LANES)
    for z in range(planes):
        for y in range(rows):
            mixed = stencil_row(padded, taps, z, y, False) + taps[0, 27][None, :]
            half = 0.5 * (1.0 + lax.erf(mixed * root_half))
            at = (z * rows + y) * extent
            active[at : at + extent, lanes] = (mixed * half).astype(active.dtype)
            slope[z, y] = half + mixed * jnp.exp(-0.5 * mixed * mixed) * inv_root_two_pi

    @pl.when(step == pl.num_programs(0) - 1)
    def _():
        wait_all(copies)
        for shift in range(count):
            rows_of = weight[here[0] ^ shift]
            product = lax.dot_general(
                rows_of.reshape(-1, rows_of.shape[-1]),
                active[...],
                (((1,), (1,)), ((), ())),
                preferred_element_type=jnp.float32,
            )
            total = inputs[shift][...].astype(jnp.float32) + product
            outputs[shift][...] = total.astype(outputs[shift].dtype)


def backward_kernel(
    here, own, row_low, row_high, plane_low, plane_high, taps, mine, other, *rest
):
    count = (len(rest) - 4) // 2
    inputs, outputs = rest[:count], rest[count : 2 * count]
    padded, grads, weight, sems = rest[2 * count :]
    step = pl.program_id(0)
    planes, rows, extent = own.shape[:3]
    copies = piece_copies(here, mine, other, weight, sems)

    @pl.when(step == 0)
    def _():
        start_all(copies)

    fill_padded(padded, own, row_low, row_high, plane_low, plane_high)
    lanes = pl.ds(pl.multiple_of(step * LANES, LANES), LANES)
    for z in range(planes):
        for y in range(rows):
            at = (z * rows + y) * extent
            total = stencil_row(padded, taps, z, y, True)
            grads[at : at + extent, lanes] = total.astype(grads.dtype)

    @pl.when(step == pl.num_programs(0) - 1)
    def _():
        wait_all(copies)
        channels = grads.shape[1]
        width = inputs[0].shape[0]
        for shift in range(count):
            start = pl.multiple_of((here[0] ^ shift) * width, width)
            columns = weight[:, :, :, pl.ds(start, width)].reshape(channels, width)
            product = jnp.dot(grads[...], columns, preferred_element_type=jnp.float32)
            total = inputs[shift][...].astype(jnp.float32) + product.T
            outputs[shift][...] = total.astype(outputs[shift].dtype)


def weight_scratch(mine):
    turns, parts, share, channels = mine.shape
    return [
        pltpu.VMEM((parts, 2 * turns, share, channels), mine.dtype),
        pltpu.SemaphoreType.DMA((2 * turns * parts,)),
    ]


def stencil(here, own, halo, taps, weight, blocks, forward):
    planes, rows, extent, channels = own.shape
    cells = planes * rows * extent
    per_table = taps.shape[2] // LANES

    def block(*lead):
        zeros = (0,) * len(lead)
        return pl.BlockSpec(lead + (LANES,), lambda c, here: zeros + (c,))

    def resident(shape):
        return pl.BlockSpec(shape, lambda c, here: (0,) * len(shape), pipeline_mode=pl.Buffered(1))

    anywhere = pl.BlockSpec(memory_space=pl.ANY)
    in_specs = [
        block(planes, rows, extent),
        block(planes, extent),
        block(planes, extent),
        block(rows + 2, extent),
        block(rows + 2, extent),
        pl.BlockSpec(
            (1, 28, LANES), lambda c, here: ((c // per_table) ^ here[0], 0, c % per_table)
        ),
        anywhere,
        anywhere,
    ]
    in_specs += [resident(piece.shape) for piece in blocks]
    out_specs = [resident(piece.shape) for piece in blocks]
    out_shape = [jax.ShapeDtypeStruct(piece.shape, piece.dtype) for piece in blocks]
    if forward:
        out_specs.append(block(planes, rows, extent))
        out_shape.append(jax.ShapeDtypeStruct(own.shape, jnp.float32))
    return pl.pallas_call(
        forward_kernel if forward else backward_kernel,
        grid_spec=pltpu.PrefetchScalarGridSpec(
            num_scalar_prefetch=1,
            grid=(channels // LANES,),
            in_specs=in_specs,
            out_specs=out_specs,
            scratch_shapes=[
                pltpu.VMEM((planes + 2, rows + 2, extent, LANES), jnp.float32),
                pltpu.VMEM((cells, channels), own.dtype),
                *weight_scratch(weight[0]),
            ],
        ),
        out_shape=out_shape,
    )(here, own, *halo, taps, *weight, *blocks)


def turn_blocks(here, inputs, turned):
    own = inputs[0].shape[0]
    for shift, block in enumerate(inputs):
        start = pl.multiple_of((here[0] ^ shift) * own, own)
        turned[:, pl.ds(start, own)] = block[...].T


def put_with_rows(value, out, first, last):
    out[...] = value
    planes, extent = first.shape[:2]
    plane = value.shape[0] // planes
    for z in range(planes):
        first[z] = value[z * plane : z * plane + extent]
        last[z] = value[(z + 1) * plane - extent : (z + 1) * plane]


def hidden_kernel(here, mine, other, *rest, count):
    inputs, (out, first, last, turned, weight, sems) = rest[:count], rest[count:]

    @pl.when(pl.program_id(0) == 0)
    def _():
        copies = piece_copies(here, mine, other, weight, sems)
        start_all(copies)
        turn_blocks(here, inputs, turned)
        wait_all(copies)

    rows_of = weight[pl.program_id(0)]
    value = lax.dot_general(
        turned[...],
        rows_of.reshape(-1, rows_of.shape[-1]),
        (((1,), (1,)), ((), ())),
        preferred_element_type=jnp.float32,
    )
    put_with_rows(value.astype(out.dtype), out, first, last)


def mix_kernel(here, mine, other, *rest, count):
    inputs, (slope, out, first, last, turned, weight, sems) = rest[:count], rest[count:]

    @pl.when(pl.program_id(0) == 0)
    def _():
        copies = piece_copies(here, mine, other, weight, sems)
        start_all(copies)
        turn_blocks(here, inputs, turned)
        wait_all(copies)

    channels, width = turned.shape[1], out.shape[1]
    start = pl.multiple_of(pl.program_id(0) * width, width)
    columns = weight[:, :, :, pl.ds(start, width)].reshape(channels, width)
    grad = jnp.dot(turned[...], columns, preferred_element_type=jnp.float32)
    grad = grad.astype(out.dtype).astype(jnp.float32)
    put_with_rows((grad * slope[...]).astype(out.dtype), out, first, last)


def product_call(here, blocks, weight, planes, slope=None):
    own, cells = blocks[0].shape
    count = len(blocks)
    channels = own * count
    dtype = blocks[0].dtype
    columns = pl.BlockSpec((cells, own), lambda c, here: (0, c))
    edge = pl.BlockSpec((planes, CX, own), lambda c, here: (0, 0, c))
    whole = pl.BlockSpec((own, cells), lambda c, here: (0, 0), pipeline_mode=pl.Buffered(1))
    anywhere = pl.BlockSpec(memory_space=pl.ANY)
    kernel, extra = (hidden_kernel, []) if slope is None else (mix_kernel, [slope])
    edge_shape = jax.ShapeDtypeStruct((planes, CX, channels), dtype)
    return pl.pallas_call(
        lambda *refs: kernel(*refs, count=count),
        grid_spec=pltpu.PrefetchScalarGridSpec(
            num_scalar_prefetch=1,
            grid=(count,),
            in_specs=[anywhere] * 2 + [whole] * count + [columns] * len(extra),
            out_specs=[columns, edge, edge],
            scratch_shapes=[pltpu.VMEM((cells, channels), dtype), *weight_scratch(weight[0])],
        ),
        out_shape=[jax.ShapeDtypeStruct((cells, channels), dtype), edge_shape, edge_shape],
    )(here, *weight, *blocks, *extra)


def shift_pairs(axis):
    count = lax.axis_size(axis)
    forward = [(i, i + 1) for i in range(count - 1)]
    return forward, [(target, source) for source, target in forward]


def split_cells_body(volume, out_grad, weight_in, weight_out, filter_taps, filter_bias):
    own, planes, cells = volume.shape
    parts = lax.axis_size("chan")
    rows = CY // parts
    width = rows * CX
    channels = own * parts
    others = ("groups", "space")
    seat = lax.axis_index(others)
    chan = lax.axis_index("chan")
    share = own // lax.axis_size(others)
    here = jnp.stack([chan, seat]).astype(jnp.int32)
    shifts = sorted(range(1, parts), key=lambda shift: (shift & (parts // 2) == 0, shift))

    def swap(part, axes, partner):
        count = lax.axis_size(axes)
        return lax.ppermute(part, axes, [(i, partner(i)) for i in range(count)])

    def exchange(blocks):
        got = {0: blocks(0)}
        for shift in shifts:
            got[shift] = swap(blocks(shift), "chan", lambda i: i ^ shift)
        return [got[shift] for shift in range(parts)]

    def cut(field):
        def blocks(shift):
            start = (chan ^ shift) * width
            piece = lax.dynamic_slice_in_dim(field, start, width, axis=2)
            return piece.reshape(own, planes * width)

        return blocks

    def paste(pieces):
        field = jnp.zeros((own, planes, cells), pieces[0].dtype)
        for shift in [0] + shifts:
            piece = pieces[shift].reshape(own, planes, width)
            field = lax.dynamic_update_slice_in_dim(field, piece, (chan ^ shift) * width, axis=2)
        return field

    def gather_weight(weight):
        piece = lax.dynamic_slice_in_dim(weight, seat * share, share, axis=0)
        column = jnp.stack(exchange(lambda shift: piece))
        over_x = swap(column, others, lambda i: i ^ 2)
        over_y = swap(column, others, lambda i: i ^ 4)
        mixed = jnp.where(seat & 1 == 0, over_y, over_x)
        far = swap(mixed, others, lambda i: i ^ (4 if i & 1 else 2))
        mine = jnp.stack([column, over_x, over_y, far])
        return mine, swap(mine, others, lambda i: i ^ 1)

    def halo_of(field, first, last):
        forward, backward = shift_pairs("chan")
        row_low = lax.ppermute(last, "chan", forward)
        row_high = lax.ppermute(first, "chan", backward)
        forward, backward = shift_pairs("space")

        def plane(z):
            return jnp.concatenate([row_low[z][None], field[z], row_high[z][None]], axis=0)

        plane_low = lax.ppermute(plane(-1), "space", forward)
        plane_high = lax.ppermute(plane(0), "space", backward)
        return row_low, row_high, plane_low, plane_high

    grid = (planes, rows, CX, channels)
    full_in = gather_weight(weight_in)
    full_out = gather_weight(weight_out)
    table = jnp.concatenate([filter_taps, filter_bias[:, None]], axis=1).T
    taps = jnp.stack(exchange(lambda shift: table))
    vol_blocks = exchange(cut(volume))
    grad_blocks = exchange(cut(out_grad))
    hidden, first, last = product_call(here, vol_blocks, full_in, planes)
    hidden = hidden.reshape(grid)
    halo = halo_of(hidden, first, last)
    *out_blocks, slope = stencil(here, hidden, halo, taps, full_out, vol_blocks, True)
    block_out = paste(exchange(lambda shift: out_blocks[shift]))
    mix_grad, first, last = product_call(
        here, grad_blocks, full_out, planes, slope.reshape(planes * width, channels)
    )
    mix_grad = mix_grad.reshape(grid)
    halo = halo_of(mix_grad, first, last)
    back_blocks = stencil(here, mix_grad, halo, taps, full_in, grad_blocks, False)
    volume_grad = paste(exchange(lambda shift: back_blocks[shift]))
    return block_out, volume_grad


def with_halo(block, axis, dim):
    forward, backward = shift_pairs(axis)
    low = lax.ppermute(lax.slice_in_dim(block, block.shape[dim] - 1, None, axis=dim), axis, forward)
    high = lax.ppermute(lax.slice_in_dim(block, 0, 1, axis=dim), axis, backward)
    return jnp.concatenate([low, block, high], axis=dim)


def core(padded, filter_taps, direction):
    extent_z = padded.shape[1] - 2
    extent_y = padded.shape[2] - 2
    extent_x = padded.shape[3] - 2
    summed = jnp.zeros((padded.shape[0], extent_z, extent_y, extent_x), jnp.float32)
    for shift_z in range(3):
        for shift_y in range(3):
            for shift_x in range(3):
                tap_index = (shift_z * 3 + shift_y) * 3 + shift_x
                begin_z = 1 + direction * (shift_z - 1)
                begin_y = 1 + direction * (shift_y - 1)
                begin_x = 1 + direction * (shift_x - 1)
                window = padded[
                    :,
                    begin_z : begin_z + extent_z,
                    begin_y : begin_y + extent_y,
                    begin_x : begin_x + extent_x,
                ]
                summed = summed + filter_taps[:, tap_index][:, None, None, None] * window
    return summed


def lift(field_z):
    extended = field_z.astype(jnp.float32).reshape(field_z.shape[0], field_z.shape[1], CY, CX)
    return jnp.pad(extended, ((0, 0), (0, 0), (1, 1), (1, 1)))


def exchange_body(volume, out_grad, weight_in, weight_out, filter_taps, filter_bias):
    slab_shape = volume.shape
    contract_first = (((0,), (0,)), ((), ()))

    def to_cells(field):
        return lax.all_to_all(
            field.reshape(field.shape[0], -1), "chan", split_axis=1, concat_axis=0, tiled=True
        )

    def to_channels(field):
        return lax.all_to_all(field, "chan", split_axis=0, concat_axis=1, tiled=True).reshape(
            slab_shape
        )

    full_in = lax.all_gather(weight_in, "chan", axis=0, tiled=True)
    full_out = lax.all_gather(weight_out, "chan", axis=0, tiled=True)
    vol_cells = to_cells(volume)
    hidden = to_channels(
        jnp.dot(full_in, vol_cells, preferred_element_type=jnp.float32).astype(jnp.bfloat16)
    )
    padded = lift(with_halo(hidden, "space", 1))
    mixed = core(padded, filter_taps, 1) + filter_bias[:, None, None, None]
    active = gelu_value(mixed).astype(jnp.bfloat16).reshape(slab_shape)
    out_cells = vol_cells.astype(jnp.float32) + jnp.dot(
        full_out, to_cells(active), preferred_element_type=jnp.float32
    )
    block_out = to_channels(out_cells.astype(jnp.bfloat16))
    grad_cells = to_cells(out_grad)
    act_part = lax.dot_general(
        full_out, grad_cells, contract_first, preferred_element_type=jnp.float32
    )
    act_grad = to_channels(act_part.astype(jnp.bfloat16))
    slope = gelu_slope(mixed)
    mix_grad = (
        (act_grad.astype(jnp.float32).reshape(slope.shape) * slope)
        .astype(jnp.bfloat16)
        .reshape(slab_shape)
    )
    padded_grad = lift(with_halo(mix_grad, "space", 1))
    hid_grad = core(padded_grad, filter_taps, -1).astype(jnp.bfloat16).reshape(slab_shape)
    back_part = lax.dot_general(
        full_in, to_cells(hid_grad), contract_first, preferred_element_type=jnp.float32
    )
    volume_grad = to_channels((grad_cells.astype(jnp.float32) + back_part).astype(jnp.bfloat16))
    return block_out, volume_grad


def body(volume, out_grad, weight_in, weight_out, filter_taps, filter_bias):
    own = volume.shape[0]
    parts = lax.axis_size("chan")
    groups, space = lax.axis_size("groups"), lax.axis_size("space")
    whole_rows = CY % parts == 0 and (CY // parts * CX) % LANES == 0 and parts & (parts - 1) == 0
    whole_shares = own % LANES == 0 and own % (16 * groups * space) == 0
    split = whole_rows and whole_shares and (groups, space) == (2, 4)
    chosen = split_cells_body if split else exchange_body
    return chosen(volume, out_grad, weight_in, weight_out, filter_taps, filter_bias)


def solution(mesh):
    field = P(("groups", "chan"), "space", None)
    placed = (field, field, P("chan", None), P("chan", None), P("chan", None), P("chan"))
    return jax.shard_map(
        body,
        mesh=mesh,
        in_specs=placed,
        out_specs=(field, field),
        check_vma=False,
    )
```

```python
import jax
import jax.numpy as jnp
from jax import lax
from jax.experimental import pallas as pl
from jax.experimental.pallas import tpu as pltpu
from jax.sharding import PartitionSpec as P

CX = 32
CY = 16
LANES = 128


root_half = 0.7071067811865476
inv_root_two_pi = 0.3989422804014327


def gelu_value(field):
    return 0.5 * field * (1.0 + lax.erf(field * root_half))


def gelu_slope(field):
    return (
        0.5 * (1.0 + lax.erf(field * root_half))
        + field * jnp.exp(-0.5 * field * field) * inv_root_two_pi
    )


def fill_padded(padded, own, row_low, row_high, plane_low, plane_high):
    planes, rows = own.shape[0], own.shape[1]
    for z in range(planes):
        padded[z + 1, 0] = row_low[z].astype(jnp.float32)
        padded[z + 1, rows + 1] = row_high[z].astype(jnp.float32)
        for y in range(rows):
            padded[z + 1, y + 1] = own[z, y].astype(jnp.float32)
    for y in range(rows + 2):
        padded[0, y] = plane_low[y].astype(jnp.float32)
        padded[planes + 1, y] = plane_high[y].astype(jnp.float32)


def stencil_row(padded, taps, z, y, flip):
    sums = [None, None, None]
    for a in range(3):
        for b in range(3):
            row = padded[z + a, y + b]
            for e in range(3):
                index = (a * 3 + b) * 3 + e
                tap = taps[0, 26 - index if flip else index]
                term = row * tap[None, :]
                sums[e] = term if sums[e] is None else sums[e] + term
    x = lax.broadcasted_iota(jnp.int32, sums[0].shape, 0)
    extent = sums[0].shape[0]
    before = jnp.where(x == 0, 0.0, pltpu.roll(sums[0], 1, 0))
    after = jnp.where(x == extent - 1, 0.0, pltpu.roll(sums[2], extent - 1, 0))
    return sums[1] + (before + after)


def doubling(count):
    masks = []
    while count > 1:
        masks.append(count - 1)
        count //= 2
    return masks


def distances(count):
    found = [0]
    for mask in doubling(count):
        found += [mask ^ distance for distance in found]
    return found


def piece_copies(here, mine, other, full, sems):
    chan, seat = here[0], here[1]
    copies = []
    for slot, distance in enumerate(distances(mine.shape[1])):
        for side, pieces in enumerate((mine, other)):
            for turn in range(pieces.shape[0]):
                copies.append(
                    pltpu.make_async_copy(
                        pieces.at[turn, slot],
                        full.at[chan ^ distance, seat ^ side ^ (2 * turn)],
                        sems.at[chan ^ distance, 2 * turn + side],
                    )
                )
    return copies


def wait_block(block, mine, other, full, sems):
    for side, pieces in enumerate((mine, other)):
        for turn in range(pieces.shape[0]):
            pltpu.make_async_copy(
                pieces.at[turn, 0], full.at[block, 2 * turn + side], sems.at[block, 2 * turn + side]
            ).wait()


def start_all(copies):
    for copy in copies:
        copy.start()


def wait_all(copies):
    for copy in copies:
        copy.wait()


def add_planes(base, product, out):
    planes, _, width = base.shape
    for z in range(planes):
        total = base[z].astype(jnp.float32) + product[:, z * width : (z + 1) * width]
        out[z] = total.astype(out.dtype)


def forward_kernel(
    here, own, row_low, row_high, plane_low, plane_high, taps, mine, other, *rest
):
    count = (len(rest) - 5) // 2
    inputs, outputs = rest[:count], rest[count : 2 * count]
    slope, padded, active, weight, sems = rest[2 * count :]
    step = pl.program_id(0)
    planes, rows, extent = own.shape[:3]
    copies = piece_copies(here, mine, other, weight, sems)

    @pl.when(step == 0)
    def _():
        start_all(copies)

    fill_padded(padded, own, row_low, row_high, plane_low, plane_high)
    lanes = pl.ds(pl.multiple_of(step * LANES, LANES), LANES)
    for z in range(planes):
        for y in range(rows):
            mixed = stencil_row(padded, taps, z, y, False) + taps[0, 27][None, :]
            half = 0.5 * (1.0 + lax.erf(mixed * root_half))
            at = (z * rows + y) * extent
            active[at : at + extent, lanes] = (mixed * half).astype(active.dtype)
            slope[z, y] = half + mixed * jnp.exp(-0.5 * mixed * mixed) * inv_root_two_pi

    @pl.when(step == pl.num_programs(0) - 1)
    def _():
        wait_all(copies)
        for shift in range(count):
            rows_of = weight[here[0] ^ shift]
            product = lax.dot_general(
                rows_of.reshape(-1, rows_of.shape[-1]),
                active[...],
                (((1,), (1,)), ((), ())),
                preferred_element_type=jnp.float32,
            )
            add_planes(inputs[shift], product, outputs[shift])


def backward_kernel(
    here, own, row_low, row_high, plane_low, plane_high, taps, mine, other, *rest
):
    count = (len(rest) - 4) // 2
    inputs, outputs = rest[:count], rest[count : 2 * count]
    padded, grads, weight, sems = rest[2 * count :]
    step = pl.program_id(0)
    planes, rows, extent = own.shape[:3]
    copies = piece_copies(here, mine, other, weight, sems)

    @pl.when(step == 0)
    def _():
        start_all(copies)

    fill_padded(padded, own, row_low, row_high, plane_low, plane_high)
    lanes = pl.ds(pl.multiple_of(step * LANES, LANES), LANES)
    for z in range(planes):
        for y in range(rows):
            at = (z * rows + y) * extent
            total = stencil_row(padded, taps, z, y, True)
            grads[at : at + extent, lanes] = total.astype(grads.dtype)

    @pl.when(step == pl.num_programs(0) - 1)
    def _():
        wait_all(copies)
        channels = grads.shape[1]
        width = inputs[0].shape[1]
        for shift in range(count):
            start = pl.multiple_of((here[0] ^ shift) * width, width)
            columns = weight[:, :, :, pl.ds(start, width)].reshape(channels, width)
            product = jnp.dot(grads[...], columns, preferred_element_type=jnp.float32)
            add_planes(inputs[shift], product.T, outputs[shift])


def weight_scratch(mine):
    turns, parts, share, channels = mine.shape
    return [
        pltpu.VMEM((parts, 2 * turns, share, channels), mine.dtype),
        pltpu.SemaphoreType.DMA((parts, 2 * turns)),
    ]


def stencil(here, own, halo, taps, weight, blocks, forward):
    planes, rows, extent, channels = own.shape
    cells = planes * rows * extent
    per_table = taps.shape[2] // LANES

    def block(*lead):
        zeros = (0,) * len(lead)
        return pl.BlockSpec(lead + (LANES,), lambda c, here: zeros + (c,))

    def resident(shape):
        return pl.BlockSpec(shape, lambda c, here: (0,) * len(shape), pipeline_mode=pl.Buffered(1))

    def table_at(c, here):
        away = (c // per_table) ^ here[0]
        slot = 0
        for place, distance in enumerate(distances(taps.shape[0])):
            slot = jnp.where(away == distance, place, slot)
        return slot, 0, c % per_table

    anywhere = pl.BlockSpec(memory_space=pl.ANY)
    in_specs = [
        block(planes, rows, extent),
        block(planes, extent),
        block(planes, extent),
        block(rows + 2, extent),
        block(rows + 2, extent),
        pl.BlockSpec((1, 28, LANES), table_at),
        anywhere,
        anywhere,
    ]
    in_specs += [resident(piece.shape) for piece in blocks]
    out_specs = [resident(piece.shape) for piece in blocks]
    out_shape = [jax.ShapeDtypeStruct(piece.shape, piece.dtype) for piece in blocks]
    if forward:
        out_specs.append(block(planes, rows, extent))
        out_shape.append(jax.ShapeDtypeStruct(own.shape, jnp.float32))
    return pl.pallas_call(
        forward_kernel if forward else backward_kernel,
        grid_spec=pltpu.PrefetchScalarGridSpec(
            num_scalar_prefetch=1,
            grid=(channels // LANES,),
            in_specs=in_specs,
            out_specs=out_specs,
            scratch_shapes=[
                pltpu.VMEM((planes + 2, rows + 2, extent, LANES), jnp.float32),
                pltpu.VMEM((cells, channels), own.dtype),
                *weight_scratch(weight[0]),
            ],
        ),
        out_shape=out_shape,
    )(here, own, *halo, taps, *weight, *blocks)


def turn_blocks(here, inputs, turned):
    planes, own, width = inputs[0].shape
    for shift, block in enumerate(inputs):
        start = pl.multiple_of((here[0] ^ shift) * own, own)
        for z in range(planes):
            turned[z * width : (z + 1) * width, pl.ds(start, own)] = block[z].T


def put_with_rows(value, out, first, last):
    out[...] = value
    planes, extent = first.shape[:2]
    plane = value.shape[0] // planes
    for z in range(planes):
        first[z] = value[z * plane : z * plane + extent]
        last[z] = value[(z + 1) * plane - extent : (z + 1) * plane]


def hidden_kernel(here, mine, other, *rest, count):
    inputs, (out, first, last, turned, weight, sems) = rest[:count], rest[count:]

    @pl.when(pl.program_id(0) == 0)
    def _():
        start_all(piece_copies(here, mine, other, weight, sems))
        turn_blocks(here, inputs, turned)

    wait_block(pl.program_id(0), mine, other, weight, sems)
    rows_of = weight[pl.program_id(0)]
    value = lax.dot_general(
        turned[...],
        rows_of.reshape(-1, rows_of.shape[-1]),
        (((1,), (1,)), ((), ())),
        preferred_element_type=jnp.float32,
    )
    put_with_rows(value.astype(out.dtype), out, first, last)


def mix_kernel(here, mine, other, *rest, count):
    inputs, (slope, out, first, last, turned, weight, sems) = rest[:count], rest[count:]

    @pl.when(pl.program_id(0) == 0)
    def _():
        copies = piece_copies(here, mine, other, weight, sems)
        start_all(copies)
        turn_blocks(here, inputs, turned)
        wait_all(copies)

    channels, width = turned.shape[1], out.shape[1]
    start = pl.multiple_of(pl.program_id(0) * width, width)
    columns = weight[:, :, :, pl.ds(start, width)].reshape(channels, width)
    grad = jnp.dot(turned[...], columns, preferred_element_type=jnp.float32)
    grad = grad.astype(out.dtype).astype(jnp.float32)
    put_with_rows((grad * slope[...]).astype(out.dtype), out, first, last)


def product_call(here, blocks, weight, slope=None):
    planes, own, width = blocks[0].shape
    cells = planes * width
    count = len(blocks)
    channels = own * count
    dtype = blocks[0].dtype
    columns = pl.BlockSpec((cells, own), lambda c, here: (0, c))
    edge = pl.BlockSpec((planes, CX, own), lambda c, here: (0, 0, c))
    whole = pl.BlockSpec(
        blocks[0].shape, lambda c, here: (0, 0, 0), pipeline_mode=pl.Buffered(1)
    )
    anywhere = pl.BlockSpec(memory_space=pl.ANY)
    kernel, extra = (hidden_kernel, []) if slope is None else (mix_kernel, [slope])
    edge_shape = jax.ShapeDtypeStruct((planes, CX, channels), dtype)
    return pl.pallas_call(
        lambda *refs: kernel(*refs, count=count),
        grid_spec=pltpu.PrefetchScalarGridSpec(
            num_scalar_prefetch=1,
            grid=(count,),
            in_specs=[anywhere] * 2 + [whole] * count + [columns] * len(extra),
            out_specs=[columns, edge, edge],
            scratch_shapes=[pltpu.VMEM((cells, channels), dtype), *weight_scratch(weight[0])],
        ),
        out_shape=[jax.ShapeDtypeStruct((cells, channels), dtype), edge_shape, edge_shape],
    )(here, *weight, *blocks, *extra)


def shift_pairs(axis):
    count = lax.axis_size(axis)
    forward = [(i, i + 1) for i in range(count - 1)]
    return forward, [(target, source) for source, target in forward]


def split_cells_body(volume, out_grad, weight_in, weight_out, filter_taps, filter_bias):
    own, planes, cells = volume.shape
    parts = lax.axis_size("chan")
    rows = CY // parts
    width = rows * CX
    channels = own * parts
    others = ("groups", "space")
    seat = lax.axis_index(others)
    chan = lax.axis_index("chan")
    share = own // lax.axis_size(others)
    here = jnp.stack([chan, seat]).astype(jnp.int32)
    shifts = sorted(range(1, parts), key=lambda shift: (shift & (parts // 2) == 0, shift))

    def swap(part, axes, partner):
        count = lax.axis_size(axes)
        return lax.ppermute(part, axes, [(i, partner(i)) for i in range(count)])

    def exchange(blocks):
        got = {0: blocks(0)}
        for shift in shifts:
            got[shift] = swap(blocks(shift), "chan", lambda i: i ^ shift)
        return [got[shift] for shift in range(parts)]

    def cut(field):
        def blocks(shift):
            start = (chan ^ shift) * width
            piece = lax.dynamic_slice_in_dim(field, start, width, axis=2)
            return lax.optimization_barrier(piece.transpose(1, 0, 2))

        return blocks

    def paste(pieces):
        field = jnp.zeros((own, planes, cells), pieces[0].dtype)
        for shift in [0] + shifts:
            piece = pieces[shift].transpose(1, 0, 2)
            field = lax.dynamic_update_slice_in_dim(field, piece, (chan ^ shift) * width, axis=2)
        return field

    def gather_column(piece):
        column = piece[None]
        for mask in doubling(parts):
            got = swap(column, "chan", lambda i: i ^ mask)
            column = jnp.concatenate([column, got])
        return column

    def gather_weight(weight):
        piece = lax.dynamic_slice_in_dim(weight, seat * share, share, axis=0)
        column = gather_column(piece)
        over_x = swap(column, others, lambda i: i ^ 2)
        over_y = swap(column, others, lambda i: i ^ 4)
        mixed = jnp.where(seat & 1 == 0, over_y, over_x)
        far = swap(mixed, others, lambda i: i ^ (4 if i & 1 else 2))
        mine = jnp.stack([column, over_x, over_y, far])
        return mine, swap(mine, others, lambda i: i ^ 1)

    def halo_of(field, first, last):
        forward, backward = shift_pairs("chan")
        row_low = lax.ppermute(last, "chan", forward)
        row_high = lax.ppermute(first, "chan", backward)
        forward, backward = shift_pairs("space")

        def plane(z):
            return jnp.concatenate([row_low[z][None], field[z], row_high[z][None]], axis=0)

        plane_low = lax.ppermute(plane(-1), "space", forward)
        plane_high = lax.ppermute(plane(0), "space", backward)
        return row_low, row_high, plane_low, plane_high

    grid = (planes, rows, CX, channels)
    full_in = gather_weight(weight_in)
    full_out = gather_weight(weight_out)
    table = jnp.concatenate([filter_taps, filter_bias[:, None]], axis=1).T
    taps = gather_column(table)
    vol_blocks = exchange(cut(volume))
    grad_blocks = exchange(cut(out_grad))
    hidden, first, last = product_call(here, vol_blocks, full_in)
    hidden = hidden.reshape(grid)
    halo = halo_of(hidden, first, last)
    *out_blocks, slope = stencil(here, hidden, halo, taps, full_out, vol_blocks, True)
    block_out = paste(exchange(lambda shift: out_blocks[shift]))
    mix_grad, first, last = product_call(
        here, grad_blocks, full_out, slope.reshape(planes * width, channels)
    )
    mix_grad = mix_grad.reshape(grid)
    halo = halo_of(mix_grad, first, last)
    back_blocks = stencil(here, mix_grad, halo, taps, full_in, grad_blocks, False)
    volume_grad = paste(exchange(lambda shift: back_blocks[shift]))
    return block_out, volume_grad


def with_halo(block, axis, dim):
    forward, backward = shift_pairs(axis)
    low = lax.ppermute(lax.slice_in_dim(block, block.shape[dim] - 1, None, axis=dim), axis, forward)
    high = lax.ppermute(lax.slice_in_dim(block, 0, 1, axis=dim), axis, backward)
    return jnp.concatenate([low, block, high], axis=dim)


def core(padded, filter_taps, direction):
    extent_z = padded.shape[1] - 2
    extent_y = padded.shape[2] - 2
    extent_x = padded.shape[3] - 2
    summed = jnp.zeros((padded.shape[0], extent_z, extent_y, extent_x), jnp.float32)
    for shift_z in range(3):
        for shift_y in range(3):
            for shift_x in range(3):
                tap_index = (shift_z * 3 + shift_y) * 3 + shift_x
                begin_z = 1 + direction * (shift_z - 1)
                begin_y = 1 + direction * (shift_y - 1)
                begin_x = 1 + direction * (shift_x - 1)
                window = padded[
                    :,
                    begin_z : begin_z + extent_z,
                    begin_y : begin_y + extent_y,
                    begin_x : begin_x + extent_x,
                ]
                summed = summed + filter_taps[:, tap_index][:, None, None, None] * window
    return summed


def lift(field_z):
    extended = field_z.astype(jnp.float32).reshape(field_z.shape[0], field_z.shape[1], CY, CX)
    return jnp.pad(extended, ((0, 0), (0, 0), (1, 1), (1, 1)))


def exchange_body(volume, out_grad, weight_in, weight_out, filter_taps, filter_bias):
    slab_shape = volume.shape
    contract_first = (((0,), (0,)), ((), ()))

    def to_cells(field):
        return lax.all_to_all(
            field.reshape(field.shape[0], -1), "chan", split_axis=1, concat_axis=0, tiled=True
        )

    def to_channels(field):
        return lax.all_to_all(field, "chan", split_axis=0, concat_axis=1, tiled=True).reshape(
            slab_shape
        )

    full_in = lax.all_gather(weight_in, "chan", axis=0, tiled=True)
    full_out = lax.all_gather(weight_out, "chan", axis=0, tiled=True)
    vol_cells = to_cells(volume)
    hidden = to_channels(
        jnp.dot(full_in, vol_cells, preferred_element_type=jnp.float32).astype(jnp.bfloat16)
    )
    padded = lift(with_halo(hidden, "space", 1))
    mixed = core(padded, filter_taps, 1) + filter_bias[:, None, None, None]
    active = gelu_value(mixed).astype(jnp.bfloat16).reshape(slab_shape)
    out_cells = vol_cells.astype(jnp.float32) + jnp.dot(
        full_out, to_cells(active), preferred_element_type=jnp.float32
    )
    block_out = to_channels(out_cells.astype(jnp.bfloat16))
    grad_cells = to_cells(out_grad)
    act_part = lax.dot_general(
        full_out, grad_cells, contract_first, preferred_element_type=jnp.float32
    )
    act_grad = to_channels(act_part.astype(jnp.bfloat16))
    slope = gelu_slope(mixed)
    mix_grad = (
        (act_grad.astype(jnp.float32).reshape(slope.shape) * slope)
        .astype(jnp.bfloat16)
        .reshape(slab_shape)
    )
    padded_grad = lift(with_halo(mix_grad, "space", 1))
    hid_grad = core(padded_grad, filter_taps, -1).astype(jnp.bfloat16).reshape(slab_shape)
    back_part = lax.dot_general(
        full_in, to_cells(hid_grad), contract_first, preferred_element_type=jnp.float32
    )
    volume_grad = to_channels((grad_cells.astype(jnp.float32) + back_part).astype(jnp.bfloat16))
    return block_out, volume_grad


def body(volume, out_grad, weight_in, weight_out, filter_taps, filter_bias):
    own = volume.shape[0]
    parts = lax.axis_size("chan")
    groups, space = lax.axis_size("groups"), lax.axis_size("space")
    whole_rows = CY % parts == 0 and (CY // parts * CX) % LANES == 0 and parts & (parts - 1) == 0
    whole_shares = own % LANES == 0 and own % (16 * groups * space) == 0
    split = whole_rows and whole_shares and (groups, space) == (2, 4)
    chosen = split_cells_body if split else exchange_body
    return chosen(volume, out_grad, weight_in, weight_out, filter_taps, filter_bias)


def solution(mesh):
    field = P(("groups", "chan"), "space", None)
    placed = (field, field, P("chan", None), P("chan", None), P("chan", None), P("chan"))
    return jax.shard_map(
        body,
        mesh=mesh,
        in_specs=placed,
        out_specs=(field, field),
        check_vma=False,
    )
```

```python
import jax
import jax.numpy as jnp
from jax import lax
from jax.experimental import pallas as pl
from jax.experimental.pallas import tpu as pltpu
from jax.sharding import PartitionSpec as P

CX = 32
CY = 16
LANES = 128


root_half = 0.7071067811865476
inv_root_two_pi = 0.3989422804014327


def gelu_value(field):
    return 0.5 * field * (1.0 + lax.erf(field * root_half))


def gelu_slope(field):
    return (
        0.5 * (1.0 + lax.erf(field * root_half))
        + field * jnp.exp(-0.5 * field * field) * inv_root_two_pi
    )


def fill_padded(padded, own, row_low, row_high, plane_low, plane_high):
    planes, rows = own.shape[0], own.shape[1]
    for z in range(planes):
        padded[z + 1, 0] = row_low[z].astype(jnp.float32)
        padded[z + 1, rows + 1] = row_high[z].astype(jnp.float32)
        for y in range(rows):
            padded[z + 1, y + 1] = own[z, y].astype(jnp.float32)
    for y in range(rows + 2):
        padded[0, y] = plane_low[y].astype(jnp.float32)
        padded[planes + 1, y] = plane_high[y].astype(jnp.float32)


def stencil_row(padded, taps, z, y, flip):
    sums = [None, None, None]
    for a in range(3):
        for b in range(3):
            row = padded[z + a, y + b]
            for e in range(3):
                index = (a * 3 + b) * 3 + e
                tap = taps[0, 26 - index if flip else index]
                term = row * tap[None, :]
                sums[e] = term if sums[e] is None else sums[e] + term
    x = lax.broadcasted_iota(jnp.int32, sums[0].shape, 0)
    extent = sums[0].shape[0]
    before = jnp.where(x == 0, 0.0, pltpu.roll(sums[0], 1, 0))
    after = jnp.where(x == extent - 1, 0.0, pltpu.roll(sums[2], extent - 1, 0))
    return sums[1] + (before + after)


def doubling(count):
    masks = []
    while count > 1:
        masks.append(count - 1)
        count //= 2
    return masks


def distances(count):
    found = [0]
    for mask in doubling(count):
        found += [mask ^ distance for distance in found]
    return found


def piece_copies(here, mine, other, full, sems):
    chan, seat = here[0], here[1]
    copies = []
    for slot, distance in enumerate(distances(mine.shape[1])):
        for side, pieces in enumerate((mine, other)):
            for turn in range(pieces.shape[0]):
                copies.append(
                    pltpu.make_async_copy(
                        pieces.at[turn, slot],
                        full.at[chan ^ distance, seat ^ side ^ (2 * turn)],
                        sems.at[chan ^ distance, 2 * turn + side],
                    )
                )
    return copies


def wait_block(block, mine, other, full, sems):
    for side, pieces in enumerate((mine, other)):
        for turn in range(pieces.shape[0]):
            pltpu.make_async_copy(
                pieces.at[turn, 0], full.at[block, 2 * turn + side], sems.at[block, 2 * turn + side]
            ).wait()


def start_all(copies):
    for copy in copies:
        copy.start()


def wait_all(copies):
    for copy in copies:
        copy.wait()


def add_planes(base, product, out):
    planes, _, width = base.shape
    for z in range(planes):
        total = base[z].astype(jnp.float32) + product[:, z * width : (z + 1) * width]
        out[z] = total.astype(out.dtype)


def forward_kernel(
    here, own, row_low, row_high, plane_low, plane_high, taps, mine, other, *rest
):
    count = (len(rest) - 5) // 2
    inputs, outputs = rest[:count], rest[count : 2 * count]
    slope, padded, active, weight, sems = rest[2 * count :]
    step = pl.program_id(0)
    planes, rows, extent = own.shape[:3]
    copies = piece_copies(here, mine, other, weight, sems)

    @pl.when(step == 0)
    def _():
        start_all(copies)

    fill_padded(padded, own, row_low, row_high, plane_low, plane_high)
    lanes = pl.ds(pl.multiple_of(step * LANES, LANES), LANES)
    for z in range(planes):
        for y in range(rows):
            mixed = stencil_row(padded, taps, z, y, False) + taps[0, 27][None, :]
            half = 0.5 * (1.0 + lax.erf(mixed * root_half))
            at = (z * rows + y) * extent
            active[at : at + extent, lanes] = (mixed * half).astype(active.dtype)
            slope[z, y] = half + mixed * jnp.exp(-0.5 * mixed * mixed) * inv_root_two_pi

    @pl.when(step == pl.num_programs(0) - 1)
    def _():
        wait_all(copies)
        for shift in range(count):
            rows_of = weight[here[0] ^ shift]
            product = lax.dot_general(
                rows_of.reshape(-1, rows_of.shape[-1]),
                active[...],
                (((1,), (1,)), ((), ())),
                preferred_element_type=jnp.float32,
            )
            add_planes(inputs[shift], product, outputs[shift])


def backward_kernel(
    here, own, row_low, row_high, plane_low, plane_high, taps, mine, other, *rest
):
    count = (len(rest) - 4) // 2
    inputs, outputs = rest[:count], rest[count : 2 * count]
    padded, grads, weight, sems = rest[2 * count :]
    step = pl.program_id(0)
    planes, rows, extent = own.shape[:3]
    copies = piece_copies(here, mine, other, weight, sems)

    @pl.when(step == 0)
    def _():
        start_all(copies)

    fill_padded(padded, own, row_low, row_high, plane_low, plane_high)
    lanes = pl.ds(pl.multiple_of(step * LANES, LANES), LANES)
    for z in range(planes):
        for y in range(rows):
            at = (z * rows + y) * extent
            total = stencil_row(padded, taps, z, y, True)
            grads[at : at + extent, lanes] = total.astype(grads.dtype)

    @pl.when(step == pl.num_programs(0) - 1)
    def _():
        wait_all(copies)
        channels = grads.shape[1]
        width = inputs[0].shape[1]
        for shift in range(count):
            start = pl.multiple_of((here[0] ^ shift) * width, width)
            columns = weight[:, :, :, pl.ds(start, width)].reshape(channels, width)
            product = jnp.dot(grads[...], columns, preferred_element_type=jnp.float32)
            add_planes(inputs[shift], product.T, outputs[shift])


def weight_scratch(mine):
    turns, parts, share, channels = mine.shape
    return [
        pltpu.VMEM((parts, 2 * turns, share, channels), mine.dtype),
        pltpu.SemaphoreType.DMA((parts, 2 * turns)),
    ]


def stencil(here, own, halo, taps, weight, blocks, forward):
    planes, rows, extent, channels = own.shape
    cells = planes * rows * extent
    per_table = taps.shape[2] // LANES

    def block(*lead):
        zeros = (0,) * len(lead)
        return pl.BlockSpec(lead + (LANES,), lambda c, here: zeros + (c,))

    def resident(shape):
        return pl.BlockSpec(shape, lambda c, here: (0,) * len(shape), pipeline_mode=pl.Buffered(1))

    def table_at(c, here):
        away = (c // per_table) ^ here[0]
        slot = 0
        for place, distance in enumerate(distances(taps.shape[0])):
            slot = jnp.where(away == distance, place, slot)
        return slot, 0, c % per_table

    anywhere = pl.BlockSpec(memory_space=pltpu.HBM)
    in_specs = [
        block(planes, rows, extent),
        block(planes, extent),
        block(planes, extent),
        block(rows + 2, extent),
        block(rows + 2, extent),
        pl.BlockSpec((1, 28, LANES), table_at),
        anywhere,
        anywhere,
    ]
    in_specs += [resident(piece.shape) for piece in blocks]
    out_specs = [resident(piece.shape) for piece in blocks]
    out_shape = [jax.ShapeDtypeStruct(piece.shape, piece.dtype) for piece in blocks]
    if forward:
        out_specs.append(block(planes, rows, extent))
        out_shape.append(jax.ShapeDtypeStruct(own.shape, jnp.float32))
    return pl.pallas_call(
        forward_kernel if forward else backward_kernel,
        grid_spec=pltpu.PrefetchScalarGridSpec(
            num_scalar_prefetch=1,
            grid=(channels // LANES,),
            in_specs=in_specs,
            out_specs=out_specs,
            scratch_shapes=[
                pltpu.VMEM((planes + 2, rows + 2, extent, LANES), jnp.float32),
                pltpu.VMEM((cells, channels), own.dtype),
                *weight_scratch(weight[0]),
            ],
        ),
        out_shape=out_shape,
    )(here, own, *halo, taps, *weight, *blocks)


def turn_blocks(here, inputs, turned):
    planes, own, width = inputs[0].shape
    for shift, block in enumerate(inputs):
        start = pl.multiple_of((here[0] ^ shift) * own, own)
        for z in range(planes):
            turned[z * width : (z + 1) * width, pl.ds(start, own)] = block[z].T


def put_with_rows(value, out, first, last):
    out[...] = value
    planes, extent = first.shape[:2]
    plane = value.shape[0] // planes
    for z in range(planes):
        first[z] = value[z * plane : z * plane + extent]
        last[z] = value[(z + 1) * plane - extent : (z + 1) * plane]


def hidden_kernel(here, mine, other, *rest, count):
    inputs, (out, first, last, turned, weight, sems) = rest[:count], rest[count:]

    @pl.when(pl.program_id(0) == 0)
    def _():
        start_all(piece_copies(here, mine, other, weight, sems))
        turn_blocks(here, inputs, turned)

    wait_block(pl.program_id(0), mine, other, weight, sems)
    rows_of = weight[pl.program_id(0)]
    value = lax.dot_general(
        turned[...],
        rows_of.reshape(-1, rows_of.shape[-1]),
        (((1,), (1,)), ((), ())),
        preferred_element_type=jnp.float32,
    )
    put_with_rows(value.astype(out.dtype), out, first, last)


def mix_kernel(here, mine, other, *rest, count):
    inputs, (slope, out, first, last, turned, weight, sems) = rest[:count], rest[count:]

    @pl.when(pl.program_id(0) == 0)
    def _():
        copies = piece_copies(here, mine, other, weight, sems)
        start_all(copies)
        turn_blocks(here, inputs, turned)
        wait_all(copies)

    channels, width = turned.shape[1], out.shape[1]
    start = pl.multiple_of(pl.program_id(0) * width, width)
    columns = weight[:, :, :, pl.ds(start, width)].reshape(channels, width)
    grad = jnp.dot(turned[...], columns, preferred_element_type=jnp.float32)
    grad = grad.astype(out.dtype).astype(jnp.float32)
    put_with_rows((grad * slope[...]).astype(out.dtype), out, first, last)


def product_call(here, blocks, weight, slope=None):
    planes, own, width = blocks[0].shape
    cells = planes * width
    count = len(blocks)
    channels = own * count
    dtype = blocks[0].dtype
    columns = pl.BlockSpec((cells, own), lambda c, here: (0, c))
    edge = pl.BlockSpec((planes, CX, own), lambda c, here: (0, 0, c))
    whole = pl.BlockSpec(
        blocks[0].shape, lambda c, here: (0, 0, 0), pipeline_mode=pl.Buffered(1)
    )
    anywhere = pl.BlockSpec(memory_space=pltpu.HBM)
    kernel, extra = (hidden_kernel, []) if slope is None else (mix_kernel, [slope])
    edge_shape = jax.ShapeDtypeStruct((planes, CX, channels), dtype)
    return pl.pallas_call(
        lambda *refs: kernel(*refs, count=count),
        grid_spec=pltpu.PrefetchScalarGridSpec(
            num_scalar_prefetch=1,
            grid=(count,),
            in_specs=[anywhere] * 2 + [whole] * count + [columns] * len(extra),
            out_specs=[columns, edge, edge],
            scratch_shapes=[pltpu.VMEM((cells, channels), dtype), *weight_scratch(weight[0])],
        ),
        out_shape=[jax.ShapeDtypeStruct((cells, channels), dtype), edge_shape, edge_shape],
    )(here, *weight, *blocks, *extra)


def shift_pairs(axis):
    count = lax.axis_size(axis)
    forward = [(i, i + 1) for i in range(count - 1)]
    return forward, [(target, source) for source, target in forward]


def split_cells_body(volume, out_grad, weight_in, weight_out, filter_taps, filter_bias):
    own, planes, cells = volume.shape
    parts = lax.axis_size("chan")
    rows = CY // parts
    width = rows * CX
    channels = own * parts
    others = ("groups", "space")
    seat = lax.axis_index(others)
    chan = lax.axis_index("chan")
    share = own // lax.axis_size(others)
    here = jnp.stack([chan, seat]).astype(jnp.int32)
    shifts = sorted(range(1, parts), key=lambda shift: (shift & (parts // 2) == 0, shift))

    def swap(part, axes, partner):
        count = lax.axis_size(axes)
        return lax.ppermute(part, axes, [(i, partner(i)) for i in range(count)])

    def exchange(blocks):
        got = {0: blocks(0)}
        for shift in shifts:
            got[shift] = swap(blocks(shift), "chan", lambda i: i ^ shift)
        return [got[shift] for shift in range(parts)]

    def cut(field):
        pieces, place = {}, chan
        for shift in shifts + [0]:
            start = (place ^ shift) * width
            piece = lax.dynamic_slice_in_dim(field, start, width, axis=2).transpose(1, 0, 2)
            pieces[shift], place = lax.optimization_barrier((piece, place))
        return lambda shift: pieces[shift]

    def paste(pieces):
        field = jnp.zeros((own, planes, cells), pieces[0].dtype)
        for shift in [0] + shifts:
            piece = pieces[shift].transpose(1, 0, 2)
            field = lax.dynamic_update_slice_in_dim(field, piece, (chan ^ shift) * width, axis=2)
        return field

    def gather_column(piece):
        column = piece[None]
        for mask in doubling(parts):
            got = swap(column, "chan", lambda i: i ^ mask)
            column = jnp.concatenate([column, got])
        return column

    def gather_weight(column):
        over_x = swap(column, others, lambda i: i ^ 2)
        over_y = swap(column, others, lambda i: i ^ 4)
        mixed = jnp.where(seat & 1 == 0, over_y, over_x)
        far = swap(mixed, others, lambda i: i ^ (4 if i & 1 else 2))
        mine = jnp.stack([column, over_x, over_y, far])
        return mine, swap(mine, others, lambda i: i ^ 1)

    def halo_of(field, first, last):
        forward, backward = shift_pairs("chan")
        row_low = lax.ppermute(last, "chan", forward)
        row_high = lax.ppermute(first, "chan", backward)
        forward, backward = shift_pairs("space")

        def plane(z):
            return jnp.concatenate([row_low[z][None], field[z], row_high[z][None]], axis=0)

        plane_low = lax.ppermute(plane(-1), "space", forward)
        plane_high = lax.ppermute(plane(0), "space", backward)
        return row_low, row_high, plane_low, plane_high

    grid = (planes, rows, CX, channels)
    pieces = [
        lax.dynamic_slice_in_dim(weight, seat * share, share, axis=0)
        for weight in (weight_in, weight_out)
    ]
    column = gather_column(jnp.concatenate(pieces))
    full_in = gather_weight(column[:, :share])
    full_out = gather_weight(column[:, share:])
    table = jnp.concatenate([filter_taps, filter_bias[:, None]], axis=1).T
    taps = gather_column(table)
    vol_blocks = exchange(cut(volume))
    grad_blocks = exchange(cut(out_grad))
    hidden, first, last = product_call(here, vol_blocks, full_in)
    hidden = hidden.reshape(grid)
    halo = halo_of(hidden, first, last)
    *out_blocks, slope = stencil(here, hidden, halo, taps, full_out, vol_blocks, True)
    block_out = paste(exchange(lambda shift: out_blocks[shift]))
    mix_grad, first, last = product_call(
        here, grad_blocks, full_out, slope.reshape(planes * width, channels)
    )
    mix_grad = mix_grad.reshape(grid)
    halo = halo_of(mix_grad, first, last)
    back_blocks = stencil(here, mix_grad, halo, taps, full_in, grad_blocks, False)
    volume_grad = paste(exchange(lambda shift: back_blocks[shift]))
    return block_out, volume_grad


def with_halo(block, axis, dim):
    forward, backward = shift_pairs(axis)
    low = lax.ppermute(lax.slice_in_dim(block, block.shape[dim] - 1, None, axis=dim), axis, forward)
    high = lax.ppermute(lax.slice_in_dim(block, 0, 1, axis=dim), axis, backward)
    return jnp.concatenate([low, block, high], axis=dim)


def core(padded, filter_taps, direction):
    extent_z = padded.shape[1] - 2
    extent_y = padded.shape[2] - 2
    extent_x = padded.shape[3] - 2
    summed = jnp.zeros((padded.shape[0], extent_z, extent_y, extent_x), jnp.float32)
    for shift_z in range(3):
        for shift_y in range(3):
            for shift_x in range(3):
                tap_index = (shift_z * 3 + shift_y) * 3 + shift_x
                begin_z = 1 + direction * (shift_z - 1)
                begin_y = 1 + direction * (shift_y - 1)
                begin_x = 1 + direction * (shift_x - 1)
                window = padded[
                    :,
                    begin_z : begin_z + extent_z,
                    begin_y : begin_y + extent_y,
                    begin_x : begin_x + extent_x,
                ]
                summed = summed + filter_taps[:, tap_index][:, None, None, None] * window
    return summed


def lift(field_z):
    extended = field_z.astype(jnp.float32).reshape(field_z.shape[0], field_z.shape[1], CY, CX)
    return jnp.pad(extended, ((0, 0), (0, 0), (1, 1), (1, 1)))


def exchange_body(volume, out_grad, weight_in, weight_out, filter_taps, filter_bias):
    slab_shape = volume.shape
    contract_first = (((0,), (0,)), ((), ()))

    def to_cells(field):
        return lax.all_to_all(
            field.reshape(field.shape[0], -1), "chan", split_axis=1, concat_axis=0, tiled=True
        )

    def to_channels(field):
        return lax.all_to_all(field, "chan", split_axis=0, concat_axis=1, tiled=True).reshape(
            slab_shape
        )

    full_in = lax.all_gather(weight_in, "chan", axis=0, tiled=True)
    full_out = lax.all_gather(weight_out, "chan", axis=0, tiled=True)
    vol_cells = to_cells(volume)
    hidden = to_channels(
        jnp.dot(full_in, vol_cells, preferred_element_type=jnp.float32).astype(jnp.bfloat16)
    )
    padded = lift(with_halo(hidden, "space", 1))
    mixed = core(padded, filter_taps, 1) + filter_bias[:, None, None, None]
    active = gelu_value(mixed).astype(jnp.bfloat16).reshape(slab_shape)
    out_cells = vol_cells.astype(jnp.float32) + jnp.dot(
        full_out, to_cells(active), preferred_element_type=jnp.float32
    )
    block_out = to_channels(out_cells.astype(jnp.bfloat16))
    grad_cells = to_cells(out_grad)
    act_part = lax.dot_general(
        full_out, grad_cells, contract_first, preferred_element_type=jnp.float32
    )
    act_grad = to_channels(act_part.astype(jnp.bfloat16))
    slope = gelu_slope(mixed)
    mix_grad = (
        (act_grad.astype(jnp.float32).reshape(slope.shape) * slope)
        .astype(jnp.bfloat16)
        .reshape(slab_shape)
    )
    padded_grad = lift(with_halo(mix_grad, "space", 1))
    hid_grad = core(padded_grad, filter_taps, -1).astype(jnp.bfloat16).reshape(slab_shape)
    back_part = lax.dot_general(
        full_in, to_cells(hid_grad), contract_first, preferred_element_type=jnp.float32
    )
    volume_grad = to_channels((grad_cells.astype(jnp.float32) + back_part).astype(jnp.bfloat16))
    return block_out, volume_grad


def body(volume, out_grad, weight_in, weight_out, filter_taps, filter_bias):
    own = volume.shape[0]
    parts = lax.axis_size("chan")
    groups, space = lax.axis_size("groups"), lax.axis_size("space")
    whole_rows = CY % parts == 0 and (CY // parts * CX) % LANES == 0 and parts & (parts - 1) == 0
    whole_shares = own % LANES == 0 and own % (16 * groups * space) == 0
    split = whole_rows and whole_shares and (groups, space) == (2, 4)
    chosen = split_cells_body if split else exchange_body
    return chosen(volume, out_grad, weight_in, weight_out, filter_taps, filter_bias)


def solution(mesh):
    field = P(("groups", "chan"), "space", None)
    placed = (field, field, P("chan", None), P("chan", None), P("chan", None), P("chan"))
    return jax.shard_map(
        body,
        mesh=mesh,
        in_specs=placed,
        out_specs=(field, field),
        check_vma=False,
    )
```

```python
import jax
import jax.numpy as jnp
from jax import lax
from jax.experimental import pallas as pl
from jax.experimental.pallas import tpu as pltpu
from jax.sharding import PartitionSpec as P

CX = 32
CY = 16
LANES = 128


root_half = 0.7071067811865476
inv_root_two_pi = 0.3989422804014327


def gelu_value(field):
    return 0.5 * field * (1.0 + lax.erf(field * root_half))


def gelu_slope(field):
    return (
        0.5 * (1.0 + lax.erf(field * root_half))
        + field * jnp.exp(-0.5 * field * field) * inv_root_two_pi
    )


def fill_padded(padded, own, row_low, row_high, plane_low, plane_high):
    planes, rows = own.shape[0], own.shape[1]
    for z in range(planes):
        padded[z + 1, 0] = row_low[z].astype(jnp.float32)
        padded[z + 1, rows + 1] = row_high[z].astype(jnp.float32)
        for y in range(rows):
            padded[z + 1, y + 1] = own[z, y].astype(jnp.float32)
    for y in range(rows + 2):
        padded[0, y] = plane_low[y].astype(jnp.float32)
        padded[planes + 1, y] = plane_high[y].astype(jnp.float32)


def stencil_row(padded, taps, z, y, flip):
    sums = [None, None, None]
    for a in range(3):
        for b in range(3):
            row = padded[z + a, y + b]
            for e in range(3):
                index = (a * 3 + b) * 3 + e
                tap = taps[0, 26 - index if flip else index]
                term = row * tap[None, :]
                sums[e] = term if sums[e] is None else sums[e] + term
    x = lax.broadcasted_iota(jnp.int32, sums[0].shape, 0)
    extent = sums[0].shape[0]
    before = jnp.where(x == 0, 0.0, pltpu.roll(sums[0], 1, 0))
    after = jnp.where(x == extent - 1, 0.0, pltpu.roll(sums[2], extent - 1, 0))
    return sums[1] + (before + after)


def doubling(count):
    masks = []
    while count > 1:
        masks.append(count - 1)
        count //= 2
    return masks


def distances(count):
    found = [0]
    for mask in doubling(count):
        found += [mask ^ distance for distance in found]
    return found


def piece_copies(here, mine, other, full, sems):
    chan, seat = here[0], here[1]
    copies = []
    for slot, distance in enumerate(distances(mine.shape[1])):
        for side, pieces in enumerate((mine, other)):
            for turn in range(pieces.shape[0]):
                copies.append(
                    pltpu.make_async_copy(
                        pieces.at[turn, slot],
                        full.at[chan ^ distance, seat ^ side ^ (2 * turn)],
                        sems.at[chan ^ distance, 2 * turn + side],
                    )
                )
    return copies


def wait_block(block, mine, other, full, sems):
    for side, pieces in enumerate((mine, other)):
        for turn in range(pieces.shape[0]):
            pltpu.make_async_copy(
                pieces.at[turn, 0], full.at[block, 2 * turn + side], sems.at[block, 2 * turn + side]
            ).wait()


def start_all(copies):
    for copy in copies:
        copy.start()


def wait_all(copies):
    for copy in copies:
        copy.wait()


def add_planes(base, product, out):
    planes, _, width = base.shape
    for z in range(planes):
        total = base[z].astype(jnp.float32) + product[:, z * width : (z + 1) * width]
        out[z] = total.astype(out.dtype)


def forward_kernel(
    here, own, row_low, row_high, plane_low, plane_high, taps, mine, other, *rest
):
    count = (len(rest) - 5) // 2
    inputs, outputs = rest[:count], rest[count : 2 * count]
    slope, padded, active, weight, sems = rest[2 * count :]
    step = pl.program_id(0)
    planes, rows, extent = own.shape[:3]
    copies = piece_copies(here, mine, other, weight, sems)

    @pl.when(step == 0)
    def _():
        start_all(copies)

    fill_padded(padded, own, row_low, row_high, plane_low, plane_high)
    lanes = pl.ds(pl.multiple_of(step * LANES, LANES), LANES)
    for z in range(planes):
        for y in range(rows):
            mixed = stencil_row(padded, taps, z, y, False) + taps[0, 27][None, :]
            half = 0.5 * (1.0 + lax.erf(mixed * root_half))
            at = (z * rows + y) * extent
            active[at : at + extent, lanes] = (mixed * half).astype(active.dtype)
            slope[z, y] = half + mixed * jnp.exp(-0.5 * mixed * mixed) * inv_root_two_pi

    @pl.when(step == pl.num_programs(0) - 1)
    def _():
        wait_all(copies)
        for shift in range(count):
            rows_of = weight[here[0] ^ shift]
            product = lax.dot_general(
                rows_of.reshape(-1, rows_of.shape[-1]),
                active[...],
                (((1,), (1,)), ((), ())),
                preferred_element_type=jnp.float32,
            )
            add_planes(inputs[shift], product, outputs[shift])


def backward_kernel(
    here, own, row_low, row_high, plane_low, plane_high, taps, mine, other, *rest
):
    count = (len(rest) - 4) // 2
    inputs, outputs = rest[:count], rest[count : 2 * count]
    padded, grads, weight, sems = rest[2 * count :]
    step = pl.program_id(0)
    planes, rows, extent = own.shape[:3]
    copies = piece_copies(here, mine, other, weight, sems)

    @pl.when(step == 0)
    def _():
        start_all(copies)

    fill_padded(padded, own, row_low, row_high, plane_low, plane_high)
    lanes = pl.ds(pl.multiple_of(step * LANES, LANES), LANES)
    for z in range(planes):
        for y in range(rows):
            at = (z * rows + y) * extent
            total = stencil_row(padded, taps, z, y, True)
            grads[at : at + extent, lanes] = total.astype(grads.dtype)

    @pl.when(step == pl.num_programs(0) - 1)
    def _():
        wait_all(copies)
        channels = grads.shape[1]
        width = inputs[0].shape[1]
        for shift in range(count):
            start = pl.multiple_of((here[0] ^ shift) * width, width)
            columns = weight[:, :, :, pl.ds(start, width)].reshape(channels, width)
            product = jnp.dot(grads[...], columns, preferred_element_type=jnp.float32)
            add_planes(inputs[shift], product.T, outputs[shift])


def weight_scratch(mine):
    turns, parts, share, channels = mine.shape
    return [
        pltpu.VMEM((parts, 2 * turns, share, channels), mine.dtype),
        pltpu.SemaphoreType.DMA((parts, 2 * turns)),
    ]


def stencil(here, own, halo, taps, weight, blocks, forward):
    planes, rows, extent, channels = own.shape
    cells = planes * rows * extent
    per_table = taps.shape[2] // LANES

    def block(*lead):
        zeros = (0,) * len(lead)
        return pl.BlockSpec(lead + (LANES,), lambda c, here: zeros + (c,))

    def resident(shape):
        return pl.BlockSpec(shape, lambda c, here: (0,) * len(shape), pipeline_mode=pl.Buffered(1))

    def table_at(c, here):
        away = (c // per_table) ^ here[0]
        slot = 0
        for place, distance in enumerate(distances(taps.shape[0])):
            slot = jnp.where(away == distance, place, slot)
        return slot, 0, c % per_table

    anywhere = pl.BlockSpec(memory_space=pltpu.HBM)
    in_specs = [
        block(planes, rows, extent),
        block(planes, extent),
        block(planes, extent),
        block(rows + 2, extent),
        block(rows + 2, extent),
        pl.BlockSpec((1, 28, LANES), table_at),
        anywhere,
        anywhere,
    ]
    in_specs += [resident(piece.shape) for piece in blocks]
    out_specs = [resident(piece.shape) for piece in blocks]
    out_shape = [jax.ShapeDtypeStruct(piece.shape, piece.dtype) for piece in blocks]
    if forward:
        out_specs.append(block(planes, rows, extent))
        out_shape.append(jax.ShapeDtypeStruct(own.shape, jnp.float32))
    return pl.pallas_call(
        forward_kernel if forward else backward_kernel,
        grid_spec=pltpu.PrefetchScalarGridSpec(
            num_scalar_prefetch=1,
            grid=(channels // LANES,),
            in_specs=in_specs,
            out_specs=out_specs,
            scratch_shapes=[
                pltpu.VMEM((planes + 2, rows + 2, extent, LANES), jnp.float32),
                pltpu.VMEM((cells, channels), own.dtype),
                *weight_scratch(weight[0]),
            ],
        ),
        out_shape=out_shape,
    )(here, own, *halo, taps, *weight, *blocks)


def turn_blocks(here, inputs, turned):
    planes, own, width = inputs[0].shape
    for shift, block in enumerate(inputs):
        start = pl.multiple_of((here[0] ^ shift) * own, own)
        for z in range(planes):
            turned[z * width : (z + 1) * width, pl.ds(start, own)] = block[z].T


def put_with_edges(value, out, first, last, fore, back):
    out[...] = value
    planes, extent, width = first.shape
    plane = value.shape[0] // planes
    rows = plane // extent
    for z in range(planes):
        first[z] = value[z * plane : z * plane + extent]
        last[z] = value[(z + 1) * plane - extent : (z + 1) * plane]
    for edge, z in ((back, 0), (fore, planes - 1)):
        edge[0] = jnp.zeros((extent, width), edge.dtype)
        edge[rows + 1] = jnp.zeros((extent, width), edge.dtype)
        for y in range(rows):
            at = z * plane + y * extent
            edge[y + 1] = value[at : at + extent]


def hidden_kernel(here, mine, other, *rest, count):
    inputs, (*outputs, turned, weight, sems) = rest[:count], rest[count:]

    @pl.when(pl.program_id(0) == 0)
    def _():
        start_all(piece_copies(here, mine, other, weight, sems))
        turn_blocks(here, inputs, turned)

    wait_block(pl.program_id(0), mine, other, weight, sems)
    rows_of = weight[pl.program_id(0)]
    value = lax.dot_general(
        turned[...],
        rows_of.reshape(-1, rows_of.shape[-1]),
        (((1,), (1,)), ((), ())),
        preferred_element_type=jnp.float32,
    )
    put_with_edges(value.astype(turned.dtype), *outputs)


def mix_kernel(here, mine, other, *rest, count):
    inputs, (slope, *outputs, turned, weight, sems) = rest[:count], rest[count:]

    @pl.when(pl.program_id(0) == 0)
    def _():
        copies = piece_copies(here, mine, other, weight, sems)
        start_all(copies)
        turn_blocks(here, inputs, turned)
        wait_all(copies)

    channels, width = turned.shape[1], slope.shape[1]
    start = pl.multiple_of(pl.program_id(0) * width, width)
    columns = weight[:, :, :, pl.ds(start, width)].reshape(channels, width)
    grad = jnp.dot(turned[...], columns, preferred_element_type=jnp.float32)
    grad = grad.astype(turned.dtype).astype(jnp.float32)
    put_with_edges((grad * slope[...]).astype(turned.dtype), *outputs)


def product_call(here, blocks, weight, slope=None):
    planes, own, width = blocks[0].shape
    cells = planes * width
    count = len(blocks)
    channels = own * count
    dtype = blocks[0].dtype
    columns = pl.BlockSpec((cells, own), lambda c, here: (0, c))
    room = width // CX + 2
    row = pl.BlockSpec((planes, CX, own), lambda c, here: (0, 0, c))
    plane = pl.BlockSpec((room, CX, own), lambda c, here: (0, 0, c))
    whole = pl.BlockSpec(
        blocks[0].shape, lambda c, here: (0, 0, 0), pipeline_mode=pl.Buffered(1)
    )
    anywhere = pl.BlockSpec(memory_space=pltpu.HBM)
    kernel, extra = (hidden_kernel, []) if slope is None else (mix_kernel, [slope])
    row_shape = jax.ShapeDtypeStruct((planes, CX, channels), dtype)
    plane_shape = jax.ShapeDtypeStruct((room, CX, channels), dtype)
    return pl.pallas_call(
        lambda *refs: kernel(*refs, count=count),
        grid_spec=pltpu.PrefetchScalarGridSpec(
            num_scalar_prefetch=1,
            grid=(count,),
            in_specs=[anywhere] * 2 + [whole] * count + [columns] * len(extra),
            out_specs=[columns, row, row, plane, plane],
            scratch_shapes=[pltpu.VMEM((cells, channels), dtype), *weight_scratch(weight[0])],
        ),
        out_shape=[
            jax.ShapeDtypeStruct((cells, channels), dtype),
            row_shape,
            row_shape,
            plane_shape,
            plane_shape,
        ],
    )(here, *weight, *blocks, *extra)


def shift_pairs(axis):
    count = lax.axis_size(axis)
    forward = [(i, i + 1) for i in range(count - 1)]
    return forward, [(target, source) for source, target in forward]


def split_cells_body(volume, out_grad, weight_in, weight_out, filter_taps, filter_bias):
    own, planes, cells = volume.shape
    parts = lax.axis_size("chan")
    rows = CY // parts
    width = rows * CX
    channels = own * parts
    others = ("groups", "space")
    seat = lax.axis_index(others)
    chan = lax.axis_index("chan")
    share = own // lax.axis_size(others)
    here = jnp.stack([chan, seat]).astype(jnp.int32)
    shifts = sorted(range(1, parts), key=lambda shift: (shift & (parts // 2) == 0, shift))

    def swap(part, axes, partner):
        count = lax.axis_size(axes)
        return lax.ppermute(part, axes, [(i, partner(i)) for i in range(count)])

    def exchange(blocks):
        got = {0: blocks[0]}
        for shift in shifts:
            got[shift] = swap(blocks[shift], "chan", lambda i: i ^ shift)
        return [got[shift] for shift in range(parts)]

    def cut(field):
        pieces, place = {}, chan
        for shift in shifts + [0]:
            start = (place ^ shift) * width
            piece = lax.dynamic_slice_in_dim(field, start, width, axis=2).transpose(1, 0, 2)
            pieces[shift], place = lax.optimization_barrier((piece, place))
        return pieces

    def paste(pieces):
        field = jnp.zeros((own, planes, cells), pieces[0].dtype)
        for shift in [0] + shifts:
            piece = pieces[shift].transpose(1, 0, 2)
            field = lax.dynamic_update_slice_in_dim(field, piece, (chan ^ shift) * width, axis=2)
        return field

    def gather_column(piece):
        column = piece[None]
        for mask in doubling(parts):
            got = swap(column, "chan", lambda i: i ^ mask)
            column = jnp.concatenate([column, got])
        return column

    def gather_weight(column):
        over_x = swap(column, others, lambda i: i ^ 2)
        over_y = swap(column, others, lambda i: i ^ 4)
        mixed = jnp.where(seat & 1 == 0, over_y, over_x)
        far = swap(mixed, others, lambda i: i ^ (4 if i & 1 else 2))
        mine = jnp.stack([column, over_x, over_y, far])
        return mine, swap(mine, others, lambda i: i ^ 1)

    def halo_of(first, last, fore, back):
        forward, backward = shift_pairs("chan")
        row_low = lax.ppermute(last, "chan", forward)
        row_high = lax.ppermute(first, "chan", backward)
        forward, backward = shift_pairs("space")

        def joined(plane, z):
            plane = lax.dynamic_update_slice_in_dim(plane, row_low[z][None], 0, axis=0)
            return lax.dynamic_update_slice_in_dim(plane, row_high[z][None], rows + 1, axis=0)

        plane_low = lax.ppermute(joined(fore, planes - 1), "space", forward)
        plane_high = lax.ppermute(joined(back, 0), "space", backward)
        return row_low, row_high, plane_low, plane_high

    grid = (planes, rows, CX, channels)
    pieces = [
        lax.dynamic_slice_in_dim(weight, seat * share, share, axis=0)
        for weight in (weight_in, weight_out)
    ]
    column = gather_column(jnp.concatenate(pieces))
    full_in = gather_weight(column[:, :share])
    full_out = gather_weight(column[:, share:])
    table = jnp.concatenate([filter_taps, filter_bias[:, None]], axis=1).T
    taps = gather_column(table)
    vol_cut, grad_cut = cut(volume), cut(out_grad)
    own_block, taps, grad_cut = lax.optimization_barrier((vol_cut[0], taps, grad_cut))
    vol_blocks = exchange({**vol_cut, 0: own_block})
    grad_blocks = exchange(grad_cut)
    hidden, *edges = product_call(here, vol_blocks, full_in)
    halo = halo_of(*edges)
    *out_blocks, slope = stencil(here, hidden.reshape(grid), halo, taps, full_out, vol_blocks, True)
    out_found = exchange(out_blocks)
    mix_grad, *edges = product_call(
        here, grad_blocks, full_out, slope.reshape(planes * width, channels)
    )
    halo = halo_of(*edges)
    back_blocks = list(
        stencil(here, mix_grad.reshape(grid), halo, taps, full_in, grad_blocks, False)
    )
    out_found, back_blocks[0] = lax.optimization_barrier((out_found, back_blocks[0]))
    block_out = paste(out_found)
    volume_grad = paste(exchange(back_blocks))
    return block_out, volume_grad


def with_halo(block, axis, dim):
    forward, backward = shift_pairs(axis)
    low = lax.ppermute(lax.slice_in_dim(block, block.shape[dim] - 1, None, axis=dim), axis, forward)
    high = lax.ppermute(lax.slice_in_dim(block, 0, 1, axis=dim), axis, backward)
    return jnp.concatenate([low, block, high], axis=dim)


def core(padded, filter_taps, direction):
    extent_z = padded.shape[1] - 2
    extent_y = padded.shape[2] - 2
    extent_x = padded.shape[3] - 2
    summed = jnp.zeros((padded.shape[0], extent_z, extent_y, extent_x), jnp.float32)
    for shift_z in range(3):
        for shift_y in range(3):
            for shift_x in range(3):
                tap_index = (shift_z * 3 + shift_y) * 3 + shift_x
                begin_z = 1 + direction * (shift_z - 1)
                begin_y = 1 + direction * (shift_y - 1)
                begin_x = 1 + direction * (shift_x - 1)
                window = padded[
                    :,
                    begin_z : begin_z + extent_z,
                    begin_y : begin_y + extent_y,
                    begin_x : begin_x + extent_x,
                ]
                summed = summed + filter_taps[:, tap_index][:, None, None, None] * window
    return summed


def lift(field_z):
    extended = field_z.astype(jnp.float32).reshape(field_z.shape[0], field_z.shape[1], CY, CX)
    return jnp.pad(extended, ((0, 0), (0, 0), (1, 1), (1, 1)))


def exchange_body(volume, out_grad, weight_in, weight_out, filter_taps, filter_bias):
    slab_shape = volume.shape
    contract_first = (((0,), (0,)), ((), ()))

    def to_cells(field):
        return lax.all_to_all(
            field.reshape(field.shape[0], -1), "chan", split_axis=1, concat_axis=0, tiled=True
        )

    def to_channels(field):
        return lax.all_to_all(field, "chan", split_axis=0, concat_axis=1, tiled=True).reshape(
            slab_shape
        )

    full_in = lax.all_gather(weight_in, "chan", axis=0, tiled=True)
    full_out = lax.all_gather(weight_out, "chan", axis=0, tiled=True)
    vol_cells = to_cells(volume)
    hidden = to_channels(
        jnp.dot(full_in, vol_cells, preferred_element_type=jnp.float32).astype(jnp.bfloat16)
    )
    padded = lift(with_halo(hidden, "space", 1))
    mixed = core(padded, filter_taps, 1) + filter_bias[:, None, None, None]
    active = gelu_value(mixed).astype(jnp.bfloat16).reshape(slab_shape)
    out_cells = vol_cells.astype(jnp.float32) + jnp.dot(
        full_out, to_cells(active), preferred_element_type=jnp.float32
    )
    block_out = to_channels(out_cells.astype(jnp.bfloat16))
    grad_cells = to_cells(out_grad)
    act_part = lax.dot_general(
        full_out, grad_cells, contract_first, preferred_element_type=jnp.float32
    )
    act_grad = to_channels(act_part.astype(jnp.bfloat16))
    slope = gelu_slope(mixed)
    mix_grad = (
        (act_grad.astype(jnp.float32).reshape(slope.shape) * slope)
        .astype(jnp.bfloat16)
        .reshape(slab_shape)
    )
    padded_grad = lift(with_halo(mix_grad, "space", 1))
    hid_grad = core(padded_grad, filter_taps, -1).astype(jnp.bfloat16).reshape(slab_shape)
    back_part = lax.dot_general(
        full_in, to_cells(hid_grad), contract_first, preferred_element_type=jnp.float32
    )
    volume_grad = to_channels((grad_cells.astype(jnp.float32) + back_part).astype(jnp.bfloat16))
    return block_out, volume_grad


def body(volume, out_grad, weight_in, weight_out, filter_taps, filter_bias):
    own = volume.shape[0]
    parts = lax.axis_size("chan")
    groups, space = lax.axis_size("groups"), lax.axis_size("space")
    whole_rows = CY % parts == 0 and (CY // parts * CX) % LANES == 0 and parts & (parts - 1) == 0
    whole_shares = own % LANES == 0 and own % (16 * groups * space) == 0
    split = whole_rows and whole_shares and (groups, space) == (2, 4)
    chosen = split_cells_body if split else exchange_body
    return chosen(volume, out_grad, weight_in, weight_out, filter_taps, filter_bias)


def solution(mesh):
    field = P(("groups", "chan"), "space", None)
    placed = (field, field, P("chan", None), P("chan", None), P("chan", None), P("chan"))
    return jax.shard_map(
        body,
        mesh=mesh,
        in_specs=placed,
        out_specs=(field, field),
        check_vma=False,
    )
```

```python
import jax
import jax.numpy as jnp
from jax import lax
from jax.experimental import pallas as pl
from jax.experimental.pallas import tpu as pltpu
from jax.sharding import PartitionSpec as P

CX = 32
CY = 16
LANES = 128


root_half = 0.7071067811865476
inv_root_two_pi = 0.3989422804014327


def gelu_value(field):
    return 0.5 * field * (1.0 + lax.erf(field * root_half))


def gelu_slope(field):
    return (
        0.5 * (1.0 + lax.erf(field * root_half))
        + field * jnp.exp(-0.5 * field * field) * inv_root_two_pi
    )


def fill_padded(padded, own, row_low, row_high, plane_low, plane_high):
    planes, rows = own.shape[0], own.shape[1]
    for z in range(planes):
        padded[z + 1, 0] = row_low[z].astype(jnp.float32)
        padded[z + 1, rows + 1] = row_high[z].astype(jnp.float32)
        for y in range(rows):
            padded[z + 1, y + 1] = own[z, y].astype(jnp.float32)
    for y in range(rows + 2):
        padded[0, y] = plane_low[y].astype(jnp.float32)
        padded[planes + 1, y] = plane_high[y].astype(jnp.float32)


def stencil_row(padded, taps, z, y, flip):
    sums = [None, None, None]
    for a in range(3):
        for b in range(3):
            row = padded[z + a, y + b]
            for e in range(3):
                index = (a * 3 + b) * 3 + e
                tap = taps[0, 26 - index if flip else index]
                term = row * tap[None, :]
                sums[e] = term if sums[e] is None else sums[e] + term
    x = lax.broadcasted_iota(jnp.int32, sums[0].shape, 0)
    extent = sums[0].shape[0]
    before = jnp.where(x == 0, 0.0, pltpu.roll(sums[0], 1, 0))
    after = jnp.where(x == extent - 1, 0.0, pltpu.roll(sums[2], extent - 1, 0))
    return sums[1] + (before + after)


def doubling(count):
    masks = []
    while count > 1:
        masks.append(count - 1)
        count //= 2
    return masks


def distances(count):
    found = [0]
    for mask in doubling(count):
        found += [mask ^ distance for distance in found]
    return found


def piece_copies(here, mine, other, full, sems):
    chan, seat = here[0], here[1]
    copies = []
    for slot, distance in enumerate(distances(mine.shape[1])):
        for side, pieces in enumerate((mine, other)):
            for turn in range(pieces.shape[0]):
                copies.append(
                    pltpu.make_async_copy(
                        pieces.at[turn, slot],
                        full.at[chan ^ distance, seat ^ side ^ (2 * turn)],
                        sems.at[chan ^ distance, 2 * turn + side],
                    )
                )
    return copies


def wait_block(block, mine, other, full, sems):
    for side, pieces in enumerate((mine, other)):
        for turn in range(pieces.shape[0]):
            pltpu.make_async_copy(
                pieces.at[turn, 0], full.at[block, 2 * turn + side], sems.at[block, 2 * turn + side]
            ).wait()


def start_all(copies):
    for copy in copies:
        copy.start()


def wait_all(copies):
    for copy in copies:
        copy.wait()


def add_planes(base, product, out):
    planes, _, width = base.shape
    for z in range(planes):
        total = base[z].astype(jnp.float32) + product[:, z * width : (z + 1) * width]
        out[z] = total.astype(out.dtype)


def forward_kernel(
    here, own, row_low, row_high, plane_low, plane_high, taps, mine, other, *rest
):
    count = (len(rest) - 5) // 2
    inputs, outputs = rest[:count], rest[count : 2 * count]
    slope, padded, active, weight, sems = rest[2 * count :]
    step = pl.program_id(0)
    planes, rows, extent = own.shape[:3]
    copies = piece_copies(here, mine, other, weight, sems)

    @pl.when(step == 0)
    def _():
        start_all(copies)

    fill_padded(padded, own, row_low, row_high, plane_low, plane_high)
    lanes = pl.ds(pl.multiple_of(step * LANES, LANES), LANES)
    for z in range(planes):
        for y in range(rows):
            mixed = stencil_row(padded, taps, z, y, False) + taps[0, 27][None, :]
            half = 0.5 * (1.0 + lax.erf(mixed * root_half))
            at = (z * rows + y) * extent
            active[at : at + extent, lanes] = (mixed * half).astype(active.dtype)
            slope[z, y] = half + mixed * jnp.exp(-0.5 * mixed * mixed) * inv_root_two_pi

    @pl.when(step == pl.num_programs(0) - 1)
    def _():
        wait_all(copies)
        for shift in range(count):
            rows_of = weight[here[0] ^ shift]
            product = lax.dot_general(
                rows_of.reshape(-1, rows_of.shape[-1]),
                active[...],
                (((1,), (1,)), ((), ())),
                preferred_element_type=jnp.float32,
            )
            add_planes(inputs[shift], product, outputs[shift])


def backward_kernel(
    here, own, row_low, row_high, plane_low, plane_high, taps, mine, other, *rest
):
    count = (len(rest) - 4) // 2
    inputs, outputs = rest[:count], rest[count : 2 * count]
    padded, grads, weight, sems = rest[2 * count :]
    step = pl.program_id(0)
    planes, rows, extent = own.shape[:3]
    copies = piece_copies(here, mine, other, weight, sems)

    @pl.when(step == 0)
    def _():
        start_all(copies)

    fill_padded(padded, own, row_low, row_high, plane_low, plane_high)
    lanes = pl.ds(pl.multiple_of(step * LANES, LANES), LANES)
    for z in range(planes):
        for y in range(rows):
            at = (z * rows + y) * extent
            total = stencil_row(padded, taps, z, y, True)
            grads[at : at + extent, lanes] = total.astype(grads.dtype)

    @pl.when(step == pl.num_programs(0) - 1)
    def _():
        wait_all(copies)
        channels = grads.shape[1]
        width = inputs[0].shape[1]
        for shift in range(count):
            start = pl.multiple_of((here[0] ^ shift) * width, width)
            columns = weight[:, :, :, pl.ds(start, width)].reshape(channels, width)
            product = jnp.dot(grads[...], columns, preferred_element_type=jnp.float32)
            add_planes(inputs[shift], product.T, outputs[shift])


def weight_scratch(mine):
    turns, parts, share, channels = mine.shape
    return [
        pltpu.VMEM((parts, 2 * turns, share, channels), mine.dtype),
        pltpu.SemaphoreType.DMA((parts, 2 * turns)),
    ]


def stencil(here, own, halo, taps, weight, blocks, forward):
    planes, rows, extent, channels = own.shape
    cells = planes * rows * extent
    per_table = taps.shape[2] // LANES

    def block(*lead):
        zeros = (0,) * len(lead)
        return pl.BlockSpec(lead + (LANES,), lambda c, here: zeros + (c,))

    def resident(shape):
        return pl.BlockSpec(shape, lambda c, here: (0,) * len(shape), pipeline_mode=pl.Buffered(1))

    def table_at(c, here):
        away = (c // per_table) ^ here[0]
        slot = 0
        for place, distance in enumerate(distances(taps.shape[0])):
            slot = jnp.where(away == distance, place, slot)
        return slot, 0, c % per_table

    anywhere = pl.BlockSpec(memory_space=pltpu.HBM)
    in_specs = [
        block(planes, rows, extent),
        block(planes, extent),
        block(planes, extent),
        block(rows + 2, extent),
        block(rows + 2, extent),
        pl.BlockSpec((1, 28, LANES), table_at),
        anywhere,
        anywhere,
    ]
    in_specs += [resident(piece.shape) for piece in blocks]
    out_specs = [resident(piece.shape) for piece in blocks]
    out_shape = [jax.ShapeDtypeStruct(piece.shape, piece.dtype) for piece in blocks]
    if forward:
        out_specs.append(block(planes, rows, extent))
        out_shape.append(jax.ShapeDtypeStruct(own.shape, jnp.float32))
    return pl.pallas_call(
        forward_kernel if forward else backward_kernel,
        grid_spec=pltpu.PrefetchScalarGridSpec(
            num_scalar_prefetch=1,
            grid=(channels // LANES,),
            in_specs=in_specs,
            out_specs=out_specs,
            scratch_shapes=[
                pltpu.VMEM((planes + 2, rows + 2, extent, LANES), jnp.float32),
                pltpu.VMEM((cells, channels), own.dtype),
                *weight_scratch(weight[0]),
            ],
        ),
        out_shape=out_shape,
    )(here, own, *halo, taps, *weight, *blocks)


def turn_blocks(here, inputs, turned):
    planes, own, width = inputs[0].shape
    for shift, block in enumerate(inputs):
        start = pl.multiple_of((here[0] ^ shift) * own, own)
        for z in range(planes):
            turned[z * width : (z + 1) * width, pl.ds(start, own)] = block[z].T


def put_with_edges(value, out, first, last, fore, back):
    out[...] = value
    planes, extent, width = first.shape
    plane = value.shape[0] // planes
    rows = plane // extent
    for z in range(planes):
        first[z] = value[z * plane : z * plane + extent]
        last[z] = value[(z + 1) * plane - extent : (z + 1) * plane]
    for edge, z in ((back, 0), (fore, planes - 1)):
        edge[0] = jnp.zeros((extent, width), edge.dtype)
        edge[rows + 1] = jnp.zeros((extent, width), edge.dtype)
        for y in range(rows):
            at = z * plane + y * extent
            edge[y + 1] = value[at : at + extent]


def hidden_kernel(here, mine, other, *rest, count):
    inputs, (*outputs, turned, weight, sems) = rest[:count], rest[count:]

    @pl.when(pl.program_id(0) == 0)
    def _():
        start_all(piece_copies(here, mine, other, weight, sems))
        turn_blocks(here, inputs, turned)

    wait_block(pl.program_id(0), mine, other, weight, sems)
    rows_of = weight[pl.program_id(0)]
    value = lax.dot_general(
        turned[...],
        rows_of.reshape(-1, rows_of.shape[-1]),
        (((1,), (1,)), ((), ())),
        preferred_element_type=jnp.float32,
    )
    put_with_edges(value.astype(turned.dtype), *outputs)


def mix_kernel(here, mine, other, *rest, count):
    inputs, (slope, *outputs, turned, weight, sems) = rest[:count], rest[count:]

    @pl.when(pl.program_id(0) == 0)
    def _():
        copies = piece_copies(here, mine, other, weight, sems)
        start_all(copies)
        turn_blocks(here, inputs, turned)
        wait_all(copies)

    channels, width = turned.shape[1], slope.shape[1]
    start = pl.multiple_of(pl.program_id(0) * width, width)
    columns = weight[:, :, :, pl.ds(start, width)].reshape(channels, width)
    grad = jnp.dot(turned[...], columns, preferred_element_type=jnp.float32)
    grad = grad.astype(turned.dtype).astype(jnp.float32)
    put_with_edges((grad * slope[...]).astype(turned.dtype), *outputs)


def product_call(here, blocks, weight, slope=None):
    planes, own, width = blocks[0].shape
    cells = planes * width
    count = len(blocks)
    channels = own * count
    dtype = blocks[0].dtype
    columns = pl.BlockSpec((cells, own), lambda c, here: (0, c))
    room = width // CX + 2
    row = pl.BlockSpec((planes, CX, own), lambda c, here: (0, 0, c))
    plane = pl.BlockSpec((room, CX, own), lambda c, here: (0, 0, c))
    whole = pl.BlockSpec(
        blocks[0].shape, lambda c, here: (0, 0, 0), pipeline_mode=pl.Buffered(1)
    )
    anywhere = pl.BlockSpec(memory_space=pltpu.HBM)
    kernel, extra = (hidden_kernel, []) if slope is None else (mix_kernel, [slope])
    row_shape = jax.ShapeDtypeStruct((planes, CX, channels), dtype)
    plane_shape = jax.ShapeDtypeStruct((room, CX, channels), dtype)
    return pl.pallas_call(
        lambda *refs: kernel(*refs, count=count),
        grid_spec=pltpu.PrefetchScalarGridSpec(
            num_scalar_prefetch=1,
            grid=(count,),
            in_specs=[anywhere] * 2 + [whole] * count + [columns] * len(extra),
            out_specs=[columns, row, row, plane, plane],
            scratch_shapes=[pltpu.VMEM((cells, channels), dtype), *weight_scratch(weight[0])],
        ),
        out_shape=[
            jax.ShapeDtypeStruct((cells, channels), dtype),
            row_shape,
            row_shape,
            plane_shape,
            plane_shape,
        ],
    )(here, *weight, *blocks, *extra)


def shift_pairs(axis):
    count = lax.axis_size(axis)
    forward = [(i, i + 1) for i in range(count - 1)]
    return forward, [(target, source) for source, target in forward]


def split_cells_body(volume, out_grad, weight_in, weight_out, filter_taps, filter_bias):
    own, planes, cells = volume.shape
    parts = lax.axis_size("chan")
    rows = CY // parts
    width = rows * CX
    channels = own * parts
    others = ("groups", "space")
    seat = lax.axis_index(others)
    chan = lax.axis_index("chan")
    share = own // lax.axis_size(others)
    here = jnp.stack([chan, seat]).astype(jnp.int32)
    shifts = sorted(range(1, parts), key=lambda shift: (shift & (parts // 2) == 0, shift))

    def swap(part, axes, partner):
        count = lax.axis_size(axes)
        return lax.ppermute(part, axes, [(i, partner(i)) for i in range(count)])

    def exchange(blocks):
        got = {0: blocks[0]}
        for shift in shifts:
            got[shift] = swap(blocks[shift], "chan", lambda i: i ^ shift)
        return [got[shift] for shift in range(parts)]

    def cut(field, order, place):
        pieces = {}
        for shift in order:
            start = (place ^ shift) * width
            piece = lax.dynamic_slice_in_dim(field, start, width, axis=2).transpose(1, 0, 2)
            pieces[shift], place = lax.optimization_barrier((piece, place))
        return pieces

    def paste(pieces):
        field = jnp.zeros((own, planes, cells), pieces[0].dtype)
        for shift in [0] + shifts:
            piece = pieces[shift].transpose(1, 0, 2)
            field = lax.dynamic_update_slice_in_dim(field, piece, (chan ^ shift) * width, axis=2)
        return field

    def gather_column(piece, beside=None):
        column = piece[None]
        for mask in doubling(parts):
            if mask == 1 and beside is not None:
                column, beside = lax.optimization_barrier((column, beside))
            got = swap(column, "chan", lambda i: i ^ mask)
            column = jnp.concatenate([column, got])
        return column, beside

    def gather_weight(column):
        over_x = swap(column, others, lambda i: i ^ 2)
        over_y = swap(column, others, lambda i: i ^ 4)
        mixed = jnp.where(seat & 1 == 0, over_y, over_x)
        far = swap(mixed, others, lambda i: i ^ (4 if i & 1 else 2))
        mine = jnp.stack([column, over_x, over_y, far])
        return mine, swap(mine, others, lambda i: i ^ 1)

    def halo_of(first, last, fore, back):
        forward, backward = shift_pairs("chan")
        row_low = lax.ppermute(last, "chan", forward)
        row_high = lax.ppermute(first, "chan", backward)
        forward, backward = shift_pairs("space")

        def joined(plane, z):
            plane = lax.dynamic_update_slice_in_dim(plane, row_low[z][None], 0, axis=0)
            return lax.dynamic_update_slice_in_dim(plane, row_high[z][None], rows + 1, axis=0)

        plane_low = lax.ppermute(joined(fore, planes - 1), "space", forward)
        plane_high = lax.ppermute(joined(back, 0), "space", backward)
        return row_low, row_high, plane_low, plane_high

    grid = (planes, rows, CX, channels)
    piece_in, piece_out = (
        lax.dynamic_slice_in_dim(weight, seat * share, share, axis=0)
        for weight in (weight_in, weight_out)
    )
    column, _ = gather_column(piece_in)
    vol_cut = cut(volume, shifts, chan)
    later, column = lax.optimization_barrier((chan, column))
    own_cut = cut(volume, [0], later)
    grad_cut = cut(out_grad, shifts + [0], later)
    full_in = gather_weight(column)
    column, (own_block, here, grad_cut) = gather_column(piece_out, (own_cut[0], here, grad_cut))
    full_out = gather_weight(column)
    table = jnp.concatenate([filter_taps, filter_bias[:, None]], axis=1).T
    taps, _ = gather_column(table)
    own_block, taps = lax.optimization_barrier((own_block, taps))
    vol_blocks = exchange({**vol_cut, 0: own_block})
    grad_blocks = exchange(grad_cut)
    hidden, *edges = product_call(here, vol_blocks, full_in)
    halo = halo_of(*edges)
    *out_blocks, slope = stencil(here, hidden.reshape(grid), halo, taps, full_out, vol_blocks, True)
    out_found = exchange(out_blocks)
    mix_grad, *edges = product_call(
        here, grad_blocks, full_out, slope.reshape(planes * width, channels)
    )
    halo = halo_of(*edges)
    back_blocks = list(
        stencil(here, mix_grad.reshape(grid), halo, taps, full_in, grad_blocks, False)
    )
    out_found, back_blocks[0] = lax.optimization_barrier((out_found, back_blocks[0]))
    block_out = paste(out_found)
    volume_grad = paste(exchange(back_blocks))
    return block_out, volume_grad


def with_halo(block, axis, dim):
    forward, backward = shift_pairs(axis)
    low = lax.ppermute(lax.slice_in_dim(block, block.shape[dim] - 1, None, axis=dim), axis, forward)
    high = lax.ppermute(lax.slice_in_dim(block, 0, 1, axis=dim), axis, backward)
    return jnp.concatenate([low, block, high], axis=dim)


def core(padded, filter_taps, direction):
    extent_z = padded.shape[1] - 2
    extent_y = padded.shape[2] - 2
    extent_x = padded.shape[3] - 2
    summed = jnp.zeros((padded.shape[0], extent_z, extent_y, extent_x), jnp.float32)
    for shift_z in range(3):
        for shift_y in range(3):
            for shift_x in range(3):
                tap_index = (shift_z * 3 + shift_y) * 3 + shift_x
                begin_z = 1 + direction * (shift_z - 1)
                begin_y = 1 + direction * (shift_y - 1)
                begin_x = 1 + direction * (shift_x - 1)
                window = padded[
                    :,
                    begin_z : begin_z + extent_z,
                    begin_y : begin_y + extent_y,
                    begin_x : begin_x + extent_x,
                ]
                summed = summed + filter_taps[:, tap_index][:, None, None, None] * window
    return summed


def lift(field_z):
    extended = field_z.astype(jnp.float32).reshape(field_z.shape[0], field_z.shape[1], CY, CX)
    return jnp.pad(extended, ((0, 0), (0, 0), (1, 1), (1, 1)))


def exchange_body(volume, out_grad, weight_in, weight_out, filter_taps, filter_bias):
    slab_shape = volume.shape
    contract_first = (((0,), (0,)), ((), ()))

    def to_cells(field):
        return lax.all_to_all(
            field.reshape(field.shape[0], -1), "chan", split_axis=1, concat_axis=0, tiled=True
        )

    def to_channels(field):
        return lax.all_to_all(field, "chan", split_axis=0, concat_axis=1, tiled=True).reshape(
            slab_shape
        )

    full_in = lax.all_gather(weight_in, "chan", axis=0, tiled=True)
    full_out = lax.all_gather(weight_out, "chan", axis=0, tiled=True)
    vol_cells = to_cells(volume)
    hidden = to_channels(
        jnp.dot(full_in, vol_cells, preferred_element_type=jnp.float32).astype(jnp.bfloat16)
    )
    padded = lift(with_halo(hidden, "space", 1))
    mixed = core(padded, filter_taps, 1) + filter_bias[:, None, None, None]
    active = gelu_value(mixed).astype(jnp.bfloat16).reshape(slab_shape)
    out_cells = vol_cells.astype(jnp.float32) + jnp.dot(
        full_out, to_cells(active), preferred_element_type=jnp.float32
    )
    block_out = to_channels(out_cells.astype(jnp.bfloat16))
    grad_cells = to_cells(out_grad)
    act_part = lax.dot_general(
        full_out, grad_cells, contract_first, preferred_element_type=jnp.float32
    )
    act_grad = to_channels(act_part.astype(jnp.bfloat16))
    slope = gelu_slope(mixed)
    mix_grad = (
        (act_grad.astype(jnp.float32).reshape(slope.shape) * slope)
        .astype(jnp.bfloat16)
        .reshape(slab_shape)
    )
    padded_grad = lift(with_halo(mix_grad, "space", 1))
    hid_grad = core(padded_grad, filter_taps, -1).astype(jnp.bfloat16).reshape(slab_shape)
    back_part = lax.dot_general(
        full_in, to_cells(hid_grad), contract_first, preferred_element_type=jnp.float32
    )
    volume_grad = to_channels((grad_cells.astype(jnp.float32) + back_part).astype(jnp.bfloat16))
    return block_out, volume_grad


def body(volume, out_grad, weight_in, weight_out, filter_taps, filter_bias):
    own = volume.shape[0]
    parts = lax.axis_size("chan")
    groups, space = lax.axis_size("groups"), lax.axis_size("space")
    whole_rows = CY % parts == 0 and (CY // parts * CX) % LANES == 0 and parts & (parts - 1) == 0
    whole_shares = own % LANES == 0 and own % (16 * groups * space) == 0
    split = whole_rows and whole_shares and (groups, space) == (2, 4)
    chosen = split_cells_body if split else exchange_body
    return chosen(volume, out_grad, weight_in, weight_out, filter_taps, filter_bias)


def solution(mesh):
    field = P(("groups", "chan"), "space", None)
    placed = (field, field, P("chan", None), P("chan", None), P("chan", None), P("chan"))
    return jax.shard_map(
        body,
        mesh=mesh,
        in_specs=placed,
        out_specs=(field, field),
        check_vma=False,
    )
```

```python
import jax
import jax.numpy as jnp
from jax import lax
from jax.experimental import pallas as pl
from jax.experimental.pallas import tpu as pltpu
from jax.sharding import PartitionSpec as P

CX = 32
CY = 16
LANES = 128


root_half = 0.7071067811865476
inv_root_two_pi = 0.3989422804014327


def gelu_value(field):
    return 0.5 * field * (1.0 + lax.erf(field * root_half))


def gelu_slope(field):
    return (
        0.5 * (1.0 + lax.erf(field * root_half))
        + field * jnp.exp(-0.5 * field * field) * inv_root_two_pi
    )


def fill_padded(padded, own, row_low, row_high, plane_low, plane_high):
    planes, rows = own.shape[0], own.shape[1]
    for z in range(planes):
        padded[z + 1, 0] = row_low[z].astype(jnp.float32)
        padded[z + 1, rows + 1] = row_high[z].astype(jnp.float32)
        for y in range(rows):
            padded[z + 1, y + 1] = own[z, y].astype(jnp.float32)
    for y in range(rows + 2):
        padded[0, y] = plane_low[y].astype(jnp.float32)
        padded[planes + 1, y] = plane_high[y].astype(jnp.float32)


def stencil_row(padded, taps, z, y, flip):
    sums = [None, None, None]
    for a in range(3):
        for b in range(3):
            row = padded[z + a, y + b]
            for e in range(3):
                index = (a * 3 + b) * 3 + e
                tap = taps[0, 26 - index if flip else index]
                term = row * tap[None, :]
                sums[e] = term if sums[e] is None else sums[e] + term
    x = lax.broadcasted_iota(jnp.int32, sums[0].shape, 0)
    extent = sums[0].shape[0]
    before = jnp.where(x == 0, 0.0, pltpu.roll(sums[0], 1, 0))
    after = jnp.where(x == extent - 1, 0.0, pltpu.roll(sums[2], extent - 1, 0))
    return sums[1] + (before + after)


def doubling(count):
    masks = []
    while count > 1:
        masks.append(count - 1)
        count //= 2
    return masks


def distances(count):
    found = [0]
    for mask in doubling(count):
        found += [mask ^ distance for distance in found]
    return found


def piece_copies(here, mine, other, full, sems):
    chan, seat = here[0], here[1]
    copies = []
    for slot, distance in enumerate(distances(mine.shape[1])):
        for side, pieces in enumerate((mine, other)):
            for turn in range(pieces.shape[0]):
                copies.append(
                    pltpu.make_async_copy(
                        pieces.at[turn, slot],
                        full.at[chan ^ distance, seat ^ side ^ (2 * turn)],
                        sems.at[chan ^ distance, 2 * turn + side],
                    )
                )
    return copies


def wait_block(block, mine, other, full, sems):
    for side, pieces in enumerate((mine, other)):
        for turn in range(pieces.shape[0]):
            pltpu.make_async_copy(
                pieces.at[turn, 0], full.at[block, 2 * turn + side], sems.at[block, 2 * turn + side]
            ).wait()


def start_all(copies):
    for copy in copies:
        copy.start()


def wait_all(copies):
    for copy in copies:
        copy.wait()


def add_planes(base, product, out):
    planes, _, width = base.shape
    for z in range(planes):
        total = base[z].astype(jnp.float32) + product[:, z * width : (z + 1) * width]
        out[z] = total.astype(out.dtype)


def forward_kernel(
    here, own, row_low, row_high, plane_low, plane_high, taps, mine, other, *rest
):
    count = (len(rest) - 5) // 2
    inputs, outputs = rest[:count], rest[count : 2 * count]
    slope, padded, active, weight, sems = rest[2 * count :]
    step = pl.program_id(0)
    planes, rows, extent = own.shape[:3]
    copies = piece_copies(here, mine, other, weight, sems)

    @pl.when(step == 0)
    def _():
        start_all(copies)

    fill_padded(padded, own, row_low, row_high, plane_low, plane_high)
    lanes = pl.ds(pl.multiple_of(step * LANES, LANES), LANES)
    for z in range(planes):
        for y in range(rows):
            mixed = stencil_row(padded, taps, z, y, False) + taps[0, 27][None, :]
            half = 0.5 * (1.0 + lax.erf(mixed * root_half))
            at = (z * rows + y) * extent
            active[at : at + extent, lanes] = (mixed * half).astype(active.dtype)
            slope[z, y] = half + mixed * jnp.exp(-0.5 * mixed * mixed) * inv_root_two_pi

    @pl.when(step == pl.num_programs(0) - 1)
    def _():
        wait_all(copies)
        for shift in range(count):
            rows_of = weight[here[0] ^ shift]
            product = lax.dot_general(
                rows_of.reshape(-1, rows_of.shape[-1]),
                active[...],
                (((1,), (1,)), ((), ())),
                preferred_element_type=jnp.float32,
            )
            add_planes(inputs[shift], product, outputs[shift])


def backward_kernel(
    here, own, row_low, row_high, plane_low, plane_high, taps, mine, other, *rest
):
    count = (len(rest) - 4) // 2
    inputs, outputs = rest[:count], rest[count : 2 * count]
    padded, grads, weight, sems = rest[2 * count :]
    step = pl.program_id(0)
    planes, rows, extent = own.shape[:3]
    copies = piece_copies(here, mine, other, weight, sems)

    @pl.when(step == 0)
    def _():
        start_all(copies)

    fill_padded(padded, own, row_low, row_high, plane_low, plane_high)
    lanes = pl.ds(pl.multiple_of(step * LANES, LANES), LANES)
    for z in range(planes):
        for y in range(rows):
            at = (z * rows + y) * extent
            total = stencil_row(padded, taps, z, y, True)
            grads[at : at + extent, lanes] = total.astype(grads.dtype)

    @pl.when(step == pl.num_programs(0) - 1)
    def _():
        wait_all(copies)
        channels = grads.shape[1]
        width = inputs[0].shape[1]
        for shift in range(count):
            start = pl.multiple_of((here[0] ^ shift) * width, width)
            columns = weight[:, :, :, pl.ds(start, width)].reshape(channels, width)
            product = jnp.dot(grads[...], columns, preferred_element_type=jnp.float32)
            add_planes(inputs[shift], product.T, outputs[shift])


def weight_scratch(mine):
    turns, parts, share, channels = mine.shape
    return [
        pltpu.VMEM((parts, 2 * turns, share, channels), mine.dtype),
        pltpu.SemaphoreType.DMA((parts, 2 * turns)),
    ]


def stencil(here, own, halo, taps, weight, blocks, forward):
    planes, rows, extent, channels = own.shape
    cells = planes * rows * extent
    per_table = taps.shape[2] // LANES

    def block(*lead):
        zeros = (0,) * len(lead)
        return pl.BlockSpec(lead + (LANES,), lambda c, here: zeros + (c,))

    def resident(shape):
        return pl.BlockSpec(shape, lambda c, here: (0,) * len(shape), pipeline_mode=pl.Buffered(1))

    def table_at(c, here):
        away = (c // per_table) ^ here[0]
        slot = 0
        for place, distance in enumerate(distances(taps.shape[0])):
            slot = jnp.where(away == distance, place, slot)
        return slot, 0, c % per_table

    anywhere = pl.BlockSpec(memory_space=pltpu.HBM)
    in_specs = [
        block(planes, rows, extent),
        block(planes, extent),
        block(planes, extent),
        block(rows + 2, extent),
        block(rows + 2, extent),
        pl.BlockSpec((1, 28, LANES), table_at),
        anywhere,
        anywhere,
    ]
    in_specs += [resident(piece.shape) for piece in blocks]
    out_specs = [resident(piece.shape) for piece in blocks]
    out_shape = [jax.ShapeDtypeStruct(piece.shape, piece.dtype) for piece in blocks]
    if forward:
        out_specs.append(block(planes, rows, extent))
        out_shape.append(jax.ShapeDtypeStruct(own.shape, jnp.float32))
    return pl.pallas_call(
        forward_kernel if forward else backward_kernel,
        grid_spec=pltpu.PrefetchScalarGridSpec(
            num_scalar_prefetch=1,
            grid=(channels // LANES,),
            in_specs=in_specs,
            out_specs=out_specs,
            scratch_shapes=[
                pltpu.VMEM((planes + 2, rows + 2, extent, LANES), jnp.float32),
                pltpu.VMEM((cells, channels), own.dtype),
                *weight_scratch(weight[0]),
            ],
        ),
        out_shape=out_shape,
    )(here, own, *halo, taps, *weight, *blocks)


def turn_blocks(here, inputs, turned):
    planes, own, width = inputs[0].shape
    for shift, block in enumerate(inputs):
        start = pl.multiple_of((here[0] ^ shift) * own, own)
        for z in range(planes):
            turned[z * width : (z + 1) * width, pl.ds(start, own)] = block[z].T


def put_with_edges(value, out, first, last, fore, back):
    out[...] = value
    planes, extent, width = first.shape
    plane = value.shape[0] // planes
    rows = plane // extent
    for z in range(planes):
        first[z] = value[z * plane : z * plane + extent]
        last[z] = value[(z + 1) * plane - extent : (z + 1) * plane]
    for edge, z in ((back, 0), (fore, planes - 1)):
        edge[0] = jnp.zeros((extent, width), edge.dtype)
        edge[rows + 1] = jnp.zeros((extent, width), edge.dtype)
        for y in range(rows):
            at = z * plane + y * extent
            edge[y + 1] = value[at : at + extent]


def hidden_kernel(here, mine, other, *rest, count):
    inputs, (*outputs, turned, weight, sems) = rest[:count], rest[count:]

    @pl.when(pl.program_id(0) == 0)
    def _():
        start_all(piece_copies(here, mine, other, weight, sems))
        turn_blocks(here, inputs, turned)

    wait_block(pl.program_id(0), mine, other, weight, sems)
    rows_of = weight[pl.program_id(0)]
    value = lax.dot_general(
        turned[...],
        rows_of.reshape(-1, rows_of.shape[-1]),
        (((1,), (1,)), ((), ())),
        preferred_element_type=jnp.float32,
    )
    put_with_edges(value.astype(turned.dtype), *outputs)


def mix_kernel(here, mine, other, *rest, count):
    inputs, (slope, *outputs, turned, weight, sems) = rest[:count], rest[count:]

    @pl.when(pl.program_id(0) == 0)
    def _():
        copies = piece_copies(here, mine, other, weight, sems)
        start_all(copies)
        turn_blocks(here, inputs, turned)
        wait_all(copies)

    channels, width = turned.shape[1], slope.shape[1]
    start = pl.multiple_of(pl.program_id(0) * width, width)
    columns = weight[:, :, :, pl.ds(start, width)].reshape(channels, width)
    grad = jnp.dot(turned[...], columns, preferred_element_type=jnp.float32)
    grad = grad.astype(turned.dtype).astype(jnp.float32)
    put_with_edges((grad * slope[...]).astype(turned.dtype), *outputs)


def product_call(here, blocks, weight, slope=None):
    planes, own, width = blocks[0].shape
    cells = planes * width
    count = len(blocks)
    channels = own * count
    dtype = blocks[0].dtype
    columns = pl.BlockSpec((cells, own), lambda c, here: (0, c))
    room = width // CX + 2
    row = pl.BlockSpec((planes, CX, own), lambda c, here: (0, 0, c))
    plane = pl.BlockSpec((room, CX, own), lambda c, here: (0, 0, c))
    whole = pl.BlockSpec(
        blocks[0].shape, lambda c, here: (0, 0, 0), pipeline_mode=pl.Buffered(1)
    )
    anywhere = pl.BlockSpec(memory_space=pltpu.HBM)
    kernel, extra = (hidden_kernel, []) if slope is None else (mix_kernel, [slope])
    row_shape = jax.ShapeDtypeStruct((planes, CX, channels), dtype)
    plane_shape = jax.ShapeDtypeStruct((room, CX, channels), dtype)
    return pl.pallas_call(
        lambda *refs: kernel(*refs, count=count),
        grid_spec=pltpu.PrefetchScalarGridSpec(
            num_scalar_prefetch=1,
            grid=(count,),
            in_specs=[anywhere] * 2 + [whole] * count + [columns] * len(extra),
            out_specs=[columns, row, row, plane, plane],
            scratch_shapes=[pltpu.VMEM((cells, channels), dtype), *weight_scratch(weight[0])],
        ),
        out_shape=[
            jax.ShapeDtypeStruct((cells, channels), dtype),
            row_shape,
            row_shape,
            plane_shape,
            plane_shape,
        ],
    )(here, *weight, *blocks, *extra)


def shift_pairs(axis):
    count = lax.axis_size(axis)
    forward = [(i, i + 1) for i in range(count - 1)]
    return forward, [(target, source) for source, target in forward]


def split_cells_body(volume, out_grad, weight_in, weight_out, filter_taps, filter_bias):
    own, planes, cells = volume.shape
    parts = lax.axis_size("chan")
    rows = CY // parts
    width = rows * CX
    channels = own * parts
    others = ("groups", "space")
    seat = lax.axis_index(others)
    chan = lax.axis_index("chan")
    share = own // lax.axis_size(others)
    here = jnp.stack([chan, seat]).astype(jnp.int32)
    shifts = sorted(range(1, parts), key=lambda shift: (shift & (parts // 2) == 0, shift))

    def swap(part, axes, partner):
        count = lax.axis_size(axes)
        return lax.ppermute(part, axes, [(i, partner(i)) for i in range(count)])

    def exchange(blocks):
        got = {0: blocks[0]}
        for shift in shifts:
            got[shift] = swap(blocks[shift], "chan", lambda i: i ^ shift)
        return [got[shift] for shift in range(parts)]

    def cut(field, order, place):
        pieces = {}
        for shift in order:
            start = (place ^ shift) * width
            piece = lax.dynamic_slice_in_dim(field, start, width, axis=2).transpose(1, 0, 2)
            pieces[shift], place = lax.optimization_barrier((piece, place))
        return pieces

    def paste(pieces):
        field = jnp.zeros((own, planes, cells), pieces[0].dtype)
        for shift in [0] + shifts:
            piece = pieces[shift].transpose(1, 0, 2)
            field = lax.dynamic_update_slice_in_dim(field, piece, (chan ^ shift) * width, axis=2)
        return field

    def gather_column(piece):
        column = piece[None]
        for mask in doubling(parts):
            got = swap(column, "chan", lambda i: i ^ mask)
            column = jnp.concatenate([column, got])
        return column

    def gather_weight(column, beside=None):
        over_x = swap(column, others, lambda i: i ^ 2)
        over_y = swap(column, others, lambda i: i ^ 4)
        mixed = jnp.where(seat & 1 == 0, over_y, over_x)
        mixed, beside = lax.optimization_barrier((mixed, beside))
        far = swap(mixed, others, lambda i: i ^ (4 if i & 1 else 2))
        mine = jnp.stack([column, over_x, over_y, far])
        return (mine, swap(mine, others, lambda i: i ^ 1)), beside

    def halo_of(first, last, fore, back):
        forward, backward = shift_pairs("chan")
        row_low = lax.ppermute(last, "chan", forward)
        row_high = lax.ppermute(first, "chan", backward)
        forward, backward = shift_pairs("space")

        def joined(plane, z):
            plane = lax.dynamic_update_slice_in_dim(plane, row_low[z][None], 0, axis=0)
            return lax.dynamic_update_slice_in_dim(plane, row_high[z][None], rows + 1, axis=0)

        plane_low = lax.ppermute(joined(fore, planes - 1), "space", forward)
        plane_high = lax.ppermute(joined(back, 0), "space", backward)
        return row_low, row_high, plane_low, plane_high

    grid = (planes, rows, CX, channels)
    piece_in, piece_out = (
        lax.dynamic_slice_in_dim(weight, seat * share, share, axis=0)
        for weight in (weight_in, weight_out)
    )
    column = gather_column(piece_in)
    vol_cut = cut(volume, shifts, chan)
    later, column = lax.optimization_barrier((chan, column))
    own_cut = cut(volume, [0], later)
    grad_cut = cut(out_grad, shifts + [0], later)
    full_in, (own_block, here, grad_cut) = gather_weight(column, (own_cut[0], here, grad_cut))
    full_out, _ = gather_weight(gather_column(piece_out))
    table = jnp.concatenate([filter_taps, filter_bias[:, None]], axis=1).T
    taps = gather_column(table)
    own_block, taps = lax.optimization_barrier((own_block, taps))
    vol_blocks = exchange({**vol_cut, 0: own_block})
    grad_blocks = exchange(grad_cut)
    hidden, *edges = product_call(here, vol_blocks, full_in)
    halo = halo_of(*edges)
    *out_blocks, slope = stencil(here, hidden.reshape(grid), halo, taps, full_out, vol_blocks, True)
    out_found = exchange(out_blocks)
    mix_grad, *edges = product_call(
        here, grad_blocks, full_out, slope.reshape(planes * width, channels)
    )
    halo = halo_of(*edges)
    back_blocks = list(
        stencil(here, mix_grad.reshape(grid), halo, taps, full_in, grad_blocks, False)
    )
    out_found, back_blocks[0] = lax.optimization_barrier((out_found, back_blocks[0]))
    block_out = paste(out_found)
    volume_grad = paste(exchange(back_blocks))
    return block_out, volume_grad


def with_halo(block, axis, dim):
    forward, backward = shift_pairs(axis)
    low = lax.ppermute(lax.slice_in_dim(block, block.shape[dim] - 1, None, axis=dim), axis, forward)
    high = lax.ppermute(lax.slice_in_dim(block, 0, 1, axis=dim), axis, backward)
    return jnp.concatenate([low, block, high], axis=dim)


def core(padded, filter_taps, direction):
    extent_z = padded.shape[1] - 2
    extent_y = padded.shape[2] - 2
    extent_x = padded.shape[3] - 2
    summed = jnp.zeros((padded.shape[0], extent_z, extent_y, extent_x), jnp.float32)
    for shift_z in range(3):
        for shift_y in range(3):
            for shift_x in range(3):
                tap_index = (shift_z * 3 + shift_y) * 3 + shift_x
                begin_z = 1 + direction * (shift_z - 1)
                begin_y = 1 + direction * (shift_y - 1)
                begin_x = 1 + direction * (shift_x - 1)
                window = padded[
                    :,
                    begin_z : begin_z + extent_z,
                    begin_y : begin_y + extent_y,
                    begin_x : begin_x + extent_x,
                ]
                summed = summed + filter_taps[:, tap_index][:, None, None, None] * window
    return summed


def lift(field_z):
    extended = field_z.astype(jnp.float32).reshape(field_z.shape[0], field_z.shape[1], CY, CX)
    return jnp.pad(extended, ((0, 0), (0, 0), (1, 1), (1, 1)))


def exchange_body(volume, out_grad, weight_in, weight_out, filter_taps, filter_bias):
    slab_shape = volume.shape
    contract_first = (((0,), (0,)), ((), ()))

    def to_cells(field):
        return lax.all_to_all(
            field.reshape(field.shape[0], -1), "chan", split_axis=1, concat_axis=0, tiled=True
        )

    def to_channels(field):
        return lax.all_to_all(field, "chan", split_axis=0, concat_axis=1, tiled=True).reshape(
            slab_shape
        )

    full_in = lax.all_gather(weight_in, "chan", axis=0, tiled=True)
    full_out = lax.all_gather(weight_out, "chan", axis=0, tiled=True)
    vol_cells = to_cells(volume)
    hidden = to_channels(
        jnp.dot(full_in, vol_cells, preferred_element_type=jnp.float32).astype(jnp.bfloat16)
    )
    padded = lift(with_halo(hidden, "space", 1))
    mixed = core(padded, filter_taps, 1) + filter_bias[:, None, None, None]
    active = gelu_value(mixed).astype(jnp.bfloat16).reshape(slab_shape)
    out_cells = vol_cells.astype(jnp.float32) + jnp.dot(
        full_out, to_cells(active), preferred_element_type=jnp.float32
    )
    block_out = to_channels(out_cells.astype(jnp.bfloat16))
    grad_cells = to_cells(out_grad)
    act_part = lax.dot_general(
        full_out, grad_cells, contract_first, preferred_element_type=jnp.float32
    )
    act_grad = to_channels(act_part.astype(jnp.bfloat16))
    slope = gelu_slope(mixed)
    mix_grad = (
        (act_grad.astype(jnp.float32).reshape(slope.shape) * slope)
        .astype(jnp.bfloat16)
        .reshape(slab_shape)
    )
    padded_grad = lift(with_halo(mix_grad, "space", 1))
    hid_grad = core(padded_grad, filter_taps, -1).astype(jnp.bfloat16).reshape(slab_shape)
    back_part = lax.dot_general(
        full_in, to_cells(hid_grad), contract_first, preferred_element_type=jnp.float32
    )
    volume_grad = to_channels((grad_cells.astype(jnp.float32) + back_part).astype(jnp.bfloat16))
    return block_out, volume_grad


def body(volume, out_grad, weight_in, weight_out, filter_taps, filter_bias):
    own = volume.shape[0]
    parts = lax.axis_size("chan")
    groups, space = lax.axis_size("groups"), lax.axis_size("space")
    whole_rows = CY % parts == 0 and (CY // parts * CX) % LANES == 0 and parts & (parts - 1) == 0
    whole_shares = own % LANES == 0 and own % (16 * groups * space) == 0
    split = whole_rows and whole_shares and (groups, space) == (2, 4)
    chosen = split_cells_body if split else exchange_body
    return chosen(volume, out_grad, weight_in, weight_out, filter_taps, filter_bias)


def solution(mesh):
    field = P(("groups", "chan"), "space", None)
    placed = (field, field, P("chan", None), P("chan", None), P("chan", None), P("chan"))
    return jax.shard_map(
        body,
        mesh=mesh,
        in_specs=placed,
        out_specs=(field, field),
        check_vma=False,
    )
```

```python
import jax
import jax.numpy as jnp
from jax import lax
from jax.experimental import pallas as pl
from jax.experimental.pallas import tpu as pltpu
from jax.sharding import PartitionSpec as P

CX = 32
CY = 16
LANES = 128


root_half = 0.7071067811865476
inv_root_two_pi = 0.3989422804014327


def gelu_value(field):
    return 0.5 * field * (1.0 + lax.erf(field * root_half))


def gelu_slope(field):
    return (
        0.5 * (1.0 + lax.erf(field * root_half))
        + field * jnp.exp(-0.5 * field * field) * inv_root_two_pi
    )


def fill_padded(padded, own, row_low, row_high, plane_low, plane_high):
    planes, rows = own.shape[0], own.shape[1]
    for z in range(planes):
        padded[z + 1, 0] = row_low[z].astype(jnp.float32)
        padded[z + 1, rows + 1] = row_high[z].astype(jnp.float32)
        for y in range(rows):
            padded[z + 1, y + 1] = own[z, y].astype(jnp.float32)
    for y in range(rows + 2):
        padded[0, y] = plane_low[y].astype(jnp.float32)
        padded[planes + 1, y] = plane_high[y].astype(jnp.float32)


def stencil_row(padded, taps, z, y, flip):
    sums = [None, None, None]
    for a in range(3):
        for b in range(3):
            row = padded[z + a, y + b]
            for e in range(3):
                index = (a * 3 + b) * 3 + e
                tap = taps[0, 26 - index if flip else index]
                term = row * tap[None, :]
                sums[e] = term if sums[e] is None else sums[e] + term
    x = lax.broadcasted_iota(jnp.int32, sums[0].shape, 0)
    extent = sums[0].shape[0]
    before = jnp.where(x == 0, 0.0, pltpu.roll(sums[0], 1, 0))
    after = jnp.where(x == extent - 1, 0.0, pltpu.roll(sums[2], extent - 1, 0))
    return sums[1] + (before + after)


def doubling(count):
    masks = []
    while count > 1:
        masks.append(count - 1)
        count //= 2
    return masks


def distances(count):
    found = [0]
    for mask in doubling(count):
        found += [mask ^ distance for distance in found]
    return found


def slot_of(distance, count):
    slot = 0
    for place, held in enumerate(distances(count)):
        slot = jnp.where(distance == held, place, slot)
    return slot


def piece_copies(here, mine, other, full, sems, blocks, columns=None):
    chan, seat = here[0], here[1]
    copies = []
    for index, block in enumerate(blocks):
        slot = slot_of(chan ^ block, mine.shape[1])
        for side, pieces in enumerate((mine, other)):
            for turn in range(pieces.shape[0]):
                source = pieces.at[turn, slot]
                if columns is not None:
                    source = source.at[:, columns]
                copies.append(
                    pltpu.make_async_copy(
                        source,
                        full.at[index, seat ^ side ^ (2 * turn)],
                        sems.at[index, 2 * turn + side],
                    )
                )
    return copies


def start_all(copies):
    for copy in copies:
        copy.start()


def wait_all(copies):
    for copy in copies:
        copy.wait()


def add_planes(base, product, out):
    planes, _, width = base.shape
    for z in range(planes):
        total = base[z].astype(jnp.float32) + product[:, z * width : (z + 1) * width]
        out[z] = total.astype(out.dtype)


def forward_cells(fields, taps, padded, active, lanes, slope):
    planes, rows, extent = fields[0].shape[:3]
    fill_padded(padded, *fields)
    for z in range(planes):
        for y in range(rows):
            mixed = stencil_row(padded, taps, z, y, False) + taps[0, 27][None, :]
            half = 0.5 * (1.0 + lax.erf(mixed * root_half))
            at = (z * rows + y) * extent
            active[at : at + extent, lanes] = (mixed * half).astype(active.dtype)
            slope[z, y] = half + mixed * jnp.exp(-0.5 * mixed * mixed) * inv_root_two_pi


def backward_cells(fields, taps, padded, grads, lanes):
    planes, rows, extent = fields[0].shape[:3]
    fill_padded(padded, *fields)
    for z in range(planes):
        for y in range(rows):
            at = (z * rows + y) * extent
            total = stencil_row(padded, taps, z, y, True)
            grads[at : at + extent, lanes] = total.astype(grads.dtype)


def lane_block():
    return pl.ds(pl.multiple_of(pl.program_id(0) * LANES, LANES), LANES)


def forward_first(here, *refs):
    fields, (taps, active, slope, padded) = refs[:5], refs[5:]
    forward_cells(fields, taps, padded, active, slice(None), slope)


def backward_first(here, *refs):
    fields, (taps, grads, padded) = refs[:5], refs[5:]
    backward_cells(fields, taps, padded, grads, slice(None))


def forward_last(here, *refs, count):
    fields, (taps, mine, other, before) = refs[:5], refs[5:9]
    inputs, outputs = refs[9 : 9 + count], refs[9 + count : 9 + 2 * count]
    slope, padded, active, weight, sems = refs[9 + 2 * count :]
    step = pl.program_id(0)

    @pl.when(step == 0)
    def _():
        start_all(piece_copies(here, mine, other, weight, sems, range(count)))

    forward_cells(fields, taps, padded, active, lane_block(), slope)

    @pl.when(step == pl.num_programs(0) - 1)
    def _():
        wait_all(piece_copies(here, mine, other, weight, sems, range(count)))
        half = active.shape[1]
        for shift in range(count):
            rows_of = weight[here[0] ^ shift]
            rows_of = rows_of.reshape(-1, rows_of.shape[-1])
            product = sum(
                lax.dot_general(
                    rows_of[:, part * half : (part + 1) * half],
                    field[...],
                    (((1,), (1,)), ((), ())),
                    preferred_element_type=jnp.float32,
                )
                for part, field in enumerate((before, active))
            )
            add_planes(inputs[shift], product, outputs[shift])


def backward_last(here, *refs, count):
    fields, (taps, mine, other, before) = refs[:5], refs[5:9]
    inputs, outputs = refs[9 : 9 + count], refs[9 + count : 9 + 2 * count]
    padded, grads, weight, sems = refs[9 + 2 * count :]
    step = pl.program_id(0)

    @pl.when(step == 0)
    def _():
        start_all(piece_copies(here, mine, other, weight, sems, range(count)))

    backward_cells(fields, taps, padded, grads, lane_block())

    @pl.when(step == pl.num_programs(0) - 1)
    def _():
        wait_all(piece_copies(here, mine, other, weight, sems, range(count)))
        half = grads.shape[1]
        width = inputs[0].shape[1]
        for shift in range(count):
            start = pl.multiple_of((here[0] ^ shift) * width, width)
            columns = weight[:, :, :, pl.ds(start, width)].reshape(2 * half, width)
            product = sum(
                jnp.dot(
                    field[...],
                    columns[part * half : (part + 1) * half],
                    preferred_element_type=jnp.float32,
                )
                for part, field in enumerate((before, grads))
            )
            add_planes(inputs[shift], product.T, outputs[shift])


def weight_scratch(mine, blocks, columns):
    turns, _, share, _ = mine.shape
    return [
        pltpu.VMEM((blocks, 2 * turns, share, columns), mine.dtype),
        pltpu.SemaphoreType.DMA((blocks, 2 * turns)),
    ]


def stencil(here, own, halo, taps, part, forward, last=None):
    planes, rows, extent, channels = own.shape
    cells = planes * rows * extent
    per_table = taps.shape[2] // LANES
    steps = channels // LANES

    def block(*lead):
        zeros = (0,) * len(lead)
        return pl.BlockSpec(lead + (LANES,), lambda c, here: zeros + (c,))

    def resident(shape):
        return pl.BlockSpec(shape, lambda c, here: (0,) * len(shape), pipeline_mode=pl.Buffered(1))

    def table_at(c, here):
        away = ((part * steps + c) // per_table) ^ here[0]
        return slot_of(away, taps.shape[0]), 0, (part * steps + c) % per_table

    in_specs = [
        block(planes, rows, extent),
        block(planes, extent),
        block(planes, extent),
        block(rows + 2, extent),
        block(rows + 2, extent),
        pl.BlockSpec((1, 28, LANES), table_at),
    ]
    args = [own, *halo, taps]
    scratch = [pltpu.VMEM((planes + 2, rows + 2, extent, LANES), jnp.float32)]
    slope_spec = [block(planes, rows, extent)] if forward else []
    slope_shape = [jax.ShapeDtypeStruct(own.shape, jnp.float32)] if forward else []
    if last is None:
        kernel = forward_first if forward else backward_first
        out_specs = [block(cells)] + slope_spec
        out_shape = [jax.ShapeDtypeStruct((cells, channels), own.dtype)] + slope_shape
    else:
        weight, before, blocks = last
        body_of = forward_last if forward else backward_last

        def kernel(*refs):
            body_of(*refs, count=len(blocks))

        anywhere = pl.BlockSpec(memory_space=pltpu.HBM)
        in_specs += [anywhere, anywhere, resident(before.shape)]
        in_specs += [resident(piece.shape) for piece in blocks]
        args += [*weight, before, *blocks]
        out_specs = [resident(piece.shape) for piece in blocks] + slope_spec
        out_shape = [jax.ShapeDtypeStruct(piece.shape, piece.dtype) for piece in blocks]
        out_shape += slope_shape
        scratch.append(pltpu.VMEM((cells, channels), own.dtype))
        scratch += weight_scratch(weight[0], len(blocks), weight[0].shape[3])
    return pl.pallas_call(
        kernel,
        grid_spec=pltpu.PrefetchScalarGridSpec(
            num_scalar_prefetch=1,
            grid=(steps,),
            in_specs=in_specs,
            out_specs=out_specs,
            scratch_shapes=scratch,
        ),
        out_shape=out_shape,
    )(here, *args)


def turn_blocks(here, inputs, turned):
    planes, own, width = inputs[0].shape
    for shift, block in enumerate(inputs):
        start = pl.multiple_of((here[0] ^ shift) * own, own)
        for z in range(planes):
            turned[z * width : (z + 1) * width, pl.ds(start, own)] = block[z].T


def put_with_edges(value, out, first, last, fore, back):
    out[...] = value
    planes, extent, width = first.shape
    plane = value.shape[0] // planes
    rows = plane // extent
    for z in range(planes):
        first[z] = value[z * plane : z * plane + extent]
        last[z] = value[(z + 1) * plane - extent : (z + 1) * plane]
    for edge, z in ((back, 0), (fore, planes - 1)):
        edge[0] = jnp.zeros((extent, width), edge.dtype)
        edge[rows + 1] = jnp.zeros((extent, width), edge.dtype)
        for y in range(rows):
            at = z * plane + y * extent
            edge[y + 1] = value[at : at + extent]


def hidden_kernel(here, mine, other, *rest, count, part):
    inputs, (*outputs, turned, weight, sems) = rest[:count], rest[count:]
    half = count // 2
    copies = piece_copies(
        here, mine, other, weight, sems, range(part * half, (part + 1) * half)
    )

    @pl.when(pl.program_id(0) == 0)
    def _():
        start_all(copies)
        turn_blocks(here, inputs, turned)
        wait_all(copies)

    rows_of = weight[pl.program_id(0)]
    value = lax.dot_general(
        turned[...],
        rows_of.reshape(-1, rows_of.shape[-1]),
        (((1,), (1,)), ((), ())),
        preferred_element_type=jnp.float32,
    )
    put_with_edges(value.astype(turned.dtype), *outputs)


def mix_kernel(here, mine, other, *rest, count, part):
    inputs, (slope, *outputs, turned, weight, sems) = rest[:count], rest[count:]
    channels, width = turned.shape[1], slope.shape[1]
    half = channels // 2

    @pl.when(pl.program_id(0) == 0)
    def _():
        columns = slice(part * half, (part + 1) * half)
        copies = piece_copies(here, mine, other, weight, sems, range(count), columns)
        start_all(copies)
        turn_blocks(here, inputs, turned)
        wait_all(copies)

    start = pl.multiple_of(pl.program_id(0) * width, width)
    columns = weight[:, :, :, pl.ds(start, width)].reshape(channels, width)
    grad = jnp.dot(turned[...], columns, preferred_element_type=jnp.float32)
    grad = grad.astype(turned.dtype).astype(jnp.float32)
    put_with_edges((grad * slope[...]).astype(turned.dtype), *outputs)


def product_call(here, blocks, weight, part, slope=None):
    planes, own, width = blocks[0].shape
    cells = planes * width
    count = len(blocks)
    channels = own * count
    half = channels // 2
    dtype = blocks[0].dtype
    columns = pl.BlockSpec((cells, own), lambda c, here: (0, c))
    room = width // CX + 2
    row = pl.BlockSpec((planes, CX, own), lambda c, here: (0, 0, c))
    plane = pl.BlockSpec((room, CX, own), lambda c, here: (0, 0, c))
    whole = pl.BlockSpec(
        blocks[0].shape, lambda c, here: (0, 0, 0), pipeline_mode=pl.Buffered(1)
    )
    anywhere = pl.BlockSpec(memory_space=pltpu.HBM)
    if slope is None:
        kernel, extra = hidden_kernel, []
        scratch = weight_scratch(weight[0], count // 2, channels)
    else:
        kernel, extra = mix_kernel, [slope]
        scratch = weight_scratch(weight[0], count, half)
    row_shape = jax.ShapeDtypeStruct((planes, CX, half), dtype)
    plane_shape = jax.ShapeDtypeStruct((room, CX, half), dtype)
    return pl.pallas_call(
        lambda *refs: kernel(*refs, count=count, part=part),
        grid_spec=pltpu.PrefetchScalarGridSpec(
            num_scalar_prefetch=1,
            grid=(count // 2,),
            in_specs=[anywhere] * 2 + [whole] * count + [columns] * len(extra),
            out_specs=[columns, row, row, plane, plane],
            scratch_shapes=[pltpu.VMEM((cells, channels), dtype), *scratch],
        ),
        out_shape=[
            jax.ShapeDtypeStruct((cells, half), dtype),
            row_shape,
            row_shape,
            plane_shape,
            plane_shape,
        ],
    )(here, *weight, *blocks, *extra)


def shift_pairs(axis):
    count = lax.axis_size(axis)
    forward = [(i, i + 1) for i in range(count - 1)]
    return forward, [(target, source) for source, target in forward]


def split_cells_body(volume, out_grad, weight_in, weight_out, filter_taps, filter_bias):
    own, planes, cells = volume.shape
    parts = lax.axis_size("chan")
    rows = CY // parts
    width = rows * CX
    channels = own * parts
    others = ("groups", "space")
    seat = lax.axis_index(others)
    chan = lax.axis_index("chan")
    share = own // lax.axis_size(others)
    here = jnp.stack([chan, seat]).astype(jnp.int32)
    shifts = sorted(range(1, parts), key=lambda shift: (shift & (parts // 2) == 0, shift))

    def swap(part, axes, partner):
        count = lax.axis_size(axes)
        return lax.ppermute(part, axes, [(i, partner(i)) for i in range(count)])

    def exchange(blocks):
        got = {0: blocks[0]}
        for shift in shifts:
            got[shift] = swap(blocks[shift], "chan", lambda i: i ^ shift)
        return [got[shift] for shift in range(parts)]

    def cut(field, order, place):
        pieces = {}
        for shift in order:
            start = (place ^ shift) * width
            piece = lax.dynamic_slice_in_dim(field, start, width, axis=2).transpose(1, 0, 2)
            pieces[shift], place = lax.optimization_barrier((piece, place))
        return pieces

    def paste(pieces):
        field = jnp.zeros((own, planes, cells), pieces[0].dtype)
        for shift in [0] + shifts:
            piece = pieces[shift].transpose(1, 0, 2)
            field = lax.dynamic_update_slice_in_dim(field, piece, (chan ^ shift) * width, axis=2)
        return field

    def gather_column(piece):
        column = piece[None]
        for mask in doubling(parts):
            got = swap(column, "chan", lambda i: i ^ mask)
            column = jnp.concatenate([column, got])
        return column

    def gather_weight(column, beside=None):
        over_x = swap(column, others, lambda i: i ^ 2)
        over_y = swap(column, others, lambda i: i ^ 4)
        mixed = jnp.where(seat & 1 == 0, over_y, over_x)
        mixed, beside = lax.optimization_barrier((mixed, beside))
        far = swap(mixed, others, lambda i: i ^ (4 if i & 1 else 2))
        mine = jnp.stack([column, over_x, over_y, far])
        return (mine, swap(mine, others, lambda i: i ^ 1)), beside

    def halo_of(first, last, fore, back):
        forward, backward = shift_pairs("chan")
        row_low = lax.ppermute(last, "chan", forward)
        row_high = lax.ppermute(first, "chan", backward)
        forward, backward = shift_pairs("space")

        def joined(plane, z):
            plane = lax.dynamic_update_slice_in_dim(plane, row_low[z][None], 0, axis=0)
            return lax.dynamic_update_slice_in_dim(plane, row_high[z][None], rows + 1, axis=0)

        plane_low = lax.ppermute(joined(fore, planes - 1), "space", forward)
        plane_high = lax.ppermute(joined(back, 0), "space", backward)
        return row_low, row_high, plane_low, plane_high

    piece_in, piece_out = (
        lax.dynamic_slice_in_dim(weight, seat * share, share, axis=0)
        for weight in (weight_in, weight_out)
    )
    column = gather_column(piece_in)
    vol_cut = cut(volume, shifts, chan)
    later, column = lax.optimization_barrier((chan, column))
    own_cut = cut(volume, [0], later)
    grad_cut = cut(out_grad, shifts + [0], later)
    full_in, (own_block, here, grad_cut) = gather_weight(column, (own_cut[0], here, grad_cut))
    full_out, _ = gather_weight(gather_column(piece_out))
    table = jnp.concatenate([filter_taps, filter_bias[:, None]], axis=1).T
    taps = gather_column(table)
    own_block, taps = lax.optimization_barrier((own_block, taps))
    vol_blocks = exchange({**vol_cut, 0: own_block})
    grad_blocks = exchange(grad_cut)
    halves = range(2)
    grid = (planes, rows, CX, channels // 2)
    hidden, halos = [], []
    for part in halves:
        field, *edges = product_call(here, vol_blocks, full_in, part)
        hidden.append(field.reshape(grid))
        halos.append(halo_of(*edges))
    active, slope0 = stencil(here, hidden[0], halos[0], taps, 0, True)
    *out_blocks, slope1 = stencil(
        here, hidden[1], halos[1], taps, 1, True, (full_out, active, vol_blocks)
    )
    out_found = exchange(out_blocks)
    mixed, halos = [], []
    for part, slope in enumerate((slope0, slope1)):
        field, *edges = product_call(
            here, grad_blocks, full_out, part, slope.reshape(planes * width, channels // 2)
        )
        mixed.append(field.reshape(grid))
        halos.append(halo_of(*edges))
    (grads,) = stencil(here, mixed[0], halos[0], taps, 0, False)
    back_blocks = list(
        stencil(here, mixed[1], halos[1], taps, 1, False, (full_in, grads, grad_blocks))
    )
    out_found, back_blocks[0] = lax.optimization_barrier((out_found, back_blocks[0]))
    block_out = paste(out_found)
    volume_grad = paste(exchange(back_blocks))
    return block_out, volume_grad


def with_halo(block, axis, dim):
    forward, backward = shift_pairs(axis)
    low = lax.ppermute(lax.slice_in_dim(block, block.shape[dim] - 1, None, axis=dim), axis, forward)
    high = lax.ppermute(lax.slice_in_dim(block, 0, 1, axis=dim), axis, backward)
    return jnp.concatenate([low, block, high], axis=dim)


def core(padded, filter_taps, direction):
    extent_z = padded.shape[1] - 2
    extent_y = padded.shape[2] - 2
    extent_x = padded.shape[3] - 2
    summed = jnp.zeros((padded.shape[0], extent_z, extent_y, extent_x), jnp.float32)
    for shift_z in range(3):
        for shift_y in range(3):
            for shift_x in range(3):
                tap_index = (shift_z * 3 + shift_y) * 3 + shift_x
                begin_z = 1 + direction * (shift_z - 1)
                begin_y = 1 + direction * (shift_y - 1)
                begin_x = 1 + direction * (shift_x - 1)
                window = padded[
                    :,
                    begin_z : begin_z + extent_z,
                    begin_y : begin_y + extent_y,
                    begin_x : begin_x + extent_x,
                ]
                summed = summed + filter_taps[:, tap_index][:, None, None, None] * window
    return summed


def lift(field_z):
    extended = field_z.astype(jnp.float32).reshape(field_z.shape[0], field_z.shape[1], CY, CX)
    return jnp.pad(extended, ((0, 0), (0, 0), (1, 1), (1, 1)))


def exchange_body(volume, out_grad, weight_in, weight_out, filter_taps, filter_bias):
    slab_shape = volume.shape
    contract_first = (((0,), (0,)), ((), ()))

    def to_cells(field):
        return lax.all_to_all(
            field.reshape(field.shape[0], -1), "chan", split_axis=1, concat_axis=0, tiled=True
        )

    def to_channels(field):
        return lax.all_to_all(field, "chan", split_axis=0, concat_axis=1, tiled=True).reshape(
            slab_shape
        )

    full_in = lax.all_gather(weight_in, "chan", axis=0, tiled=True)
    full_out = lax.all_gather(weight_out, "chan", axis=0, tiled=True)
    vol_cells = to_cells(volume)
    hidden = to_channels(
        jnp.dot(full_in, vol_cells, preferred_element_type=jnp.float32).astype(jnp.bfloat16)
    )
    padded = lift(with_halo(hidden, "space", 1))
    mixed = core(padded, filter_taps, 1) + filter_bias[:, None, None, None]
    active = gelu_value(mixed).astype(jnp.bfloat16).reshape(slab_shape)
    out_cells = vol_cells.astype(jnp.float32) + jnp.dot(
        full_out, to_cells(active), preferred_element_type=jnp.float32
    )
    block_out = to_channels(out_cells.astype(jnp.bfloat16))
    grad_cells = to_cells(out_grad)
    act_part = lax.dot_general(
        full_out, grad_cells, contract_first, preferred_element_type=jnp.float32
    )
    act_grad = to_channels(act_part.astype(jnp.bfloat16))
    slope = gelu_slope(mixed)
    mix_grad = (
        (act_grad.astype(jnp.float32).reshape(slope.shape) * slope)
        .astype(jnp.bfloat16)
        .reshape(slab_shape)
    )
    padded_grad = lift(with_halo(mix_grad, "space", 1))
    hid_grad = core(padded_grad, filter_taps, -1).astype(jnp.bfloat16).reshape(slab_shape)
    back_part = lax.dot_general(
        full_in, to_cells(hid_grad), contract_first, preferred_element_type=jnp.float32
    )
    volume_grad = to_channels((grad_cells.astype(jnp.float32) + back_part).astype(jnp.bfloat16))
    return block_out, volume_grad


def body(volume, out_grad, weight_in, weight_out, filter_taps, filter_bias):
    own = volume.shape[0]
    parts = lax.axis_size("chan")
    groups, space = lax.axis_size("groups"), lax.axis_size("space")
    whole_rows = CY % parts == 0 and (CY // parts * CX) % LANES == 0 and parts > 1 and parts & (parts - 1) == 0
    whole_shares = own % LANES == 0 and own % (16 * groups * space) == 0
    split = whole_rows and whole_shares and (groups, space) == (2, 4)
    chosen = split_cells_body if split else exchange_body
    return chosen(volume, out_grad, weight_in, weight_out, filter_taps, filter_bias)


def solution(mesh):
    field = P(("groups", "chan"), "space", None)
    placed = (field, field, P("chan", None), P("chan", None), P("chan", None), P("chan"))
    return jax.shard_map(
        body,
        mesh=mesh,
        in_specs=placed,
        out_specs=(field, field),
        check_vma=False,
    )
```

```python
import jax
import jax.numpy as jnp
from jax import lax
from jax.experimental import pallas as pl
from jax.experimental.pallas import tpu as pltpu
from jax.sharding import PartitionSpec as P

CX = 32
CY = 16
LANES = 128


root_half = 0.7071067811865476
inv_root_two_pi = 0.3989422804014327


def gelu_value(field):
    return 0.5 * field * (1.0 + lax.erf(field * root_half))


def gelu_slope(field):
    return (
        0.5 * (1.0 + lax.erf(field * root_half))
        + field * jnp.exp(-0.5 * field * field) * inv_root_two_pi
    )


def fill_padded(padded, own, row_low, row_high, plane_low, plane_high):
    planes, rows = own.shape[0], own.shape[1]
    for z in range(planes):
        padded[z + 1, 0] = row_low[z].astype(jnp.float32)
        padded[z + 1, rows + 1] = row_high[z].astype(jnp.float32)
        for y in range(rows):
            padded[z + 1, y + 1] = own[z, y].astype(jnp.float32)
    for y in range(rows + 2):
        padded[0, y] = plane_low[y].astype(jnp.float32)
        padded[planes + 1, y] = plane_high[y].astype(jnp.float32)


def stencil_row(padded, taps, z, y, flip):
    sums = [None, None, None]
    for a in range(3):
        for b in range(3):
            row = padded[z + a, y + b]
            for e in range(3):
                index = (a * 3 + b) * 3 + e
                tap = taps[0, 26 - index if flip else index]
                term = row * tap[None, :]
                sums[e] = term if sums[e] is None else sums[e] + term
    x = lax.broadcasted_iota(jnp.int32, sums[0].shape, 0)
    extent = sums[0].shape[0]
    before = jnp.where(x == 0, 0.0, pltpu.roll(sums[0], 1, 0))
    after = jnp.where(x == extent - 1, 0.0, pltpu.roll(sums[2], extent - 1, 0))
    return sums[1] + (before + after)


def doubling(count):
    masks = []
    while count > 1:
        masks.append(count - 1)
        count //= 2
    return masks


def distances(count):
    found = [0]
    for mask in doubling(count):
        found += [mask ^ distance for distance in found]
    return found


def piece_copies(here, mine, other, full, sems):
    chan, seat = here[0], here[1]
    copies = []
    for slot, distance in enumerate(distances(mine.shape[1])):
        for side, pieces in enumerate((mine, other)):
            for turn in range(pieces.shape[0]):
                copies.append(
                    pltpu.make_async_copy(
                        pieces.at[turn, slot],
                        full.at[chan ^ distance, seat ^ side ^ (2 * turn)],
                        sems.at[chan ^ distance, 2 * turn + side],
                    )
                )
    return copies


def wait_block(block, mine, other, full, sems):
    for side, pieces in enumerate((mine, other)):
        for turn in range(pieces.shape[0]):
            pltpu.make_async_copy(
                pieces.at[turn, 0], full.at[block, 2 * turn + side], sems.at[block, 2 * turn + side]
            ).wait()


def start_all(copies):
    for copy in copies:
        copy.start()


def wait_all(copies):
    for copy in copies:
        copy.wait()


def add_planes(base, product, out):
    planes, _, width = base.shape
    for z in range(planes):
        total = base[z].astype(jnp.float32) + product[:, z * width : (z + 1) * width]
        out[z] = total.astype(out.dtype)


def forward_kernel(
    here, own, row_low, row_high, plane_low, plane_high, taps, mine, other, *rest
):
    count = (len(rest) - 5) // 2
    inputs, outputs = rest[:count], rest[count : 2 * count]
    slope, padded, active, weight, sems = rest[2 * count :]
    step = pl.program_id(0)
    planes, rows, extent = own.shape[:3]
    copies = piece_copies(here, mine, other, weight, sems)

    @pl.when(step == 0)
    def _():
        start_all(copies)

    fill_padded(padded, own, row_low, row_high, plane_low, plane_high)
    lanes = pl.ds(pl.multiple_of(step * LANES, LANES), LANES)
    for z in range(planes):
        for y in range(rows):
            mixed = stencil_row(padded, taps, z, y, False) + taps[0, 27][None, :]
            half = 0.5 * (1.0 + lax.erf(mixed * root_half))
            at = (z * rows + y) * extent
            active[at : at + extent, lanes] = (mixed * half).astype(active.dtype)
            slope[z, y] = half + mixed * jnp.exp(-0.5 * mixed * mixed) * inv_root_two_pi

    @pl.when(step == pl.num_programs(0) - 1)
    def _():
        wait_all(copies)
        for shift in range(count):
            rows_of = weight[here[0] ^ shift]
            product = lax.dot_general(
                rows_of.reshape(-1, rows_of.shape[-1]),
                active[...],
                (((1,), (1,)), ((), ())),
                preferred_element_type=jnp.float32,
            )
            add_planes(inputs[shift], product, outputs[shift])


def backward_kernel(
    here, own, row_low, row_high, plane_low, plane_high, taps, mine, other, *rest
):
    count = (len(rest) - 4) // 2
    inputs, outputs = rest[:count], rest[count : 2 * count]
    padded, grads, weight, sems = rest[2 * count :]
    step = pl.program_id(0)
    planes, rows, extent = own.shape[:3]
    copies = piece_copies(here, mine, other, weight, sems)

    @pl.when(step == 0)
    def _():
        start_all(copies)

    fill_padded(padded, own, row_low, row_high, plane_low, plane_high)
    lanes = pl.ds(pl.multiple_of(step * LANES, LANES), LANES)
    for z in range(planes):
        for y in range(rows):
            at = (z * rows + y) * extent
            total = stencil_row(padded, taps, z, y, True)
            grads[at : at + extent, lanes] = total.astype(grads.dtype)

    @pl.when(step == pl.num_programs(0) - 1)
    def _():
        wait_all(copies)
        channels = grads.shape[1]
        width = inputs[0].shape[1]
        for shift in range(count):
            start = pl.multiple_of((here[0] ^ shift) * width, width)
            columns = weight[:, :, :, pl.ds(start, width)].reshape(channels, width)
            product = jnp.dot(grads[...], columns, preferred_element_type=jnp.float32)
            add_planes(inputs[shift], product.T, outputs[shift])


def weight_scratch(mine):
    turns, parts, share, channels = mine.shape
    return [
        pltpu.VMEM((parts, 2 * turns, share, channels), mine.dtype),
        pltpu.SemaphoreType.DMA((parts, 2 * turns)),
    ]


def stencil(here, own, halo, taps, weight, blocks, forward):
    planes, rows, extent, channels = own.shape
    cells = planes * rows * extent
    per_table = taps.shape[2] // LANES

    def block(*lead):
        zeros = (0,) * len(lead)
        return pl.BlockSpec(lead + (LANES,), lambda c, here: zeros + (c,))

    def resident(shape):
        return pl.BlockSpec(shape, lambda c, here: (0,) * len(shape), pipeline_mode=pl.Buffered(1))

    def table_at(c, here):
        away = (c // per_table) ^ here[0]
        slot = 0
        for place, distance in enumerate(distances(taps.shape[0])):
            slot = jnp.where(away == distance, place, slot)
        return slot, 0, c % per_table

    anywhere = pl.BlockSpec(memory_space=pltpu.HBM)
    in_specs = [
        block(planes, rows, extent),
        block(planes, extent),
        block(planes, extent),
        block(rows + 2, extent),
        block(rows + 2, extent),
        pl.BlockSpec((1, 28, LANES), table_at),
        anywhere,
        anywhere,
    ]
    in_specs += [resident(piece.shape) for piece in blocks]
    out_specs = [resident(piece.shape) for piece in blocks]
    out_shape = [jax.ShapeDtypeStruct(piece.shape, piece.dtype) for piece in blocks]
    if forward:
        out_specs.append(block(planes, rows, extent))
        out_shape.append(jax.ShapeDtypeStruct(own.shape, jnp.float32))
    return pl.pallas_call(
        forward_kernel if forward else backward_kernel,
        grid_spec=pltpu.PrefetchScalarGridSpec(
            num_scalar_prefetch=1,
            grid=(channels // LANES,),
            in_specs=in_specs,
            out_specs=out_specs,
            scratch_shapes=[
                pltpu.VMEM((planes + 2, rows + 2, extent, LANES), jnp.float32),
                pltpu.VMEM((cells, channels), own.dtype),
                *weight_scratch(weight[0]),
            ],
        ),
        out_shape=out_shape,
    )(here, own, *halo, taps, *weight, *blocks)


def turn_blocks(here, inputs, turned):
    planes, own, width = inputs[0].shape
    for shift, block in enumerate(inputs):
        start = pl.multiple_of((here[0] ^ shift) * own, own)
        for z in range(planes):
            turned[z * width : (z + 1) * width, pl.ds(start, own)] = block[z].T


def put_with_edges(value, out, first, last, fore, back):
    out[...] = value
    planes, extent, width = first.shape
    plane = value.shape[0] // planes
    rows = plane // extent
    for z in range(planes):
        first[z] = value[z * plane : z * plane + extent]
        last[z] = value[(z + 1) * plane - extent : (z + 1) * plane]
    for edge, z in ((back, 0), (fore, planes - 1)):
        edge[0] = jnp.zeros((extent, width), edge.dtype)
        edge[rows + 1] = jnp.zeros((extent, width), edge.dtype)
        for y in range(rows):
            at = z * plane + y * extent
            edge[y + 1] = value[at : at + extent]


def hidden_kernel(here, mine, other, *rest, count):
    inputs, (*outputs, turned, weight, sems) = rest[:count], rest[count:]

    @pl.when(pl.program_id(0) == 0)
    def _():
        start_all(piece_copies(here, mine, other, weight, sems))
        turn_blocks(here, inputs, turned)

    wait_block(pl.program_id(0), mine, other, weight, sems)
    rows_of = weight[pl.program_id(0)]
    value = lax.dot_general(
        turned[...],
        rows_of.reshape(-1, rows_of.shape[-1]),
        (((1,), (1,)), ((), ())),
        preferred_element_type=jnp.float32,
    )
    put_with_edges(value.astype(turned.dtype), *outputs)


def mix_kernel(here, mine, other, *rest, count):
    inputs, (slope, *outputs, turned, weight, sems) = rest[:count], rest[count:]

    @pl.when(pl.program_id(0) == 0)
    def _():
        copies = piece_copies(here, mine, other, weight, sems)
        start_all(copies)
        turn_blocks(here, inputs, turned)
        wait_all(copies)

    channels, width = turned.shape[1], slope.shape[1]
    start = pl.multiple_of(pl.program_id(0) * width, width)
    columns = weight[:, :, :, pl.ds(start, width)].reshape(channels, width)
    grad = jnp.dot(turned[...], columns, preferred_element_type=jnp.float32)
    grad = grad.astype(turned.dtype).astype(jnp.float32)
    put_with_edges((grad * slope[...]).astype(turned.dtype), *outputs)


def product_call(here, blocks, weight, slope=None):
    planes, own, width = blocks[0].shape
    cells = planes * width
    count = len(blocks)
    channels = own * count
    dtype = blocks[0].dtype
    columns = pl.BlockSpec((cells, own), lambda c, here: (0, c))
    room = width // CX + 2
    row = pl.BlockSpec((planes, CX, own), lambda c, here: (0, 0, c))
    plane = pl.BlockSpec((room, CX, own), lambda c, here: (0, 0, c))
    whole = pl.BlockSpec(
        blocks[0].shape, lambda c, here: (0, 0, 0), pipeline_mode=pl.Buffered(1)
    )
    anywhere = pl.BlockSpec(memory_space=pltpu.HBM)
    kernel, extra = (hidden_kernel, []) if slope is None else (mix_kernel, [slope])
    row_shape = jax.ShapeDtypeStruct((planes, CX, channels), dtype)
    plane_shape = jax.ShapeDtypeStruct((room, CX, channels), dtype)
    return pl.pallas_call(
        lambda *refs: kernel(*refs, count=count),
        grid_spec=pltpu.PrefetchScalarGridSpec(
            num_scalar_prefetch=1,
            grid=(count,),
            in_specs=[anywhere] * 2 + [whole] * count + [columns] * len(extra),
            out_specs=[columns, row, row, plane, plane],
            scratch_shapes=[pltpu.VMEM((cells, channels), dtype), *weight_scratch(weight[0])],
        ),
        out_shape=[
            jax.ShapeDtypeStruct((cells, channels), dtype),
            row_shape,
            row_shape,
            plane_shape,
            plane_shape,
        ],
    )(here, *weight, *blocks, *extra)


def shift_pairs(axis):
    count = lax.axis_size(axis)
    forward = [(i, i + 1) for i in range(count - 1)]
    return forward, [(target, source) for source, target in forward]


def split_cells_body(volume, out_grad, weight_in, weight_out, filter_taps, filter_bias):
    own, planes, cells = volume.shape
    parts = lax.axis_size("chan")
    rows = CY // parts
    width = rows * CX
    channels = own * parts
    others = ("groups", "space")
    seat = lax.axis_index(others)
    chan = lax.axis_index("chan")
    share = own // lax.axis_size(others)
    here = jnp.stack([chan, seat]).astype(jnp.int32)
    shifts = sorted(range(1, parts), key=lambda shift: (shift & (parts // 2) == 0, shift))

    def swap(part, axes, partner):
        count = lax.axis_size(axes)
        return lax.ppermute(part, axes, [(i, partner(i)) for i in range(count)])

    def exchange(blocks):
        got = {0: blocks[0]}
        for shift in shifts:
            got[shift] = swap(blocks[shift], "chan", lambda i: i ^ shift)
        return [got[shift] for shift in range(parts)]

    def cut(field, order, place):
        pieces = {}
        for shift in order:
            start = (place ^ shift) * width
            piece = lax.dynamic_slice_in_dim(field, start, width, axis=2).transpose(1, 0, 2)
            pieces[shift], place = lax.optimization_barrier((piece, place))
        return pieces

    def paste(pieces):
        field = jnp.zeros((own, planes, cells), pieces[0].dtype)
        for shift in [0] + shifts:
            piece = pieces[shift].transpose(1, 0, 2)
            field = lax.dynamic_update_slice_in_dim(field, piece, (chan ^ shift) * width, axis=2)
        return field

    def gather_column(piece):
        column = piece[None]
        for mask in doubling(parts):
            got = swap(column, "chan", lambda i: i ^ mask)
            column = jnp.concatenate([column, got])
        return column

    def gather_weight(column, beside=None):
        over_x = swap(column, others, lambda i: i ^ 2)
        over_y = swap(column, others, lambda i: i ^ 4)
        mixed = jnp.where(seat & 1 == 0, over_y, over_x)
        mixed, beside = lax.optimization_barrier((mixed, beside))
        far = swap(mixed, others, lambda i: i ^ (4 if i & 1 else 2))
        mine = jnp.stack([column, over_x, over_y, far])
        return (mine, swap(mine, others, lambda i: i ^ 1)), beside

    def halo_of(first, last, fore, back):
        forward, backward = shift_pairs("chan")
        row_low = lax.ppermute(last, "chan", forward)
        row_high = lax.ppermute(first, "chan", backward)
        forward, backward = shift_pairs("space")

        def joined(plane, z):
            plane = lax.dynamic_update_slice_in_dim(plane, row_low[z][None], 0, axis=0)
            return lax.dynamic_update_slice_in_dim(plane, row_high[z][None], rows + 1, axis=0)

        plane_low = lax.ppermute(joined(fore, planes - 1), "space", forward)
        plane_high = lax.ppermute(joined(back, 0), "space", backward)
        return row_low, row_high, plane_low, plane_high

    grid = (planes, rows, CX, channels)
    pieces = [
        lax.dynamic_slice_in_dim(weight, seat * share, share, axis=0)
        for weight in (weight_in, weight_out)
    ]
    column = gather_column(jnp.concatenate(pieces))
    vol_cut = cut(volume, shifts, chan)
    later, column = lax.optimization_barrier((chan, column))
    own_cut = cut(volume, [0], later)
    grad_cut = cut(out_grad, shifts + [0], later)
    full_in, (own_block, here, grad_cut) = gather_weight(
        column[:, :share], (own_cut[0], here, grad_cut)
    )
    full_out, _ = gather_weight(column[:, share:])
    table = jnp.concatenate([filter_taps, filter_bias[:, None]], axis=1).T
    taps = gather_column(table)
    own_block, taps = lax.optimization_barrier((own_block, taps))
    vol_blocks = exchange({**vol_cut, 0: own_block})
    grad_blocks = exchange(grad_cut)
    hidden, *edges = product_call(here, vol_blocks, full_in)
    halo = halo_of(*edges)
    *out_blocks, slope = stencil(here, hidden.reshape(grid), halo, taps, full_out, vol_blocks, True)
    out_found = exchange(out_blocks)
    mix_grad, *edges = product_call(
        here, grad_blocks, full_out, slope.reshape(planes * width, channels)
    )
    halo = halo_of(*edges)
    back_blocks = list(
        stencil(here, mix_grad.reshape(grid), halo, taps, full_in, grad_blocks, False)
    )
    out_found, back_blocks[0] = lax.optimization_barrier((out_found, back_blocks[0]))
    block_out = paste(out_found)
    volume_grad = paste(exchange(back_blocks))
    return block_out, volume_grad


def with_halo(block, axis, dim):
    forward, backward = shift_pairs(axis)
    low = lax.ppermute(lax.slice_in_dim(block, block.shape[dim] - 1, None, axis=dim), axis, forward)
    high = lax.ppermute(lax.slice_in_dim(block, 0, 1, axis=dim), axis, backward)
    return jnp.concatenate([low, block, high], axis=dim)


def core(padded, filter_taps, direction):
    extent_z = padded.shape[1] - 2
    extent_y = padded.shape[2] - 2
    extent_x = padded.shape[3] - 2
    summed = jnp.zeros((padded.shape[0], extent_z, extent_y, extent_x), jnp.float32)
    for shift_z in range(3):
        for shift_y in range(3):
            for shift_x in range(3):
                tap_index = (shift_z * 3 + shift_y) * 3 + shift_x
                begin_z = 1 + direction * (shift_z - 1)
                begin_y = 1 + direction * (shift_y - 1)
                begin_x = 1 + direction * (shift_x - 1)
                window = padded[
                    :,
                    begin_z : begin_z + extent_z,
                    begin_y : begin_y + extent_y,
                    begin_x : begin_x + extent_x,
                ]
                summed = summed + filter_taps[:, tap_index][:, None, None, None] * window
    return summed


def lift(field_z):
    extended = field_z.astype(jnp.float32).reshape(field_z.shape[0], field_z.shape[1], CY, CX)
    return jnp.pad(extended, ((0, 0), (0, 0), (1, 1), (1, 1)))


def exchange_body(volume, out_grad, weight_in, weight_out, filter_taps, filter_bias):
    slab_shape = volume.shape
    contract_first = (((0,), (0,)), ((), ()))

    def to_cells(field):
        return lax.all_to_all(
            field.reshape(field.shape[0], -1), "chan", split_axis=1, concat_axis=0, tiled=True
        )

    def to_channels(field):
        return lax.all_to_all(field, "chan", split_axis=0, concat_axis=1, tiled=True).reshape(
            slab_shape
        )

    full_in = lax.all_gather(weight_in, "chan", axis=0, tiled=True)
    full_out = lax.all_gather(weight_out, "chan", axis=0, tiled=True)
    vol_cells = to_cells(volume)
    hidden = to_channels(
        jnp.dot(full_in, vol_cells, preferred_element_type=jnp.float32).astype(jnp.bfloat16)
    )
    padded = lift(with_halo(hidden, "space", 1))
    mixed = core(padded, filter_taps, 1) + filter_bias[:, None, None, None]
    active = gelu_value(mixed).astype(jnp.bfloat16).reshape(slab_shape)
    out_cells = vol_cells.astype(jnp.float32) + jnp.dot(
        full_out, to_cells(active), preferred_element_type=jnp.float32
    )
    block_out = to_channels(out_cells.astype(jnp.bfloat16))
    grad_cells = to_cells(out_grad)
    act_part = lax.dot_general(
        full_out, grad_cells, contract_first, preferred_element_type=jnp.float32
    )
    act_grad = to_channels(act_part.astype(jnp.bfloat16))
    slope = gelu_slope(mixed)
    mix_grad = (
        (act_grad.astype(jnp.float32).reshape(slope.shape) * slope)
        .astype(jnp.bfloat16)
        .reshape(slab_shape)
    )
    padded_grad = lift(with_halo(mix_grad, "space", 1))
    hid_grad = core(padded_grad, filter_taps, -1).astype(jnp.bfloat16).reshape(slab_shape)
    back_part = lax.dot_general(
        full_in, to_cells(hid_grad), contract_first, preferred_element_type=jnp.float32
    )
    volume_grad = to_channels((grad_cells.astype(jnp.float32) + back_part).astype(jnp.bfloat16))
    return block_out, volume_grad


def body(volume, out_grad, weight_in, weight_out, filter_taps, filter_bias):
    own = volume.shape[0]
    parts = lax.axis_size("chan")
    groups, space = lax.axis_size("groups"), lax.axis_size("space")
    whole_rows = CY % parts == 0 and (CY // parts * CX) % LANES == 0 and parts & (parts - 1) == 0
    whole_shares = own % LANES == 0 and own % (16 * groups * space) == 0
    split = whole_rows and whole_shares and (groups, space) == (2, 4)
    chosen = split_cells_body if split else exchange_body
    return chosen(volume, out_grad, weight_in, weight_out, filter_taps, filter_bias)


def solution(mesh):
    field = P(("groups", "chan"), "space", None)
    placed = (field, field, P("chan", None), P("chan", None), P("chan", None), P("chan"))
    return jax.shard_map(
        body,
        mesh=mesh,
        in_specs=placed,
        out_specs=(field, field),
        check_vma=False,
    )
```

```python
import jax
import jax.numpy as jnp
from jax import lax
from jax.experimental import pallas as pl
from jax.experimental.pallas import tpu as pltpu
from jax.sharding import PartitionSpec as P

CX = 32
CY = 16
LANES = 128


root_half = 0.7071067811865476
inv_root_two_pi = 0.3989422804014327


def gelu_value(field):
    return 0.5 * field * (1.0 + lax.erf(field * root_half))


def gelu_slope(field):
    return (
        0.5 * (1.0 + lax.erf(field * root_half))
        + field * jnp.exp(-0.5 * field * field) * inv_root_two_pi
    )


def fill_pairs(pairs, own, row_low, row_high, plane_low, plane_high):
    planes, rows = own.shape[:2]
    for p in range(planes + 2):
        if p == 0:
            fields = [plane_low[y] for y in range(rows + 2)]
        elif p == planes + 1:
            fields = [plane_high[y] for y in range(rows + 2)]
        else:
            fields = [row_low[p - 1]] + [own[p - 1, y] for y in range(rows)] + [row_high[p - 1]]
        fields = [field.astype(jnp.float32) for field in fields]
        for t in range(rows // 2):
            d0, d1, d2, d3 = fields[2 * t : 2 * t + 4]
            pairs[p, t, 0] = d0 - d2
            pairs[p, t, 1] = d1 + d2
            pairs[p, t, 2] = d2 - d1
            pairs[p, t, 3] = d1 - d3


def fill_factors(factors, taps, flip):
    for a in range(3):
        for e in range(3):
            g = []
            for b in range(3):
                index = (a * 3 + b) * 3 + e
                g.append(taps[0, 26 - index if flip else index])
            ends = g[0] + g[2]
            at = (a * 3 + e) * 4
            factors[at] = g[0]
            factors[at + 1] = 0.5 * (ends + g[1])
            factors[at + 2] = 0.5 * (ends - g[1])
            factors[at + 3] = g[2]


def stencil_pair(pairs, factors, z, t):
    sums = ([], [])
    for e in range(3):
        terms = []
        for i in range(4):
            total = None
            for a in range(3):
                term = pairs[z + a, t, i] * factors[(a * 3 + e) * 4 + i][None, :]
                total = term if total is None else total + term
            terms.append(total)
        sums[0].append(terms[0] + terms[1] + terms[2])
        sums[1].append(terms[1] - terms[2] - terms[3])
    extent = sums[0][0].shape[0]
    x = lax.broadcasted_iota(jnp.int32, sums[0][0].shape, 0)
    for left, here, right in sums:
        before = jnp.where(x == 0, 0.0, pltpu.roll(left, 1, 0))
        after = jnp.where(x == extent - 1, 0.0, pltpu.roll(right, extent - 1, 0))
        yield here + (before + after)


def doubling(count):
    masks = []
    while count > 1:
        masks.append(count - 1)
        count //= 2
    return masks


def distances(count):
    found = [0]
    for mask in doubling(count):
        found += [mask ^ distance for distance in found]
    return found


def piece_copies(here, mine, other, full, sems):
    chan, seat = here[0], here[1]
    copies = []
    for slot, distance in enumerate(distances(mine.shape[1])):
        for side, pieces in enumerate((mine, other)):
            for turn in range(pieces.shape[0]):
                copies.append(
                    pltpu.make_async_copy(
                        pieces.at[turn, slot],
                        full.at[chan ^ distance, seat ^ side ^ (2 * turn)],
                        sems.at[chan ^ distance, 2 * turn + side],
                    )
                )
    return copies


def wait_block(block, mine, other, full, sems):
    for side, pieces in enumerate((mine, other)):
        for turn in range(pieces.shape[0]):
            pltpu.make_async_copy(
                pieces.at[turn, 0], full.at[block, 2 * turn + side], sems.at[block, 2 * turn + side]
            ).wait()


def start_all(copies):
    for copy in copies:
        copy.start()


def wait_all(copies):
    for copy in copies:
        copy.wait()


def add_planes(base, product, out):
    planes, _, width = base.shape
    for z in range(planes):
        total = base[z].astype(jnp.float32) + product[:, z * width : (z + 1) * width]
        out[z] = total.astype(out.dtype)


def forward_kernel(
    here, own, row_low, row_high, plane_low, plane_high, taps, mine, other, *rest
):
    count = (len(rest) - 6) // 2
    inputs, outputs = rest[:count], rest[count : 2 * count]
    slope, pairs, factors, active, weight, sems = rest[2 * count :]
    step = pl.program_id(0)
    planes, rows, extent = own.shape[:3]
    copies = piece_copies(here, mine, other, weight, sems)

    @pl.when(step == 0)
    def _():
        start_all(copies)

    fill_pairs(pairs, own, row_low, row_high, plane_low, plane_high)
    fill_factors(factors, taps, False)
    lanes = pl.ds(pl.multiple_of(step * LANES, LANES), LANES)
    for z in range(planes):
        for t in range(rows // 2):
            for odd, mixed in enumerate(stencil_pair(pairs, factors, z, t)):
                y = 2 * t + odd
                mixed = mixed + taps[0, 27][None, :]
                half = 0.5 * (1.0 + lax.erf(mixed * root_half))
                at = (z * rows + y) * extent
                active[at : at + extent, lanes] = (mixed * half).astype(active.dtype)
                slope[z, y] = half + mixed * jnp.exp(-0.5 * mixed * mixed) * inv_root_two_pi

    @pl.when(step == pl.num_programs(0) - 1)
    def _():
        wait_all(copies)
        for shift in range(count):
            rows_of = weight[here[0] ^ shift]
            product = lax.dot_general(
                rows_of.reshape(-1, rows_of.shape[-1]),
                active[...],
                (((1,), (1,)), ((), ())),
                preferred_element_type=jnp.float32,
            )
            add_planes(inputs[shift], product, outputs[shift])


def backward_kernel(
    here, own, row_low, row_high, plane_low, plane_high, taps, mine, other, *rest
):
    count = (len(rest) - 5) // 2
    inputs, outputs = rest[:count], rest[count : 2 * count]
    pairs, factors, grads, weight, sems = rest[2 * count :]
    step = pl.program_id(0)
    planes, rows, extent = own.shape[:3]
    copies = piece_copies(here, mine, other, weight, sems)

    @pl.when(step == 0)
    def _():
        start_all(copies)

    fill_pairs(pairs, own, row_low, row_high, plane_low, plane_high)
    fill_factors(factors, taps, True)
    lanes = pl.ds(pl.multiple_of(step * LANES, LANES), LANES)
    for z in range(planes):
        for t in range(rows // 2):
            for odd, total in enumerate(stencil_pair(pairs, factors, z, t)):
                at = (z * rows + 2 * t + odd) * extent
                grads[at : at + extent, lanes] = total.astype(grads.dtype)

    @pl.when(step == pl.num_programs(0) - 1)
    def _():
        wait_all(copies)
        channels = grads.shape[1]
        width = inputs[0].shape[1]
        for shift in range(count):
            start = pl.multiple_of((here[0] ^ shift) * width, width)
            columns = weight[:, :, :, pl.ds(start, width)].reshape(channels, width)
            product = jnp.dot(grads[...], columns, preferred_element_type=jnp.float32)
            add_planes(inputs[shift], product.T, outputs[shift])


def weight_scratch(mine):
    turns, parts, share, channels = mine.shape
    return [
        pltpu.VMEM((parts, 2 * turns, share, channels), mine.dtype),
        pltpu.SemaphoreType.DMA((parts, 2 * turns)),
    ]


def stencil(here, own, halo, taps, weight, blocks, forward):
    planes, rows, extent, channels = own.shape
    cells = planes * rows * extent
    per_table = taps.shape[2] // LANES

    def block(*lead):
        zeros = (0,) * len(lead)
        return pl.BlockSpec(lead + (LANES,), lambda c, here: zeros + (c,))

    def resident(shape):
        return pl.BlockSpec(shape, lambda c, here: (0,) * len(shape), pipeline_mode=pl.Buffered(1))

    def table_at(c, here):
        away = (c // per_table) ^ here[0]
        slot = 0
        for place, distance in enumerate(distances(taps.shape[0])):
            slot = jnp.where(away == distance, place, slot)
        return slot, 0, c % per_table

    anywhere = pl.BlockSpec(memory_space=pltpu.HBM)
    in_specs = [
        block(planes, rows, extent),
        block(planes, extent),
        block(planes, extent),
        block(rows + 2, extent),
        block(rows + 2, extent),
        pl.BlockSpec((1, 28, LANES), table_at),
        anywhere,
        anywhere,
    ]
    in_specs += [resident(piece.shape) for piece in blocks]
    out_specs = [resident(piece.shape) for piece in blocks]
    out_shape = [jax.ShapeDtypeStruct(piece.shape, piece.dtype) for piece in blocks]
    if forward:
        out_specs.append(block(planes, rows, extent))
        out_shape.append(jax.ShapeDtypeStruct(own.shape, jnp.float32))
    return pl.pallas_call(
        forward_kernel if forward else backward_kernel,
        grid_spec=pltpu.PrefetchScalarGridSpec(
            num_scalar_prefetch=1,
            grid=(channels // LANES,),
            in_specs=in_specs,
            out_specs=out_specs,
            scratch_shapes=[
                pltpu.VMEM((planes + 2, rows // 2, 4, extent, LANES), jnp.float32),
                pltpu.VMEM((36, LANES), jnp.float32),
                pltpu.VMEM((cells, channels), own.dtype),
                *weight_scratch(weight[0]),
            ],
        ),
        out_shape=out_shape,
    )(here, own, *halo, taps, *weight, *blocks)


def block_copies(inputs, held, sems):
    return [
        pltpu.make_async_copy(block, held.at[shift], sems.at[shift])
        for shift, block in enumerate(inputs)
    ]


def turn_blocks(here, copies, held, turned):
    _, planes, own, width = held.shape
    for shift, copy in enumerate(copies):
        copy.wait()
        block = held.at[shift]
        start = pl.multiple_of((here[0] ^ shift) * own, own)
        for z in range(planes):
            turned[z * width : (z + 1) * width, pl.ds(start, own)] = block[z].T


def put_with_edges(value, out, first, last, fore, back):
    out[...] = value
    planes, extent, width = first.shape
    plane = value.shape[0] // planes
    rows = plane // extent
    for z in range(planes):
        first[z] = value[z * plane : z * plane + extent]
        last[z] = value[(z + 1) * plane - extent : (z + 1) * plane]
    for edge, z in ((back, 0), (fore, planes - 1)):
        edge[0] = jnp.zeros((extent, width), edge.dtype)
        edge[rows + 1] = jnp.zeros((extent, width), edge.dtype)
        for y in range(rows):
            at = z * plane + y * extent
            edge[y + 1] = value[at : at + extent]


def hidden_kernel(here, mine, other, *rest, count):
    inputs, (*outputs, turned, held, arrived, weight, sems) = rest[:count], rest[count:]

    @pl.when(pl.program_id(0) == 0)
    def _():
        blocks = block_copies(inputs, held, arrived)
        start_all(blocks)
        start_all(piece_copies(here, mine, other, weight, sems))
        turn_blocks(here, blocks, held, turned)

    wait_block(pl.program_id(0), mine, other, weight, sems)
    rows_of = weight[pl.program_id(0)]
    value = lax.dot_general(
        turned[...],
        rows_of.reshape(-1, rows_of.shape[-1]),
        (((1,), (1,)), ((), ())),
        preferred_element_type=jnp.float32,
    )
    put_with_edges(value.astype(turned.dtype), *outputs)


def mix_kernel(here, mine, other, *rest, count):
    inputs, (slope, *outputs, turned, held, arrived, weight, sems) = rest[:count], rest[count:]

    @pl.when(pl.program_id(0) == 0)
    def _():
        blocks = block_copies(inputs, held, arrived)
        start_all(blocks)
        copies = piece_copies(here, mine, other, weight, sems)
        start_all(copies)
        turn_blocks(here, blocks, held, turned)
        wait_all(copies)

    channels, width = turned.shape[1], slope.shape[1]
    start = pl.multiple_of(pl.program_id(0) * width, width)
    columns = weight[:, :, :, pl.ds(start, width)].reshape(channels, width)
    grad = jnp.dot(turned[...], columns, preferred_element_type=jnp.float32)
    grad = grad.astype(turned.dtype).astype(jnp.float32)
    put_with_edges((grad * slope[...]).astype(turned.dtype), *outputs)


def product_call(here, blocks, weight, slope=None):
    planes, own, width = blocks[0].shape
    cells = planes * width
    count = len(blocks)
    channels = own * count
    dtype = blocks[0].dtype
    columns = pl.BlockSpec((cells, own), lambda c, here: (0, c))
    room = width // CX + 2
    row = pl.BlockSpec((planes, CX, own), lambda c, here: (0, 0, c))
    plane = pl.BlockSpec((room, CX, own), lambda c, here: (0, 0, c))
    anywhere = pl.BlockSpec(memory_space=pltpu.HBM)
    kernel, extra = (hidden_kernel, []) if slope is None else (mix_kernel, [slope])
    row_shape = jax.ShapeDtypeStruct((planes, CX, channels), dtype)
    plane_shape = jax.ShapeDtypeStruct((room, CX, channels), dtype)
    return pl.pallas_call(
        lambda *refs: kernel(*refs, count=count),
        grid_spec=pltpu.PrefetchScalarGridSpec(
            num_scalar_prefetch=1,
            grid=(count,),
            in_specs=[anywhere] * (2 + count) + [columns] * len(extra),
            out_specs=[columns, row, row, plane, plane],
            scratch_shapes=[
                pltpu.VMEM((cells, channels), dtype),
                pltpu.VMEM((count, planes, own, width), dtype),
                pltpu.SemaphoreType.DMA((count,)),
                *weight_scratch(weight[0]),
            ],
        ),
        out_shape=[
            jax.ShapeDtypeStruct((cells, channels), dtype),
            row_shape,
            row_shape,
            plane_shape,
            plane_shape,
        ],
    )(here, *weight, *blocks, *extra)


def shift_pairs(axis):
    count = lax.axis_size(axis)
    forward = [(i, i + 1) for i in range(count - 1)]
    return forward, [(target, source) for source, target in forward]


def split_cells_body(volume, out_grad, weight_in, weight_out, filter_taps, filter_bias):
    own, planes, cells = volume.shape
    parts = lax.axis_size("chan")
    rows = CY // parts
    width = rows * CX
    channels = own * parts
    others = ("groups", "space")
    seat = lax.axis_index(others)
    chan = lax.axis_index("chan")
    share = own // lax.axis_size(others)
    here = jnp.stack([chan, seat]).astype(jnp.int32)
    shifts = sorted(range(1, parts), key=lambda shift: (shift & (parts // 2) == 0, shift))

    def swap(part, axes, partner):
        count = lax.axis_size(axes)
        return lax.ppermute(part, axes, [(i, partner(i)) for i in range(count)])

    def exchange(blocks):
        got = {0: blocks[0]}
        for shift in shifts:
            got[shift] = swap(blocks[shift], "chan", lambda i: i ^ shift)
        return [got[shift] for shift in range(parts)]

    def cut(field, order, place):
        pieces = {}
        for shift in order:
            start = (place ^ shift) * width
            piece = lax.dynamic_slice_in_dim(field, start, width, axis=2).transpose(1, 0, 2)
            pieces[shift], place = lax.optimization_barrier((piece, place))
        return pieces

    def paste(pieces):
        field = jnp.zeros((own, planes, cells), pieces[0].dtype)
        for shift in [0] + shifts:
            piece = pieces[shift].transpose(1, 0, 2)
            field = lax.dynamic_update_slice_in_dim(field, piece, (chan ^ shift) * width, axis=2)
        return field

    def gather_column(piece):
        column = piece[None]
        for mask in doubling(parts):
            got = swap(column, "chan", lambda i: i ^ mask)
            column = jnp.concatenate([column, got])
        return column

    def gather_weight(column, beside=None):
        over_x = swap(column, others, lambda i: i ^ 2)
        over_y = swap(column, others, lambda i: i ^ 4)
        mixed = jnp.where(seat & 1 == 0, over_y, over_x)
        mixed, beside = lax.optimization_barrier((mixed, beside))
        far = swap(mixed, others, lambda i: i ^ (4 if i & 1 else 2))
        mine = jnp.stack([column, over_x, over_y, far])
        return (mine, swap(mine, others, lambda i: i ^ 1)), beside

    def halo_of(first, last, fore, back):
        forward, backward = shift_pairs("chan")
        row_low = lax.ppermute(last, "chan", forward)
        row_high = lax.ppermute(first, "chan", backward)
        forward, backward = shift_pairs("space")

        def joined(plane, z):
            plane = lax.dynamic_update_slice_in_dim(plane, row_low[z][None], 0, axis=0)
            return lax.dynamic_update_slice_in_dim(plane, row_high[z][None], rows + 1, axis=0)

        plane_low = lax.ppermute(joined(fore, planes - 1), "space", forward)
        plane_high = lax.ppermute(joined(back, 0), "space", backward)
        return row_low, row_high, plane_low, plane_high

    grid = (planes, rows, CX, channels)
    piece_in, piece_out = (
        lax.dynamic_slice_in_dim(weight, seat * share, share, axis=0)
        for weight in (weight_in, weight_out)
    )
    column = gather_column(piece_in)
    vol_cut = cut(volume, shifts, chan)
    later, column = lax.optimization_barrier((chan, column))
    own_cut = cut(volume, [0], later)
    grad_cut = cut(out_grad, shifts + [0], later)
    full_in, (own_block, here, grad_cut) = gather_weight(column, (own_cut[0], here, grad_cut))
    full_out, _ = gather_weight(gather_column(piece_out))
    table = jnp.concatenate([filter_taps, filter_bias[:, None]], axis=1).T
    taps = gather_column(table)
    own_block, taps = lax.optimization_barrier((own_block, taps))
    vol_blocks = exchange({**vol_cut, 0: own_block})
    grad_blocks = exchange(grad_cut)
    hidden, *edges = product_call(here, vol_blocks, full_in)
    halo = halo_of(*edges)
    *out_blocks, slope = stencil(here, hidden.reshape(grid), halo, taps, full_out, vol_blocks, True)
    out_found = exchange(out_blocks)
    mix_grad, *edges = product_call(
        here, grad_blocks, full_out, slope.reshape(planes * width, channels)
    )
    halo = halo_of(*edges)
    back_blocks = list(
        stencil(here, mix_grad.reshape(grid), halo, taps, full_in, grad_blocks, False)
    )
    out_found, back_blocks[0] = lax.optimization_barrier((out_found, back_blocks[0]))
    block_out = paste(out_found)
    volume_grad = paste(exchange(back_blocks))
    return block_out, volume_grad


def with_halo(block, axis, dim):
    forward, backward = shift_pairs(axis)
    low = lax.ppermute(lax.slice_in_dim(block, block.shape[dim] - 1, None, axis=dim), axis, forward)
    high = lax.ppermute(lax.slice_in_dim(block, 0, 1, axis=dim), axis, backward)
    return jnp.concatenate([low, block, high], axis=dim)


def core(padded, filter_taps, direction):
    extent_z = padded.shape[1] - 2
    extent_y = padded.shape[2] - 2
    extent_x = padded.shape[3] - 2
    summed = jnp.zeros((padded.shape[0], extent_z, extent_y, extent_x), jnp.float32)
    for shift_z in range(3):
        for shift_y in range(3):
            for shift_x in range(3):
                tap_index = (shift_z * 3 + shift_y) * 3 + shift_x
                begin_z = 1 + direction * (shift_z - 1)
                begin_y = 1 + direction * (shift_y - 1)
                begin_x = 1 + direction * (shift_x - 1)
                window = padded[
                    :,
                    begin_z : begin_z + extent_z,
                    begin_y : begin_y + extent_y,
                    begin_x : begin_x + extent_x,
                ]
                summed = summed + filter_taps[:, tap_index][:, None, None, None] * window
    return summed


def lift(field_z):
    extended = field_z.astype(jnp.float32).reshape(field_z.shape[0], field_z.shape[1], CY, CX)
    return jnp.pad(extended, ((0, 0), (0, 0), (1, 1), (1, 1)))


def exchange_body(volume, out_grad, weight_in, weight_out, filter_taps, filter_bias):
    slab_shape = volume.shape
    contract_first = (((0,), (0,)), ((), ()))

    def to_cells(field):
        return lax.all_to_all(
            field.reshape(field.shape[0], -1), "chan", split_axis=1, concat_axis=0, tiled=True
        )

    def to_channels(field):
        return lax.all_to_all(field, "chan", split_axis=0, concat_axis=1, tiled=True).reshape(
            slab_shape
        )

    full_in = lax.all_gather(weight_in, "chan", axis=0, tiled=True)
    full_out = lax.all_gather(weight_out, "chan", axis=0, tiled=True)
    vol_cells = to_cells(volume)
    hidden = to_channels(
        jnp.dot(full_in, vol_cells, preferred_element_type=jnp.float32).astype(jnp.bfloat16)
    )
    padded = lift(with_halo(hidden, "space", 1))
    mixed = core(padded, filter_taps, 1) + filter_bias[:, None, None, None]
    active = gelu_value(mixed).astype(jnp.bfloat16).reshape(slab_shape)
    out_cells = vol_cells.astype(jnp.float32) + jnp.dot(
        full_out, to_cells(active), preferred_element_type=jnp.float32
    )
    block_out = to_channels(out_cells.astype(jnp.bfloat16))
    grad_cells = to_cells(out_grad)
    act_part = lax.dot_general(
        full_out, grad_cells, contract_first, preferred_element_type=jnp.float32
    )
    act_grad = to_channels(act_part.astype(jnp.bfloat16))
    slope = gelu_slope(mixed)
    mix_grad = (
        (act_grad.astype(jnp.float32).reshape(slope.shape) * slope)
        .astype(jnp.bfloat16)
        .reshape(slab_shape)
    )
    padded_grad = lift(with_halo(mix_grad, "space", 1))
    hid_grad = core(padded_grad, filter_taps, -1).astype(jnp.bfloat16).reshape(slab_shape)
    back_part = lax.dot_general(
        full_in, to_cells(hid_grad), contract_first, preferred_element_type=jnp.float32
    )
    volume_grad = to_channels((grad_cells.astype(jnp.float32) + back_part).astype(jnp.bfloat16))
    return block_out, volume_grad


def body(volume, out_grad, weight_in, weight_out, filter_taps, filter_bias):
    own = volume.shape[0]
    parts = lax.axis_size("chan")
    groups, space = lax.axis_size("groups"), lax.axis_size("space")
    whole_rows = CY % (2 * parts) == 0 and (CY // parts * CX) % LANES == 0
    whole_rows = whole_rows and parts & (parts - 1) == 0
    whole_shares = own % LANES == 0 and own % (16 * groups * space) == 0
    split = whole_rows and whole_shares and (groups, space) == (2, 4)
    chosen = split_cells_body if split else exchange_body
    return chosen(volume, out_grad, weight_in, weight_out, filter_taps, filter_bias)


def solution(mesh):
    field = P(("groups", "chan"), "space", None)
    placed = (field, field, P("chan", None), P("chan", None), P("chan", None), P("chan"))
    return jax.shard_map(
        body,
        mesh=mesh,
        in_specs=placed,
        out_specs=(field, field),
        check_vma=False,
    )
```

```python
import jax
import jax.numpy as jnp
from jax import lax
from jax.experimental import pallas as pl
from jax.experimental.pallas import tpu as pltpu
from jax.sharding import PartitionSpec as P

CX = 32
CY = 16
LANES = 128


root_half = 0.7071067811865476
inv_root_two_pi = 0.3989422804014327


def gelu_value(field):
    return 0.5 * field * (1.0 + lax.erf(field * root_half))


def gelu_slope(field):
    return (
        0.5 * (1.0 + lax.erf(field * root_half))
        + field * jnp.exp(-0.5 * field * field) * inv_root_two_pi
    )


def fill_pairs(pairs, own, row_low, row_high, plane_low, plane_high):
    planes, rows = own.shape[:2]
    for p in range(planes + 2):
        if p == 0:
            fields = [plane_low[y] for y in range(rows + 2)]
        elif p == planes + 1:
            fields = [plane_high[y] for y in range(rows + 2)]
        else:
            fields = [row_low[p - 1]] + [own[p - 1, y] for y in range(rows)] + [row_high[p - 1]]
        fields = [field.astype(jnp.float32) for field in fields]
        for t in range(rows // 2):
            d0, d1, d2, d3 = fields[2 * t : 2 * t + 4]
            pairs[p, t, 0] = d0 - d2
            pairs[p, t, 1] = d1 + d2
            pairs[p, t, 2] = d2 - d1
            pairs[p, t, 3] = d1 - d3


def fill_factors(factors, taps, flip):
    for a in range(3):
        for e in range(3):
            g = []
            for b in range(3):
                index = (a * 3 + b) * 3 + e
                g.append(taps[0, 26 - index if flip else index])
            ends = g[0] + g[2]
            at = (a * 3 + e) * 4
            factors[at] = g[0]
            factors[at + 1] = 0.5 * (ends + g[1])
            factors[at + 2] = 0.5 * (ends - g[1])
            factors[at + 3] = g[2]


def stencil_pair(pairs, factors, z, t):
    sums = ([], [])
    for e in range(3):
        terms = []
        for i in range(4):
            total = None
            for a in range(3):
                term = pairs[z + a, t, i] * factors[(a * 3 + e) * 4 + i][None, :]
                total = term if total is None else total + term
            terms.append(total)
        sums[0].append(terms[0] + terms[1] + terms[2])
        sums[1].append(terms[1] - terms[2] - terms[3])
    extent = sums[0][0].shape[0]
    x = lax.broadcasted_iota(jnp.int32, sums[0][0].shape, 0)
    for left, here, right in sums:
        before = jnp.where(x == 0, 0.0, pltpu.roll(left, 1, 0))
        after = jnp.where(x == extent - 1, 0.0, pltpu.roll(right, extent - 1, 0))
        yield here + (before + after)


def doubling(count):
    masks = []
    while count > 1:
        masks.append(count - 1)
        count //= 2
    return masks


def distances(count):
    found = [0]
    for mask in doubling(count):
        found += [mask ^ distance for distance in found]
    return found


def piece_copies(here, mine, other, full, sems):
    chan, seat = here[0], here[1]
    copies = []
    for slot, distance in enumerate(distances(mine.shape[1])):
        for side, pieces in enumerate((mine, other)):
            for turn in range(pieces.shape[0]):
                copies.append(
                    pltpu.make_async_copy(
                        pieces.at[turn, slot],
                        full.at[chan ^ distance, seat ^ side ^ (2 * turn)],
                        sems.at[chan ^ distance, 2 * turn + side],
                    )
                )
    return copies


def wait_block(block, mine, other, full, sems):
    for side, pieces in enumerate((mine, other)):
        for turn in range(pieces.shape[0]):
            pltpu.make_async_copy(
                pieces.at[turn, 0], full.at[block, 2 * turn + side], sems.at[block, 2 * turn + side]
            ).wait()


def start_all(copies):
    for copy in copies:
        copy.start()


def wait_all(copies):
    for copy in copies:
        copy.wait()


def add_planes(base, product, out):
    planes, _, width = base.shape
    for z in range(planes):
        total = base[z].astype(jnp.float32) + product[:, z * width : (z + 1) * width]
        out[z] = total.astype(out.dtype)


def put_copy(shift, ready, outputs, left):
    return pltpu.make_async_copy(ready.at[shift], outputs[shift], left.at[shift])


def forward_kernel(
    here, own, row_low, row_high, plane_low, plane_high, taps, mine, other, *rest
):
    count = (len(rest) - 10) // 2
    inputs, outputs = rest[:count], rest[count : 2 * count]
    slope, pairs, factors, active, *blocks, weight, sems = rest[2 * count :]
    held, ready, arrived, left = blocks
    step = pl.program_id(0)
    planes, rows, extent = own.shape[:3]
    copies = piece_copies(here, mine, other, weight, sems)

    @pl.when(step == 0)
    def _():
        start_all(copies)
        start_all(block_copies(inputs, held, arrived))

    fill_pairs(pairs, own, row_low, row_high, plane_low, plane_high)
    fill_factors(factors, taps, False)
    lanes = pl.ds(pl.multiple_of(step * LANES, LANES), LANES)
    for z in range(planes):
        for t in range(rows // 2):
            for odd, mixed in enumerate(stencil_pair(pairs, factors, z, t)):
                y = 2 * t + odd
                mixed = mixed + taps[0, 27][None, :]
                half = 0.5 * (1.0 + lax.erf(mixed * root_half))
                at = (z * rows + y) * extent
                active[at : at + extent, lanes] = (mixed * half).astype(active.dtype)
                bell = jnp.exp(-0.5 * mixed * mixed) * inv_root_two_pi
                slope[z, y] = (half + mixed * bell).astype(slope.dtype)

    @pl.when(step == pl.num_programs(0) - 1)
    def _():
        wait_all(copies)
        wait_all(block_copies(inputs, held, arrived))
        for shift in range(count):
            rows_of = weight[here[0] ^ shift]
            product = lax.dot_general(
                rows_of.reshape(-1, rows_of.shape[-1]),
                active[...],
                (((1,), (1,)), ((), ())),
                preferred_element_type=jnp.float32,
            )
            add_planes(held.at[shift], product, ready.at[shift])
            put_copy(shift, ready, outputs, left).start()
        for shift in range(count):
            put_copy(shift, ready, outputs, left).wait()


def backward_kernel(
    here, own, row_low, row_high, plane_low, plane_high, taps, mine, other, *rest
):
    count = (len(rest) - 9) // 2
    inputs, outputs = rest[:count], rest[count : 2 * count]
    pairs, factors, grads, *blocks, weight, sems = rest[2 * count :]
    held, ready, arrived, left = blocks
    step = pl.program_id(0)
    planes, rows, extent = own.shape[:3]
    copies = piece_copies(here, mine, other, weight, sems)

    @pl.when(step == 0)
    def _():
        start_all(copies)
        start_all(block_copies(inputs, held, arrived))

    fill_pairs(pairs, own, row_low, row_high, plane_low, plane_high)
    fill_factors(factors, taps, True)
    lanes = pl.ds(pl.multiple_of(step * LANES, LANES), LANES)
    for z in range(planes):
        for t in range(rows // 2):
            for odd, total in enumerate(stencil_pair(pairs, factors, z, t)):
                at = (z * rows + 2 * t + odd) * extent
                grads[at : at + extent, lanes] = total.astype(grads.dtype)

    @pl.when(step == pl.num_programs(0) - 1)
    def _():
        wait_all(copies)
        wait_all(block_copies(inputs, held, arrived))
        channels = grads.shape[1]
        width = held.shape[2]
        for shift in range(count):
            start = pl.multiple_of((here[0] ^ shift) * width, width)
            columns = weight[:, :, :, pl.ds(start, width)].reshape(channels, width)
            product = jnp.dot(grads[...], columns, preferred_element_type=jnp.float32)
            add_planes(held.at[shift], product.T, ready.at[shift])
            put_copy(shift, ready, outputs, left).start()
        for shift in range(count):
            put_copy(shift, ready, outputs, left).wait()


def weight_scratch(mine):
    turns, parts, share, channels = mine.shape
    return [
        pltpu.VMEM((parts, 2 * turns, share, channels), mine.dtype),
        pltpu.SemaphoreType.DMA((parts, 2 * turns)),
    ]


def stencil(here, own, halo, taps, weight, blocks, forward):
    planes, rows, extent, channels = own.shape
    cells = planes * rows * extent
    per_table = taps.shape[2] // LANES

    def block(*lead):
        zeros = (0,) * len(lead)
        return pl.BlockSpec(lead + (LANES,), lambda c, here: zeros + (c,))

    def table_at(c, here):
        away = (c // per_table) ^ here[0]
        slot = 0
        for place, distance in enumerate(distances(taps.shape[0])):
            slot = jnp.where(away == distance, place, slot)
        return slot, 0, c % per_table

    anywhere = pl.BlockSpec(memory_space=pltpu.HBM)
    in_specs = [
        block(planes, rows, extent),
        block(planes, extent),
        block(planes, extent),
        block(rows + 2, extent),
        block(rows + 2, extent),
        pl.BlockSpec((1, 28, LANES), table_at),
        anywhere,
        anywhere,
    ]
    in_specs += [anywhere for _ in blocks]
    out_specs = [anywhere for _ in blocks]
    out_shape = [jax.ShapeDtypeStruct(piece.shape, piece.dtype) for piece in blocks]
    if forward:
        out_specs.append(block(planes, rows, extent))
        out_shape.append(jax.ShapeDtypeStruct(own.shape, own.dtype))
    return pl.pallas_call(
        forward_kernel if forward else backward_kernel,
        grid_spec=pltpu.PrefetchScalarGridSpec(
            num_scalar_prefetch=1,
            grid=(channels // LANES,),
            in_specs=in_specs,
            out_specs=out_specs,
            scratch_shapes=[
                pltpu.VMEM((planes + 2, rows // 2, 4, extent, LANES), jnp.float32),
                pltpu.VMEM((36, LANES), jnp.float32),
                pltpu.VMEM((cells, channels), own.dtype),
                pltpu.VMEM((len(blocks),) + blocks[0].shape, own.dtype),
                pltpu.VMEM((len(blocks),) + blocks[0].shape, own.dtype),
                pltpu.SemaphoreType.DMA((len(blocks),)),
                pltpu.SemaphoreType.DMA((len(blocks),)),
                *weight_scratch(weight[0]),
            ],
        ),
        out_shape=out_shape,
    )(here, own, *halo, taps, *weight, *blocks)


def block_copies(inputs, held, sems):
    return [
        pltpu.make_async_copy(block, held.at[shift], sems.at[shift])
        for shift, block in enumerate(inputs)
    ]


def turn_blocks(here, copies, held, turned):
    _, planes, own, width = held.shape
    for shift, copy in enumerate(copies):
        copy.wait()
        block = held.at[shift]
        start = pl.multiple_of((here[0] ^ shift) * own, own)
        for z in range(planes):
            turned[z * width : (z + 1) * width, pl.ds(start, own)] = block[z].T


def put_with_edges(value, out, first, last, fore, back):
    out[...] = value
    planes, extent, width = first.shape
    plane = value.shape[0] // planes
    rows = plane // extent
    for z in range(planes):
        first[z] = value[z * plane : z * plane + extent]
        last[z] = value[(z + 1) * plane - extent : (z + 1) * plane]
    for edge, z in ((back, 0), (fore, planes - 1)):
        edge[0] = jnp.zeros((extent, width), edge.dtype)
        edge[rows + 1] = jnp.zeros((extent, width), edge.dtype)
        for y in range(rows):
            at = z * plane + y * extent
            edge[y + 1] = value[at : at + extent]


def hidden_kernel(here, mine, other, *rest, count):
    inputs, (*outputs, turned, held, arrived, weight, sems) = rest[:count], rest[count:]

    @pl.when(pl.program_id(0) == 0)
    def _():
        blocks = block_copies(inputs, held, arrived)
        start_all(blocks)
        start_all(piece_copies(here, mine, other, weight, sems))
        turn_blocks(here, blocks, held, turned)

    wait_block(pl.program_id(0), mine, other, weight, sems)
    rows_of = weight[pl.program_id(0)]
    value = lax.dot_general(
        turned[...],
        rows_of.reshape(-1, rows_of.shape[-1]),
        (((1,), (1,)), ((), ())),
        preferred_element_type=jnp.float32,
    )
    put_with_edges(value.astype(turned.dtype), *outputs)


def mix_kernel(here, mine, other, *rest, count):
    inputs, (slope, *outputs, turned, held, arrived, weight, sems) = rest[:count], rest[count:]

    @pl.when(pl.program_id(0) == 0)
    def _():
        blocks = block_copies(inputs, held, arrived)
        start_all(blocks)
        copies = piece_copies(here, mine, other, weight, sems)
        start_all(copies)
        turn_blocks(here, blocks, held, turned)
        wait_all(copies)

    channels, width = turned.shape[1], slope.shape[1]
    start = pl.multiple_of(pl.program_id(0) * width, width)
    columns = weight[:, :, :, pl.ds(start, width)].reshape(channels, width)
    grad = jnp.dot(turned[...], columns, preferred_element_type=jnp.float32)
    grad = grad.astype(turned.dtype).astype(jnp.float32)
    put_with_edges((grad * slope[...].astype(jnp.float32)).astype(turned.dtype), *outputs)


def product_call(here, blocks, weight, slope=None):
    planes, own, width = blocks[0].shape
    cells = planes * width
    count = len(blocks)
    channels = own * count
    dtype = blocks[0].dtype
    columns = pl.BlockSpec((cells, own), lambda c, here: (0, c))
    room = width // CX + 2
    row = pl.BlockSpec((planes, CX, own), lambda c, here: (0, 0, c))
    plane = pl.BlockSpec((room, CX, own), lambda c, here: (0, 0, c))
    anywhere = pl.BlockSpec(memory_space=pltpu.HBM)
    kernel, extra = (hidden_kernel, []) if slope is None else (mix_kernel, [slope])
    row_shape = jax.ShapeDtypeStruct((planes, CX, channels), dtype)
    plane_shape = jax.ShapeDtypeStruct((room, CX, channels), dtype)
    return pl.pallas_call(
        lambda *refs: kernel(*refs, count=count),
        grid_spec=pltpu.PrefetchScalarGridSpec(
            num_scalar_prefetch=1,
            grid=(count,),
            in_specs=[anywhere] * (2 + count) + [columns] * len(extra),
            out_specs=[columns, row, row, plane, plane],
            scratch_shapes=[
                pltpu.VMEM((cells, channels), dtype),
                pltpu.VMEM((count, planes, own, width), dtype),
                pltpu.SemaphoreType.DMA((count,)),
                *weight_scratch(weight[0]),
            ],
        ),
        out_shape=[
            jax.ShapeDtypeStruct((cells, channels), dtype),
            row_shape,
            row_shape,
            plane_shape,
            plane_shape,
        ],
    )(here, *weight, *blocks, *extra)


def shift_pairs(axis):
    count = lax.axis_size(axis)
    forward = [(i, i + 1) for i in range(count - 1)]
    return forward, [(target, source) for source, target in forward]


def split_cells_body(volume, out_grad, weight_in, weight_out, filter_taps, filter_bias):
    own, planes, cells = volume.shape
    parts = lax.axis_size("chan")
    rows = CY // parts
    width = rows * CX
    channels = own * parts
    others = ("groups", "space")
    seat = lax.axis_index(others)
    chan = lax.axis_index("chan")
    share = own // lax.axis_size(others)
    here = jnp.stack([chan, seat]).astype(jnp.int32)
    shifts = sorted(range(1, parts), key=lambda shift: (shift & (parts // 2) == 0, shift))

    def swap(part, axes, partner):
        count = lax.axis_size(axes)
        return lax.ppermute(part, axes, [(i, partner(i)) for i in range(count)])

    def exchange(blocks):
        got = {0: blocks[0]}
        for shift in shifts:
            got[shift] = swap(blocks[shift], "chan", lambda i: i ^ shift)
        return [got[shift] for shift in range(parts)]

    def cut(field, order, place):
        pieces = {}
        for shift in order:
            start = (place ^ shift) * width
            piece = lax.dynamic_slice_in_dim(field, start, width, axis=2).transpose(1, 0, 2)
            pieces[shift], place = lax.optimization_barrier((piece, place))
        return pieces

    def paste(pieces):
        field = jnp.zeros((own, planes, cells), pieces[0].dtype)
        for shift in [0] + shifts:
            piece = pieces[shift].transpose(1, 0, 2)
            field = lax.dynamic_update_slice_in_dim(field, piece, (chan ^ shift) * width, axis=2)
        return field

    def gather_column(piece):
        column = piece[None]
        for mask in doubling(parts):
            got = swap(column, "chan", lambda i: i ^ mask)
            column = jnp.concatenate([column, got])
        return column

    def gather_weight(column, beside=None):
        over_x = swap(column, others, lambda i: i ^ 2)
        over_y = swap(column, others, lambda i: i ^ 4)
        mixed = jnp.where(seat & 1 == 0, over_y, over_x)
        mixed, beside = lax.optimization_barrier((mixed, beside))
        far = swap(mixed, others, lambda i: i ^ (4 if i & 1 else 2))
        mine = jnp.stack([column, over_x, over_y, far])
        return (mine, swap(mine, others, lambda i: i ^ 1)), beside

    def halo_of(first, last, fore, back):
        forward, backward = shift_pairs("chan")
        row_low = lax.ppermute(last, "chan", forward)
        row_high = lax.ppermute(first, "chan", backward)
        forward, backward = shift_pairs("space")

        def joined(plane, z):
            plane = lax.dynamic_update_slice_in_dim(plane, row_low[z][None], 0, axis=0)
            return lax.dynamic_update_slice_in_dim(plane, row_high[z][None], rows + 1, axis=0)

        plane_low = lax.ppermute(joined(fore, planes - 1), "space", forward)
        plane_high = lax.ppermute(joined(back, 0), "space", backward)
        return row_low, row_high, plane_low, plane_high

    grid = (planes, rows, CX, channels)
    piece_in, piece_out = (
        lax.dynamic_slice_in_dim(weight, seat * share, share, axis=0)
        for weight in (weight_in, weight_out)
    )
    column = gather_column(piece_in)
    vol_cut = cut(volume, shifts, chan)
    later, column = lax.optimization_barrier((chan, column))
    own_cut = cut(volume, [0], later)
    grad_cut = cut(out_grad, shifts + [0], later)
    full_in, (own_block, here, grad_cut) = gather_weight(column, (own_cut[0], here, grad_cut))
    full_out, _ = gather_weight(gather_column(piece_out))
    table = jnp.concatenate([filter_taps, filter_bias[:, None]], axis=1).T
    taps = gather_column(table)
    own_block, taps = lax.optimization_barrier((own_block, taps))
    vol_blocks = exchange({**vol_cut, 0: own_block})
    grad_blocks = exchange(grad_cut)
    hidden, *edges = product_call(here, vol_blocks, full_in)
    halo = halo_of(*edges)
    *out_blocks, slope = stencil(here, hidden.reshape(grid), halo, taps, full_out, vol_blocks, True)
    out_found = exchange(out_blocks)
    mix_grad, *edges = product_call(
        here, grad_blocks, full_out, slope.reshape(planes * width, channels)
    )
    halo = halo_of(*edges)
    back_blocks = list(
        stencil(here, mix_grad.reshape(grid), halo, taps, full_in, grad_blocks, False)
    )
    out_found, back_blocks[0] = lax.optimization_barrier((out_found, back_blocks[0]))
    block_out = paste(out_found)
    volume_grad = paste(exchange(back_blocks))
    return block_out, volume_grad


def with_halo(block, axis, dim):
    forward, backward = shift_pairs(axis)
    low = lax.ppermute(lax.slice_in_dim(block, block.shape[dim] - 1, None, axis=dim), axis, forward)
    high = lax.ppermute(lax.slice_in_dim(block, 0, 1, axis=dim), axis, backward)
    return jnp.concatenate([low, block, high], axis=dim)


def core(padded, filter_taps, direction):
    extent_z = padded.shape[1] - 2
    extent_y = padded.shape[2] - 2
    extent_x = padded.shape[3] - 2
    summed = jnp.zeros((padded.shape[0], extent_z, extent_y, extent_x), jnp.float32)
    for shift_z in range(3):
        for shift_y in range(3):
            for shift_x in range(3):
                tap_index = (shift_z * 3 + shift_y) * 3 + shift_x
                begin_z = 1 + direction * (shift_z - 1)
                begin_y = 1 + direction * (shift_y - 1)
                begin_x = 1 + direction * (shift_x - 1)
                window = padded[
                    :,
                    begin_z : begin_z + extent_z,
                    begin_y : begin_y + extent_y,
                    begin_x : begin_x + extent_x,
                ]
                summed = summed + filter_taps[:, tap_index][:, None, None, None] * window
    return summed


def lift(field_z):
    extended = field_z.astype(jnp.float32).reshape(field_z.shape[0], field_z.shape[1], CY, CX)
    return jnp.pad(extended, ((0, 0), (0, 0), (1, 1), (1, 1)))


def exchange_body(volume, out_grad, weight_in, weight_out, filter_taps, filter_bias):
    slab_shape = volume.shape
    contract_first = (((0,), (0,)), ((), ()))

    def to_cells(field):
        return lax.all_to_all(
            field.reshape(field.shape[0], -1), "chan", split_axis=1, concat_axis=0, tiled=True
        )

    def to_channels(field):
        return lax.all_to_all(field, "chan", split_axis=0, concat_axis=1, tiled=True).reshape(
            slab_shape
        )

    full_in = lax.all_gather(weight_in, "chan", axis=0, tiled=True)
    full_out = lax.all_gather(weight_out, "chan", axis=0, tiled=True)
    vol_cells = to_cells(volume)
    hidden = to_channels(
        jnp.dot(full_in, vol_cells, preferred_element_type=jnp.float32).astype(jnp.bfloat16)
    )
    padded = lift(with_halo(hidden, "space", 1))
    mixed = core(padded, filter_taps, 1) + filter_bias[:, None, None, None]
    active = gelu_value(mixed).astype(jnp.bfloat16).reshape(slab_shape)
    out_cells = vol_cells.astype(jnp.float32) + jnp.dot(
        full_out, to_cells(active), preferred_element_type=jnp.float32
    )
    block_out = to_channels(out_cells.astype(jnp.bfloat16))
    grad_cells = to_cells(out_grad)
    act_part = lax.dot_general(
        full_out, grad_cells, contract_first, preferred_element_type=jnp.float32
    )
    act_grad = to_channels(act_part.astype(jnp.bfloat16))
    slope = gelu_slope(mixed)
    mix_grad = (
        (act_grad.astype(jnp.float32).reshape(slope.shape) * slope)
        .astype(jnp.bfloat16)
        .reshape(slab_shape)
    )
    padded_grad = lift(with_halo(mix_grad, "space", 1))
    hid_grad = core(padded_grad, filter_taps, -1).astype(jnp.bfloat16).reshape(slab_shape)
    back_part = lax.dot_general(
        full_in, to_cells(hid_grad), contract_first, preferred_element_type=jnp.float32
    )
    volume_grad = to_channels((grad_cells.astype(jnp.float32) + back_part).astype(jnp.bfloat16))
    return block_out, volume_grad


def body(volume, out_grad, weight_in, weight_out, filter_taps, filter_bias):
    own = volume.shape[0]
    parts = lax.axis_size("chan")
    groups, space = lax.axis_size("groups"), lax.axis_size("space")
    whole_rows = CY % (2 * parts) == 0 and (CY // parts * CX) % LANES == 0
    whole_rows = whole_rows and parts & (parts - 1) == 0
    whole_shares = own % LANES == 0 and own % (16 * groups * space) == 0
    split = whole_rows and whole_shares and (groups, space) == (2, 4)
    chosen = split_cells_body if split else exchange_body
    return chosen(volume, out_grad, weight_in, weight_out, filter_taps, filter_bias)


def solution(mesh):
    field = P(("groups", "chan"), "space", None)
    placed = (field, field, P("chan", None), P("chan", None), P("chan", None), P("chan"))
    return jax.shard_map(
        body,
        mesh=mesh,
        in_specs=placed,
        out_specs=(field, field),
        check_vma=False,
    )
```

```python
import jax
import jax.numpy as jnp
from jax import lax
from jax.experimental import pallas as pl
from jax.experimental.pallas import tpu as pltpu
from jax.sharding import PartitionSpec as P

CX = 32
CY = 16
LANES = 128
BLOCK = 2 * LANES


root_half = 0.7071067811865476
inv_root_two_pi = 0.3989422804014327


def gelu_value(field):
    return 0.5 * field * (1.0 + lax.erf(field * root_half))


def gelu_slope(field):
    return (
        0.5 * (1.0 + lax.erf(field * root_half))
        + field * jnp.exp(-0.5 * field * field) * inv_root_two_pi
    )


def fill_pairs(pairs, own, row_low, row_high, plane_low, plane_high):
    planes, rows = own.shape[:2]
    for p in range(planes + 2):
        if p == 0:
            fields = [plane_low[y] for y in range(rows + 2)]
        elif p == planes + 1:
            fields = [plane_high[y] for y in range(rows + 2)]
        else:
            fields = [row_low[p - 1]] + [own[p - 1, y] for y in range(rows)] + [row_high[p - 1]]
        fields = [field.astype(jnp.float32) for field in fields]
        for t in range(rows // 2):
            d0, d1, d2, d3 = fields[2 * t : 2 * t + 4]
            pairs[p, t, 0] = d0 - d2
            pairs[p, t, 1] = d1 + d2
            pairs[p, t, 2] = d2 - d1
            pairs[p, t, 3] = d1 - d3


def fill_factors(factors, taps, flip):
    for a in range(3):
        for e in range(3):
            g = []
            for b in range(3):
                index = (a * 3 + b) * 3 + e
                g.append(taps[0, 26 - index if flip else index])
            ends = g[0] + g[2]
            at = (a * 3 + e) * 4
            factors[at] = g[0]
            factors[at + 1] = 0.5 * (ends + g[1])
            factors[at + 2] = 0.5 * (ends - g[1])
            factors[at + 3] = g[2]


def stencil_pair(pairs, factors, z, t):
    sums = ([], [])
    for e in range(3):
        terms = []
        for i in range(4):
            total = None
            for a in range(3):
                term = pairs[z + a, t, i] * factors[(a * 3 + e) * 4 + i][None, :]
                total = term if total is None else total + term
            terms.append(total)
        sums[0].append(terms[0] + terms[1] + terms[2])
        sums[1].append(terms[1] - terms[2] - terms[3])
    extent = sums[0][0].shape[0]
    x = lax.broadcasted_iota(jnp.int32, sums[0][0].shape, 0)
    for left, here, right in sums:
        before = jnp.where(x == 0, 0.0, pltpu.roll(left, 1, 0))
        after = jnp.where(x == extent - 1, 0.0, pltpu.roll(right, extent - 1, 0))
        yield here + (before + after)


def doubling(count):
    masks = []
    while count > 1:
        masks.append(count - 1)
        count //= 2
    return masks


def distances(count):
    found = [0]
    for mask in doubling(count):
        found += [mask ^ distance for distance in found]
    return found


def piece_copies(here, mine, other, full, sems):
    chan, seat = here[0], here[1]
    copies = []
    for slot, distance in enumerate(distances(mine.shape[1])):
        for side, pieces in enumerate((mine, other)):
            for turn in range(pieces.shape[0]):
                copies.append(
                    pltpu.make_async_copy(
                        pieces.at[turn, slot],
                        full.at[chan ^ distance, seat ^ side ^ (2 * turn)],
                        sems.at[chan ^ distance, 2 * turn + side],
                    )
                )
    return copies


def wait_block(block, mine, other, full, sems):
    for side, pieces in enumerate((mine, other)):
        for turn in range(pieces.shape[0]):
            pltpu.make_async_copy(
                pieces.at[turn, 0], full.at[block, 2 * turn + side], sems.at[block, 2 * turn + side]
            ).wait()


def start_all(copies):
    for copy in copies:
        copy.start()


def wait_all(copies):
    for copy in copies:
        copy.wait()


def add_planes(base, product, out):
    planes, _, width = base.shape
    for z in range(planes):
        total = base[z].astype(jnp.float32) + product[:, z * width : (z + 1) * width]
        out[z] = total.astype(out.dtype)


def part_of(ref, sub):
    lanes = slice(sub * LANES, (sub + 1) * LANES)
    return ref.at[(slice(None),) * (len(ref.shape) - 1) + (lanes,)]


def put_copy(shift, ready, outputs, left):
    return pltpu.make_async_copy(ready.at[shift], outputs[shift], left.at[shift])


def forward_kernel(
    here, own, row_low, row_high, plane_low, plane_high, taps, mine, other, *rest
):
    count = (len(rest) - 10) // 2
    inputs, outputs = rest[:count], rest[count : 2 * count]
    slope, pairs, factors, active, *blocks, weight, sems = rest[2 * count :]
    held, ready, arrived, left = blocks
    step = pl.program_id(0)
    planes, rows, extent = own.shape[:3]
    copies = piece_copies(here, mine, other, weight, sems)

    @pl.when(step == 0)
    def _():
        start_all(copies)
        start_all(block_copies(inputs, held, arrived))

    for sub in range(BLOCK // LANES):
        fields = [part_of(f, sub) for f in (own, row_low, row_high, plane_low, plane_high)]
        table, result = part_of(taps, sub), part_of(slope, sub)
        fill_pairs(pairs, *fields)
        fill_factors(factors, table, False)
        lanes = pl.ds(pl.multiple_of(step * BLOCK + sub * LANES, LANES), LANES)
        for z in range(planes):
            for t in range(rows // 2):
                for odd, mixed in enumerate(stencil_pair(pairs, factors, z, t)):
                    y = 2 * t + odd
                    mixed = mixed + table[0, 27][None, :]
                    half = 0.5 * (1.0 + lax.erf(mixed * root_half))
                    at = (z * rows + y) * extent
                    active[at : at + extent, lanes] = (mixed * half).astype(active.dtype)
                    bell = jnp.exp(-0.5 * mixed * mixed) * inv_root_two_pi
                    result[z, y] = (half + mixed * bell).astype(result.dtype)

    @pl.when(step == pl.num_programs(0) - 1)
    def _():
        wait_all(copies)
        wait_all(block_copies(inputs, held, arrived))
        for shift in range(count):
            rows_of = weight[here[0] ^ shift]
            product = lax.dot_general(
                rows_of.reshape(-1, rows_of.shape[-1]),
                active[...],
                (((1,), (1,)), ((), ())),
                preferred_element_type=jnp.float32,
            )
            add_planes(held.at[shift], product, ready.at[shift])
            put_copy(shift, ready, outputs, left).start()
        for shift in range(count):
            put_copy(shift, ready, outputs, left).wait()


def backward_kernel(
    here, own, row_low, row_high, plane_low, plane_high, taps, mine, other, *rest
):
    count = (len(rest) - 9) // 2
    inputs, outputs = rest[:count], rest[count : 2 * count]
    pairs, factors, grads, *blocks, weight, sems = rest[2 * count :]
    held, ready, arrived, left = blocks
    step = pl.program_id(0)
    planes, rows, extent = own.shape[:3]
    copies = piece_copies(here, mine, other, weight, sems)

    @pl.when(step == 0)
    def _():
        start_all(copies)
        start_all(block_copies(inputs, held, arrived))

    for sub in range(BLOCK // LANES):
        fields = [part_of(f, sub) for f in (own, row_low, row_high, plane_low, plane_high)]
        fill_pairs(pairs, *fields)
        fill_factors(factors, part_of(taps, sub), True)
        lanes = pl.ds(pl.multiple_of(step * BLOCK + sub * LANES, LANES), LANES)
        for z in range(planes):
            for t in range(rows // 2):
                for odd, total in enumerate(stencil_pair(pairs, factors, z, t)):
                    at = (z * rows + 2 * t + odd) * extent
                    grads[at : at + extent, lanes] = total.astype(grads.dtype)

    @pl.when(step == pl.num_programs(0) - 1)
    def _():
        wait_all(copies)
        wait_all(block_copies(inputs, held, arrived))
        channels = grads.shape[1]
        width = held.shape[2]
        for shift in range(count):
            start = pl.multiple_of((here[0] ^ shift) * width, width)
            columns = weight[:, :, :, pl.ds(start, width)].reshape(channels, width)
            product = jnp.dot(grads[...], columns, preferred_element_type=jnp.float32)
            add_planes(held.at[shift], product.T, ready.at[shift])
            put_copy(shift, ready, outputs, left).start()
        for shift in range(count):
            put_copy(shift, ready, outputs, left).wait()


def weight_scratch(mine):
    turns, parts, share, channels = mine.shape
    return [
        pltpu.VMEM((parts, 2 * turns, share, channels), mine.dtype),
        pltpu.SemaphoreType.DMA((parts, 2 * turns)),
    ]


def stencil(here, own, halo, taps, weight, blocks, forward):
    planes, rows, extent, channels = own.shape
    cells = planes * rows * extent
    per_table = taps.shape[2] // BLOCK

    def block(*lead):
        zeros = (0,) * len(lead)
        return pl.BlockSpec(lead + (BLOCK,), lambda c, here: zeros + (c,))

    def table_at(c, here):
        away = (c // per_table) ^ here[0]
        slot = 0
        for place, distance in enumerate(distances(taps.shape[0])):
            slot = jnp.where(away == distance, place, slot)
        return slot, 0, c % per_table

    anywhere = pl.BlockSpec(memory_space=pltpu.HBM)
    in_specs = [
        block(planes, rows, extent),
        block(planes, extent),
        block(planes, extent),
        block(rows + 2, extent),
        block(rows + 2, extent),
        pl.BlockSpec((1, 28, BLOCK), table_at),
        anywhere,
        anywhere,
    ]
    in_specs += [anywhere for _ in blocks]
    out_specs = [anywhere for _ in blocks]
    out_shape = [jax.ShapeDtypeStruct(piece.shape, piece.dtype) for piece in blocks]
    if forward:
        out_specs.append(block(planes, rows, extent))
        out_shape.append(jax.ShapeDtypeStruct(own.shape, own.dtype))
    return pl.pallas_call(
        forward_kernel if forward else backward_kernel,
        grid_spec=pltpu.PrefetchScalarGridSpec(
            num_scalar_prefetch=1,
            grid=(channels // BLOCK,),
            in_specs=in_specs,
            out_specs=out_specs,
            scratch_shapes=[
                pltpu.VMEM((planes + 2, rows // 2, 4, extent, LANES), jnp.float32),
                pltpu.VMEM((36, LANES), jnp.float32),
                pltpu.VMEM((cells, channels), own.dtype),
                pltpu.VMEM((len(blocks),) + blocks[0].shape, own.dtype),
                pltpu.VMEM((len(blocks),) + blocks[0].shape, own.dtype),
                pltpu.SemaphoreType.DMA((len(blocks),)),
                pltpu.SemaphoreType.DMA((len(blocks),)),
                *weight_scratch(weight[0]),
            ],
        ),
        out_shape=out_shape,
    )(here, own, *halo, taps, *weight, *blocks)


def block_copies(inputs, held, sems):
    return [
        pltpu.make_async_copy(block, held.at[shift], sems.at[shift])
        for shift, block in enumerate(inputs)
    ]


def turn_blocks(here, copies, held, turned):
    _, planes, own, width = held.shape
    for shift, copy in enumerate(copies):
        copy.wait()
        block = held.at[shift]
        start = pl.multiple_of((here[0] ^ shift) * own, own)
        for z in range(planes):
            turned[z * width : (z + 1) * width, pl.ds(start, own)] = block[z].T


def put_with_edges(value, out, first, last, fore, back):
    out[...] = value
    planes, extent, width = first.shape
    plane = value.shape[0] // planes
    rows = plane // extent
    for z in range(planes):
        first[z] = value[z * plane : z * plane + extent]
        last[z] = value[(z + 1) * plane - extent : (z + 1) * plane]
    for edge, z in ((back, 0), (fore, planes - 1)):
        edge[0] = jnp.zeros((extent, width), edge.dtype)
        edge[rows + 1] = jnp.zeros((extent, width), edge.dtype)
        for y in range(rows):
            at = z * plane + y * extent
            edge[y + 1] = value[at : at + extent]


def hidden_kernel(here, mine, other, *rest, count):
    inputs, (*outputs, turned, held, arrived, weight, sems) = rest[:count], rest[count:]

    @pl.when(pl.program_id(0) == 0)
    def _():
        blocks = block_copies(inputs, held, arrived)
        start_all(blocks)
        start_all(piece_copies(here, mine, other, weight, sems))
        turn_blocks(here, blocks, held, turned)

    wait_block(pl.program_id(0), mine, other, weight, sems)
    rows_of = weight[pl.program_id(0)]
    value = lax.dot_general(
        turned[...],
        rows_of.reshape(-1, rows_of.shape[-1]),
        (((1,), (1,)), ((), ())),
        preferred_element_type=jnp.float32,
    )
    put_with_edges(value.astype(turned.dtype), *outputs)


def mix_kernel(here, mine, other, *rest, count):
    inputs, (slope, *outputs, turned, held, arrived, weight, sems) = rest[:count], rest[count:]

    @pl.when(pl.program_id(0) == 0)
    def _():
        blocks = block_copies(inputs, held, arrived)
        start_all(blocks)
        copies = piece_copies(here, mine, other, weight, sems)
        start_all(copies)
        turn_blocks(here, blocks, held, turned)
        wait_all(copies)

    channels, width = turned.shape[1], slope.shape[1]
    start = pl.multiple_of(pl.program_id(0) * width, width)
    columns = weight[:, :, :, pl.ds(start, width)].reshape(channels, width)
    grad = jnp.dot(turned[...], columns, preferred_element_type=jnp.float32)
    grad = grad.astype(turned.dtype).astype(jnp.float32)
    put_with_edges((grad * slope[...].astype(jnp.float32)).astype(turned.dtype), *outputs)


def product_call(here, blocks, weight, slope=None):
    planes, own, width = blocks[0].shape
    cells = planes * width
    count = len(blocks)
    channels = own * count
    dtype = blocks[0].dtype
    columns = pl.BlockSpec((cells, own), lambda c, here: (0, c))
    room = width // CX + 2
    row = pl.BlockSpec((planes, CX, own), lambda c, here: (0, 0, c))
    plane = pl.BlockSpec((room, CX, own), lambda c, here: (0, 0, c))
    anywhere = pl.BlockSpec(memory_space=pltpu.HBM)
    kernel, extra = (hidden_kernel, []) if slope is None else (mix_kernel, [slope])
    row_shape = jax.ShapeDtypeStruct((planes, CX, channels), dtype)
    plane_shape = jax.ShapeDtypeStruct((room, CX, channels), dtype)
    return pl.pallas_call(
        lambda *refs: kernel(*refs, count=count),
        grid_spec=pltpu.PrefetchScalarGridSpec(
            num_scalar_prefetch=1,
            grid=(count,),
            in_specs=[anywhere] * (2 + count) + [columns] * len(extra),
            out_specs=[columns, row, row, plane, plane],
            scratch_shapes=[
                pltpu.VMEM((cells, channels), dtype),
                pltpu.VMEM((count, planes, own, width), dtype),
                pltpu.SemaphoreType.DMA((count,)),
                *weight_scratch(weight[0]),
            ],
        ),
        out_shape=[
            jax.ShapeDtypeStruct((cells, channels), dtype),
            row_shape,
            row_shape,
            plane_shape,
            plane_shape,
        ],
    )(here, *weight, *blocks, *extra)


def shift_pairs(axis):
    count = lax.axis_size(axis)
    forward = [(i, i + 1) for i in range(count - 1)]
    return forward, [(target, source) for source, target in forward]


def split_cells_body(volume, out_grad, weight_in, weight_out, filter_taps, filter_bias):
    own, planes, cells = volume.shape
    parts = lax.axis_size("chan")
    rows = CY // parts
    width = rows * CX
    channels = own * parts
    others = ("groups", "space")
    seat = lax.axis_index(others)
    chan = lax.axis_index("chan")
    share = own // lax.axis_size(others)
    here = jnp.stack([chan, seat]).astype(jnp.int32)
    shifts = sorted(range(1, parts), key=lambda shift: (shift & (parts // 2) == 0, shift))

    def swap(part, axes, partner):
        count = lax.axis_size(axes)
        return lax.ppermute(part, axes, [(i, partner(i)) for i in range(count)])

    def exchange(blocks):
        got = {0: blocks[0]}
        for shift in shifts:
            got[shift] = swap(blocks[shift], "chan", lambda i: i ^ shift)
        return [got[shift] for shift in range(parts)]

    def cut(field, order, place):
        pieces = {}
        for shift in order:
            start = (place ^ shift) * width
            piece = lax.dynamic_slice_in_dim(field, start, width, axis=2).transpose(1, 0, 2)
            pieces[shift], place = lax.optimization_barrier((piece, place))
        return pieces

    def paste(pieces):
        field = jnp.zeros((own, planes, cells), pieces[0].dtype)
        for shift in [0] + shifts:
            piece = pieces[shift].transpose(1, 0, 2)
            field = lax.dynamic_update_slice_in_dim(field, piece, (chan ^ shift) * width, axis=2)
        return field

    def gather_column(piece):
        column = piece[None]
        for mask in doubling(parts):
            got = swap(column, "chan", lambda i: i ^ mask)
            column = jnp.concatenate([column, got])
        return column

    def gather_weight(column, beside=None):
        over_x = swap(column, others, lambda i: i ^ 2)
        over_y = swap(column, others, lambda i: i ^ 4)
        mixed = jnp.where(seat & 1 == 0, over_y, over_x)
        mixed, beside = lax.optimization_barrier((mixed, beside))
        far = swap(mixed, others, lambda i: i ^ (4 if i & 1 else 2))
        base = lax.optimization_barrier(jnp.stack([column, over_x, over_y, over_y]))
        mine = lax.dynamic_update_slice_in_dim(base, far[None], 3, axis=0)
        return (mine, swap(mine, others, lambda i: i ^ 1)), beside

    def halo_of(first, last, fore, back):
        forward, backward = shift_pairs("chan")
        row_low = lax.ppermute(last, "chan", forward)
        row_high = lax.ppermute(first, "chan", backward)
        forward, backward = shift_pairs("space")

        def joined(plane, z):
            plane = lax.dynamic_update_slice_in_dim(plane, row_low[z][None], 0, axis=0)
            return lax.dynamic_update_slice_in_dim(plane, row_high[z][None], rows + 1, axis=0)

        plane_low = lax.ppermute(joined(fore, planes - 1), "space", forward)
        plane_high = lax.ppermute(joined(back, 0), "space", backward)
        return row_low, row_high, plane_low, plane_high

    grid = (planes, rows, CX, channels)
    piece_in, piece_out = (
        lax.dynamic_slice_in_dim(weight, seat * share, share, axis=0)
        for weight in (weight_in, weight_out)
    )
    column = gather_column(piece_in)
    vol_cut = cut(volume, shifts, chan)
    later, column = lax.optimization_barrier((chan, column))
    own_cut = cut(volume, [0], later)
    grad_cut = cut(out_grad, shifts + [0], later)
    full_in, (own_block, here, grad_cut) = gather_weight(column, (own_cut[0], here, grad_cut))
    full_out, _ = gather_weight(gather_column(piece_out))
    table = jnp.concatenate([filter_taps, filter_bias[:, None]], axis=1).T
    taps = gather_column(table)
    own_block, taps = lax.optimization_barrier((own_block, taps))
    vol_blocks = exchange({**vol_cut, 0: own_block})
    grad_blocks = exchange(grad_cut)
    hidden, *edges = product_call(here, vol_blocks, full_in)
    halo = halo_of(*edges)
    *out_blocks, slope = stencil(here, hidden.reshape(grid), halo, taps, full_out, vol_blocks, True)
    out_found = exchange(out_blocks)
    mix_grad, *edges = product_call(
        here, grad_blocks, full_out, slope.reshape(planes * width, channels)
    )
    halo = halo_of(*edges)
    back_blocks = list(
        stencil(here, mix_grad.reshape(grid), halo, taps, full_in, grad_blocks, False)
    )
    out_found, back_blocks[0] = lax.optimization_barrier((out_found, back_blocks[0]))
    block_out = paste(out_found)
    volume_grad = paste(exchange(back_blocks))
    return block_out, volume_grad


def with_halo(block, axis, dim):
    forward, backward = shift_pairs(axis)
    low = lax.ppermute(lax.slice_in_dim(block, block.shape[dim] - 1, None, axis=dim), axis, forward)
    high = lax.ppermute(lax.slice_in_dim(block, 0, 1, axis=dim), axis, backward)
    return jnp.concatenate([low, block, high], axis=dim)


def core(padded, filter_taps, direction):
    extent_z = padded.shape[1] - 2
    extent_y = padded.shape[2] - 2
    extent_x = padded.shape[3] - 2
    summed = jnp.zeros((padded.shape[0], extent_z, extent_y, extent_x), jnp.float32)
    for shift_z in range(3):
        for shift_y in range(3):
            for shift_x in range(3):
                tap_index = (shift_z * 3 + shift_y) * 3 + shift_x
                begin_z = 1 + direction * (shift_z - 1)
                begin_y = 1 + direction * (shift_y - 1)
                begin_x = 1 + direction * (shift_x - 1)
                window = padded[
                    :,
                    begin_z : begin_z + extent_z,
                    begin_y : begin_y + extent_y,
                    begin_x : begin_x + extent_x,
                ]
                summed = summed + filter_taps[:, tap_index][:, None, None, None] * window
    return summed


def lift(field_z):
    extended = field_z.astype(jnp.float32).reshape(field_z.shape[0], field_z.shape[1], CY, CX)
    return jnp.pad(extended, ((0, 0), (0, 0), (1, 1), (1, 1)))


def exchange_body(volume, out_grad, weight_in, weight_out, filter_taps, filter_bias):
    slab_shape = volume.shape
    contract_first = (((0,), (0,)), ((), ()))

    def to_cells(field):
        return lax.all_to_all(
            field.reshape(field.shape[0], -1), "chan", split_axis=1, concat_axis=0, tiled=True
        )

    def to_channels(field):
        return lax.all_to_all(field, "chan", split_axis=0, concat_axis=1, tiled=True).reshape(
            slab_shape
        )

    full_in = lax.all_gather(weight_in, "chan", axis=0, tiled=True)
    full_out = lax.all_gather(weight_out, "chan", axis=0, tiled=True)
    vol_cells = to_cells(volume)
    hidden = to_channels(
        jnp.dot(full_in, vol_cells, preferred_element_type=jnp.float32).astype(jnp.bfloat16)
    )
    padded = lift(with_halo(hidden, "space", 1))
    mixed = core(padded, filter_taps, 1) + filter_bias[:, None, None, None]
    active = gelu_value(mixed).astype(jnp.bfloat16).reshape(slab_shape)
    out_cells = vol_cells.astype(jnp.float32) + jnp.dot(
        full_out, to_cells(active), preferred_element_type=jnp.float32
    )
    block_out = to_channels(out_cells.astype(jnp.bfloat16))
    grad_cells = to_cells(out_grad)
    act_part = lax.dot_general(
        full_out, grad_cells, contract_first, preferred_element_type=jnp.float32
    )
    act_grad = to_channels(act_part.astype(jnp.bfloat16))
    slope = gelu_slope(mixed)
    mix_grad = (
        (act_grad.astype(jnp.float32).reshape(slope.shape) * slope)
        .astype(jnp.bfloat16)
        .reshape(slab_shape)
    )
    padded_grad = lift(with_halo(mix_grad, "space", 1))
    hid_grad = core(padded_grad, filter_taps, -1).astype(jnp.bfloat16).reshape(slab_shape)
    back_part = lax.dot_general(
        full_in, to_cells(hid_grad), contract_first, preferred_element_type=jnp.float32
    )
    volume_grad = to_channels((grad_cells.astype(jnp.float32) + back_part).astype(jnp.bfloat16))
    return block_out, volume_grad


def body(volume, out_grad, weight_in, weight_out, filter_taps, filter_bias):
    own = volume.shape[0]
    parts = lax.axis_size("chan")
    groups, space = lax.axis_size("groups"), lax.axis_size("space")
    whole_rows = CY % (2 * parts) == 0 and (CY // parts * CX) % LANES == 0
    whole_rows = whole_rows and parts & (parts - 1) == 0
    whole_shares = own % BLOCK == 0 and own % (16 * groups * space) == 0
    split = whole_rows and whole_shares and (groups, space) == (2, 4)
    chosen = split_cells_body if split else exchange_body
    return chosen(volume, out_grad, weight_in, weight_out, filter_taps, filter_bias)


def solution(mesh):
    field = P(("groups", "chan"), "space", None)
    placed = (field, field, P("chan", None), P("chan", None), P("chan", None), P("chan"))
    return jax.shard_map(
        body,
        mesh=mesh,
        in_specs=placed,
        out_specs=(field, field),
        check_vma=False,
    )
```

```python
import jax
import jax.numpy as jnp
from jax import lax
from jax.experimental import pallas as pl
from jax.experimental.pallas import tpu as pltpu
from jax.sharding import PartitionSpec as P

CX = 32
CY = 16
LANES = 128
BLOCK = 2 * LANES


root_half = 0.7071067811865476
inv_root_two_pi = 0.3989422804014327


def gelu_value(field):
    return 0.5 * field * (1.0 + lax.erf(field * root_half))


def gelu_slope(field):
    return (
        0.5 * (1.0 + lax.erf(field * root_half))
        + field * jnp.exp(-0.5 * field * field) * inv_root_two_pi
    )


def fill_pairs(pairs, own, row_low, row_high, plane_low, plane_high):
    planes, rows = own.shape[:2]
    for p in range(planes + 2):
        if p == 0:
            fields = [plane_low[y] for y in range(rows + 2)]
        elif p == planes + 1:
            fields = [plane_high[y] for y in range(rows + 2)]
        else:
            fields = [row_low[p - 1]] + [own[p - 1, y] for y in range(rows)] + [row_high[p - 1]]
        fields = [field.astype(jnp.float32) for field in fields]
        for t in range(rows // 2):
            d0, d1, d2, d3 = fields[2 * t : 2 * t + 4]
            pairs[p, t, 0] = d0 - d2
            pairs[p, t, 1] = d1 + d2
            pairs[p, t, 2] = d2 - d1
            pairs[p, t, 3] = d1 - d3


def fill_factors(factors, taps, flip):
    for a in range(3):
        for e in range(3):
            g = []
            for b in range(3):
                index = (a * 3 + b) * 3 + e
                g.append(taps[0, 26 - index if flip else index])
            ends = g[0] + g[2]
            at = (a * 3 + e) * 4
            factors[at] = g[0]
            factors[at + 1] = 0.5 * (ends + g[1])
            factors[at + 2] = 0.5 * (ends - g[1])
            factors[at + 3] = g[2]


def stencil_pair(pairs, factors, z, t):
    sums = ([], [])
    for e in range(3):
        terms = []
        for i in range(4):
            total = None
            for a in range(3):
                term = pairs[z + a, t, i] * factors[(a * 3 + e) * 4 + i][None, :]
                total = term if total is None else total + term
            terms.append(total)
        sums[0].append(terms[0] + terms[1] + terms[2])
        sums[1].append(terms[1] - terms[2] - terms[3])
    extent = sums[0][0].shape[0]
    x = lax.broadcasted_iota(jnp.int32, sums[0][0].shape, 0)
    for left, here, right in sums:
        before = jnp.where(x == 0, 0.0, pltpu.roll(left, 1, 0))
        after = jnp.where(x == extent - 1, 0.0, pltpu.roll(right, extent - 1, 0))
        yield here + (before + after)


def doubling(count):
    masks = []
    while count > 1:
        masks.append(count - 1)
        count //= 2
    return masks


def distances(count):
    found = [0]
    for mask in doubling(count):
        found += [mask ^ distance for distance in found]
    return found


def piece_copies(here, mine, other, full, sems):
    chan, seat = here[0], here[1]
    copies = []
    for slot, distance in enumerate(distances(mine.shape[1])):
        for side, pieces in enumerate((mine, other)):
            for turn in range(pieces.shape[0]):
                copies.append(
                    pltpu.make_async_copy(
                        pieces.at[turn, slot],
                        full.at[chan ^ distance, seat ^ side ^ (2 * turn)],
                        sems.at[chan ^ distance, 2 * turn + side],
                    )
                )
    return copies


def wait_block(block, mine, other, full, sems):
    for side, pieces in enumerate((mine, other)):
        for turn in range(pieces.shape[0]):
            pltpu.make_async_copy(
                pieces.at[turn, 0], full.at[block, 2 * turn + side], sems.at[block, 2 * turn + side]
            ).wait()


def start_all(copies):
    for copy in copies:
        copy.start()


def wait_all(copies):
    for copy in copies:
        copy.wait()


def add_planes(base, product, out):
    planes, _, width = base.shape
    for z in range(planes):
        total = base[z].astype(jnp.float32) + product[:, z * width : (z + 1) * width]
        out[z] = total.astype(out.dtype)


def part_of(ref, sub):
    lanes = slice(sub * LANES, (sub + 1) * LANES)
    return ref.at[(slice(None),) * (len(ref.shape) - 1) + (lanes,)]


def put_copy(shift, ready, outputs, left):
    return pltpu.make_async_copy(ready.at[shift], outputs[shift], left.at[shift])


def forward_kernel(
    here, own, row_low, row_high, plane_low, plane_high, taps, mine, other, *rest
):
    count = (len(rest) - 10) // 2
    inputs, outputs = rest[:count], rest[count : 2 * count]
    slope, pairs, factors, active, *blocks, weight, sems = rest[2 * count :]
    held, ready, arrived, left = blocks
    step = pl.program_id(0)
    planes, rows, extent = own.shape[:3]
    copies = piece_copies(here, mine, other, weight, sems)

    @pl.when(step == 0)
    def _():
        start_all(copies)
        start_all(block_copies(inputs, held, arrived))

    for sub in range(BLOCK // LANES):
        fields = [part_of(f, sub) for f in (own, row_low, row_high, plane_low, plane_high)]
        table, result = part_of(taps, sub), part_of(slope, sub)
        fill_pairs(pairs, *fields)
        fill_factors(factors, table, False)
        lanes = pl.ds(pl.multiple_of(step * BLOCK + sub * LANES, LANES), LANES)
        for z in range(planes):
            for t in range(rows // 2):
                for odd, mixed in enumerate(stencil_pair(pairs, factors, z, t)):
                    y = 2 * t + odd
                    mixed = mixed + table[0, 27][None, :]
                    half = 0.5 * (1.0 + lax.erf(mixed * root_half))
                    at = (z * rows + y) * extent
                    active[at : at + extent, lanes] = (mixed * half).astype(active.dtype)
                    bell = jnp.exp(-0.5 * mixed * mixed) * inv_root_two_pi
                    result[z, y] = (half + mixed * bell).astype(result.dtype)

    @pl.when(step == pl.num_programs(0) - 1)
    def _():
        wait_all(copies)
        wait_all(block_copies(inputs, held, arrived))
        for shift in range(count):
            rows_of = weight[here[0] ^ shift]
            product = lax.dot_general(
                rows_of.reshape(-1, rows_of.shape[-1]),
                active[...],
                (((1,), (1,)), ((), ())),
                preferred_element_type=jnp.float32,
            )
            add_planes(held.at[shift], product, ready.at[shift])
            put_copy(shift, ready, outputs, left).start()
        for shift in range(count):
            put_copy(shift, ready, outputs, left).wait()


def backward_kernel(
    here, own, row_low, row_high, plane_low, plane_high, taps, mine, other, *rest
):
    count = (len(rest) - 9) // 2
    inputs, outputs = rest[:count], rest[count : 2 * count]
    pairs, factors, grads, *blocks, weight, sems = rest[2 * count :]
    held, ready, arrived, left = blocks
    step = pl.program_id(0)
    planes, rows, extent = own.shape[:3]
    copies = piece_copies(here, mine, other, weight, sems)

    @pl.when(step == 0)
    def _():
        start_all(copies)
        start_all(block_copies(inputs, held, arrived))

    for sub in range(BLOCK // LANES):
        fields = [part_of(f, sub) for f in (own, row_low, row_high, plane_low, plane_high)]
        fill_pairs(pairs, *fields)
        fill_factors(factors, part_of(taps, sub), True)
        lanes = pl.ds(pl.multiple_of(step * BLOCK + sub * LANES, LANES), LANES)
        for z in range(planes):
            for t in range(rows // 2):
                for odd, total in enumerate(stencil_pair(pairs, factors, z, t)):
                    at = (z * rows + 2 * t + odd) * extent
                    grads[at : at + extent, lanes] = total.astype(grads.dtype)

    @pl.when(step == pl.num_programs(0) - 1)
    def _():
        wait_all(copies)
        wait_all(block_copies(inputs, held, arrived))
        channels = grads.shape[1]
        width = held.shape[2]
        for shift in range(count):
            start = pl.multiple_of((here[0] ^ shift) * width, width)
            columns = weight[:, :, :, pl.ds(start, width)].reshape(channels, width)
            product = jnp.dot(grads[...], columns, preferred_element_type=jnp.float32)
            add_planes(held.at[shift], product.T, ready.at[shift])
            put_copy(shift, ready, outputs, left).start()
        for shift in range(count):
            put_copy(shift, ready, outputs, left).wait()


def weight_scratch(mine):
    turns, parts, share, channels = mine.shape
    return [
        pltpu.VMEM((parts, 2 * turns, share, channels), mine.dtype),
        pltpu.SemaphoreType.DMA((parts, 2 * turns)),
    ]


def stencil(here, own, halo, taps, weight, blocks, forward):
    planes, rows, extent, channels = own.shape
    cells = planes * rows * extent
    per_table = taps.shape[2] // BLOCK

    def block(*lead):
        zeros = (0,) * len(lead)
        return pl.BlockSpec(lead + (BLOCK,), lambda c, here: zeros + (c,))

    def table_at(c, here):
        away = (c // per_table) ^ here[0]
        slot = 0
        for place, distance in enumerate(distances(taps.shape[0])):
            slot = jnp.where(away == distance, place, slot)
        return slot, 0, c % per_table

    anywhere = pl.BlockSpec(memory_space=pltpu.HBM)
    in_specs = [
        block(planes, rows, extent),
        block(planes, extent),
        block(planes, extent),
        block(rows + 2, extent),
        block(rows + 2, extent),
        pl.BlockSpec((1, 28, BLOCK), table_at),
        anywhere,
        anywhere,
    ]
    in_specs += [anywhere for _ in blocks]
    out_specs = [anywhere for _ in blocks]
    out_shape = [jax.ShapeDtypeStruct(piece.shape, piece.dtype) for piece in blocks]
    if forward:
        out_specs.append(block(planes, rows, extent))
        out_shape.append(jax.ShapeDtypeStruct(own.shape, own.dtype))
    return pl.pallas_call(
        forward_kernel if forward else backward_kernel,
        grid_spec=pltpu.PrefetchScalarGridSpec(
            num_scalar_prefetch=1,
            grid=(channels // BLOCK,),
            in_specs=in_specs,
            out_specs=out_specs,
            scratch_shapes=[
                pltpu.VMEM((planes + 2, rows // 2, 4, extent, LANES), jnp.float32),
                pltpu.VMEM((36, LANES), jnp.float32),
                pltpu.VMEM((cells, channels), own.dtype),
                pltpu.VMEM((len(blocks),) + blocks[0].shape, own.dtype),
                pltpu.VMEM((len(blocks),) + blocks[0].shape, own.dtype),
                pltpu.SemaphoreType.DMA((len(blocks),)),
                pltpu.SemaphoreType.DMA((len(blocks),)),
                *weight_scratch(weight[0]),
            ],
        ),
        out_shape=out_shape,
    )(here, own, *halo, taps, *weight, *blocks)


def block_copies(inputs, held, sems):
    return [
        pltpu.make_async_copy(block, held.at[shift], sems.at[shift])
        for shift, block in enumerate(inputs)
    ]


def turn_blocks(here, copies, held, turned):
    _, planes, own, width = held.shape
    for shift, copy in enumerate(copies):
        copy.wait()
        block = held.at[shift]
        start = pl.multiple_of((here[0] ^ shift) * own, own)
        for z in range(planes):
            turned[z * width : (z + 1) * width, pl.ds(start, own)] = block[z].T


def put_with_edges(value, out, first, last, fore, back):
    out[...] = value
    planes, extent, width = first.shape
    plane = value.shape[0] // planes
    rows = plane // extent
    for z in range(planes):
        first[z] = value[z * plane : z * plane + extent]
        last[z] = value[(z + 1) * plane - extent : (z + 1) * plane]
    for edge, z in ((back, 0), (fore, planes - 1)):
        edge[0] = jnp.zeros((extent, width), edge.dtype)
        edge[rows + 1] = jnp.zeros((extent, width), edge.dtype)
        for y in range(rows):
            at = z * plane + y * extent
            edge[y + 1] = value[at : at + extent]


def hidden_kernel(here, mine, other, *rest, count):
    inputs, (*outputs, turned, held, arrived, weight, sems) = rest[:count], rest[count:]

    @pl.when(pl.program_id(0) == 0)
    def _():
        blocks = block_copies(inputs, held, arrived)
        start_all(blocks)
        start_all(piece_copies(here, mine, other, weight, sems))
        turn_blocks(here, blocks, held, turned)

    wait_block(pl.program_id(0), mine, other, weight, sems)
    rows_of = weight[pl.program_id(0)]
    value = lax.dot_general(
        turned[...],
        rows_of.reshape(-1, rows_of.shape[-1]),
        (((1,), (1,)), ((), ())),
        preferred_element_type=jnp.float32,
    )
    put_with_edges(value.astype(turned.dtype), *outputs)


def mix_kernel(here, mine, other, *rest, count):
    inputs, (slope, *outputs, turned, held, arrived, weight, sems) = rest[:count], rest[count:]

    @pl.when(pl.program_id(0) == 0)
    def _():
        blocks = block_copies(inputs, held, arrived)
        start_all(blocks)
        copies = piece_copies(here, mine, other, weight, sems)
        start_all(copies)
        turn_blocks(here, blocks, held, turned)

    width = slope.shape[1]
    start = pl.multiple_of(pl.program_id(0) * width, width)
    grad = 0.0
    for block in range(count):

        @pl.when(pl.program_id(0) == 0)
        def _():
            wait_block(block, mine, other, weight, sems)

        columns = weight[block, :, :, pl.ds(start, width)].reshape(-1, width)
        rows_of = turned[:, block * columns.shape[0] : (block + 1) * columns.shape[0]]
        grad = grad + jnp.dot(rows_of, columns, preferred_element_type=jnp.float32)
    grad = grad.astype(turned.dtype).astype(jnp.float32)
    put_with_edges((grad * slope[...].astype(jnp.float32)).astype(turned.dtype), *outputs)


def product_call(here, blocks, weight, slope=None):
    planes, own, width = blocks[0].shape
    cells = planes * width
    count = len(blocks)
    channels = own * count
    dtype = blocks[0].dtype
    columns = pl.BlockSpec((cells, own), lambda c, here: (0, c))
    room = width // CX + 2
    row = pl.BlockSpec((planes, CX, own), lambda c, here: (0, 0, c))
    plane = pl.BlockSpec((room, CX, own), lambda c, here: (0, 0, c))
    anywhere = pl.BlockSpec(memory_space=pltpu.HBM)
    kernel, extra = (hidden_kernel, []) if slope is None else (mix_kernel, [slope])
    row_shape = jax.ShapeDtypeStruct((planes, CX, channels), dtype)
    plane_shape = jax.ShapeDtypeStruct((room, CX, channels), dtype)
    return pl.pallas_call(
        lambda *refs: kernel(*refs, count=count),
        grid_spec=pltpu.PrefetchScalarGridSpec(
            num_scalar_prefetch=1,
            grid=(count,),
            in_specs=[anywhere] * (2 + count) + [columns] * len(extra),
            out_specs=[columns, row, row, plane, plane],
            scratch_shapes=[
                pltpu.VMEM((cells, channels), dtype),
                pltpu.VMEM((count, planes, own, width), dtype),
                pltpu.SemaphoreType.DMA((count,)),
                *weight_scratch(weight[0]),
            ],
        ),
        out_shape=[
            jax.ShapeDtypeStruct((cells, channels), dtype),
            row_shape,
            row_shape,
            plane_shape,
            plane_shape,
        ],
    )(here, *weight, *blocks, *extra)


def shift_pairs(axis):
    count = lax.axis_size(axis)
    forward = [(i, i + 1) for i in range(count - 1)]
    return forward, [(target, source) for source, target in forward]


def split_cells_body(volume, out_grad, weight_in, weight_out, filter_taps, filter_bias):
    own, planes, cells = volume.shape
    parts = lax.axis_size("chan")
    rows = CY // parts
    width = rows * CX
    channels = own * parts
    others = ("groups", "space")
    seat = lax.axis_index(others)
    chan = lax.axis_index("chan")
    share = own // lax.axis_size(others)
    here = jnp.stack([chan, seat]).astype(jnp.int32)
    shifts = sorted(range(1, parts), key=lambda shift: (shift & (parts // 2) == 0, shift))

    def swap(part, axes, partner):
        count = lax.axis_size(axes)
        return lax.ppermute(part, axes, [(i, partner(i)) for i in range(count)])

    def exchange(blocks):
        got = {0: blocks[0]}
        for shift in shifts:
            got[shift] = swap(blocks[shift], "chan", lambda i: i ^ shift)
        return [got[shift] for shift in range(parts)]

    def cut(field, order, place):
        pieces = {}
        for shift in order:
            start = (place ^ shift) * width
            piece = lax.dynamic_slice_in_dim(field, start, width, axis=2).transpose(1, 0, 2)
            pieces[shift], place = lax.optimization_barrier((piece, place))
        return pieces

    def paste(pieces):
        field = jnp.zeros((own, planes, cells), pieces[0].dtype)
        for shift in [0] + shifts:
            piece = pieces[shift].transpose(1, 0, 2)
            field = lax.dynamic_update_slice_in_dim(field, piece, (chan ^ shift) * width, axis=2)
        return field

    def gather_column(piece):
        column = piece[None]
        for mask in doubling(parts):
            got = swap(column, "chan", lambda i: i ^ mask)
            column = jnp.concatenate([column, got])
        return column

    def gather_weight(column, beside=None):
        over_x = swap(column, others, lambda i: i ^ 2)
        over_y = swap(column, others, lambda i: i ^ 4)
        mixed = jnp.where(seat & 1 == 0, over_y, over_x)
        mixed, beside = lax.optimization_barrier((mixed, beside))
        far = swap(mixed, others, lambda i: i ^ (4 if i & 1 else 2))
        base = lax.optimization_barrier(jnp.stack([column, over_x, over_y, over_y]))
        mine = lax.dynamic_update_slice_in_dim(base, far[None], 3, axis=0)
        return (mine, swap(mine, others, lambda i: i ^ 1)), beside

    def halo_of(first, last, fore, back):
        forward, backward = shift_pairs("chan")
        row_low = lax.ppermute(last, "chan", forward)
        row_high = lax.ppermute(first, "chan", backward)
        forward, backward = shift_pairs("space")

        def joined(plane, z):
            plane = lax.dynamic_update_slice_in_dim(plane, row_low[z][None], 0, axis=0)
            return lax.dynamic_update_slice_in_dim(plane, row_high[z][None], rows + 1, axis=0)

        plane_low = lax.ppermute(joined(fore, planes - 1), "space", forward)
        plane_high = lax.ppermute(joined(back, 0), "space", backward)
        return row_low, row_high, plane_low, plane_high

    grid = (planes, rows, CX, channels)
    piece_in, piece_out = (
        lax.dynamic_slice_in_dim(weight, seat * share, share, axis=0)
        for weight in (weight_in, weight_out)
    )
    column = gather_column(piece_in)
    vol_cut = cut(volume, shifts, chan)
    later, column = lax.optimization_barrier((chan, column))
    own_cut = cut(volume, [0], later)
    grad_cut = cut(out_grad, shifts + [0], later)
    full_in, (own_block, here, grad_cut) = gather_weight(column, (own_cut[0], here, grad_cut))
    full_out, _ = gather_weight(gather_column(piece_out))
    table = jnp.concatenate([filter_taps, filter_bias[:, None]], axis=1).T
    taps = gather_column(table)
    own_block, taps = lax.optimization_barrier((own_block, taps))
    vol_blocks = exchange({**vol_cut, 0: own_block})
    grad_blocks = exchange(grad_cut)
    hidden, *edges = product_call(here, vol_blocks, full_in)
    halo = halo_of(*edges)
    *out_blocks, slope = stencil(here, hidden.reshape(grid), halo, taps, full_out, vol_blocks, True)
    out_found = exchange(out_blocks)
    mix_grad, *edges = product_call(
        here, grad_blocks, full_out, slope.reshape(planes * width, channels)
    )
    halo = halo_of(*edges)
    back_blocks = list(
        stencil(here, mix_grad.reshape(grid), halo, taps, full_in, grad_blocks, False)
    )
    out_found, back_blocks[0] = lax.optimization_barrier((out_found, back_blocks[0]))
    block_out = paste(out_found)
    volume_grad = paste(exchange(back_blocks))
    return block_out, volume_grad


def with_halo(block, axis, dim):
    forward, backward = shift_pairs(axis)
    low = lax.ppermute(lax.slice_in_dim(block, block.shape[dim] - 1, None, axis=dim), axis, forward)
    high = lax.ppermute(lax.slice_in_dim(block, 0, 1, axis=dim), axis, backward)
    return jnp.concatenate([low, block, high], axis=dim)


def core(padded, filter_taps, direction):
    extent_z = padded.shape[1] - 2
    extent_y = padded.shape[2] - 2
    extent_x = padded.shape[3] - 2
    summed = jnp.zeros((padded.shape[0], extent_z, extent_y, extent_x), jnp.float32)
    for shift_z in range(3):
        for shift_y in range(3):
            for shift_x in range(3):
                tap_index = (shift_z * 3 + shift_y) * 3 + shift_x
                begin_z = 1 + direction * (shift_z - 1)
                begin_y = 1 + direction * (shift_y - 1)
                begin_x = 1 + direction * (shift_x - 1)
                window = padded[
                    :,
                    begin_z : begin_z + extent_z,
                    begin_y : begin_y + extent_y,
                    begin_x : begin_x + extent_x,
                ]
                summed = summed + filter_taps[:, tap_index][:, None, None, None] * window
    return summed


def lift(field_z):
    extended = field_z.astype(jnp.float32).reshape(field_z.shape[0], field_z.shape[1], CY, CX)
    return jnp.pad(extended, ((0, 0), (0, 0), (1, 1), (1, 1)))


def exchange_body(volume, out_grad, weight_in, weight_out, filter_taps, filter_bias):
    slab_shape = volume.shape
    contract_first = (((0,), (0,)), ((), ()))

    def to_cells(field):
        return lax.all_to_all(
            field.reshape(field.shape[0], -1), "chan", split_axis=1, concat_axis=0, tiled=True
        )

    def to_channels(field):
        return lax.all_to_all(field, "chan", split_axis=0, concat_axis=1, tiled=True).reshape(
            slab_shape
        )

    full_in = lax.all_gather(weight_in, "chan", axis=0, tiled=True)
    full_out = lax.all_gather(weight_out, "chan", axis=0, tiled=True)
    vol_cells = to_cells(volume)
    hidden = to_channels(
        jnp.dot(full_in, vol_cells, preferred_element_type=jnp.float32).astype(jnp.bfloat16)
    )
    padded = lift(with_halo(hidden, "space", 1))
    mixed = core(padded, filter_taps, 1) + filter_bias[:, None, None, None]
    active = gelu_value(mixed).astype(jnp.bfloat16).reshape(slab_shape)
    out_cells = vol_cells.astype(jnp.float32) + jnp.dot(
        full_out, to_cells(active), preferred_element_type=jnp.float32
    )
    block_out = to_channels(out_cells.astype(jnp.bfloat16))
    grad_cells = to_cells(out_grad)
    act_part = lax.dot_general(
        full_out, grad_cells, contract_first, preferred_element_type=jnp.float32
    )
    act_grad = to_channels(act_part.astype(jnp.bfloat16))
    slope = gelu_slope(mixed)
    mix_grad = (
        (act_grad.astype(jnp.float32).reshape(slope.shape) * slope)
        .astype(jnp.bfloat16)
        .reshape(slab_shape)
    )
    padded_grad = lift(with_halo(mix_grad, "space", 1))
    hid_grad = core(padded_grad, filter_taps, -1).astype(jnp.bfloat16).reshape(slab_shape)
    back_part = lax.dot_general(
        full_in, to_cells(hid_grad), contract_first, preferred_element_type=jnp.float32
    )
    volume_grad = to_channels((grad_cells.astype(jnp.float32) + back_part).astype(jnp.bfloat16))
    return block_out, volume_grad


def body(volume, out_grad, weight_in, weight_out, filter_taps, filter_bias):
    own = volume.shape[0]
    parts = lax.axis_size("chan")
    groups, space = lax.axis_size("groups"), lax.axis_size("space")
    whole_rows = CY % (2 * parts) == 0 and (CY // parts * CX) % LANES == 0
    whole_rows = whole_rows and parts & (parts - 1) == 0
    whole_shares = own % BLOCK == 0 and own % (16 * groups * space) == 0
    split = whole_rows and whole_shares and (groups, space) == (2, 4)
    chosen = split_cells_body if split else exchange_body
    return chosen(volume, out_grad, weight_in, weight_out, filter_taps, filter_bias)


def solution(mesh):
    field = P(("groups", "chan"), "space", None)
    placed = (field, field, P("chan", None), P("chan", None), P("chan", None), P("chan"))
    return jax.shard_map(
        body,
        mesh=mesh,
        in_specs=placed,
        out_specs=(field, field),
        check_vma=False,
    )
```
